128 devices in a mesh: dom: 32 (over x, z, core), bal: 4 (over y).
Axes of the slice: x: 4, y: 4, z: 4, core: 2. Of those that a mesh axis runs over, the one named last changes fastest.
Arguments:
- right_side: float32 [1024, 64, 128], P(('dom', 'bal')), may hold values from -100 to 100
- a_tiles: bfloat16 [1024, 5, 128, 128], P(('dom', 'bal')), may hold values from -4 to 4
- a_cols: int32 [1024, 5], P(('dom', 'bal')), may hold values from 0 to 1023, as said below
- m_tiles: bfloat16 [13312, 128, 128], P(('dom', 'bal')), may hold values from -2 to 2
- m_rows: int32 [13312], P(('dom', 'bal')), may hold values from 0 to 1023, as said below
- m_cols: int32 [13312], P(('dom', 'bal')), may hold values from 0 to 1023, as said below
- m_count: int32 [128], P(('dom', 'bal')), may hold values from 24 to 104, as said below
Outputs:
- solution: float32 [1024, 64, 128], P(('dom', 'bal'))
- residual: float32 [1024, 64, 128], P(('dom', 'bal'))
- basis: float32 [1024, 64, 128], P(('dom', 'bal'))
- shadow: float32 [1024, 64, 128], P(('dom', 'bal'))
The draws below stay inside these ranges and needn't reach their ends.
Inputs may be any that keep to these rules, and one draw needn't show every extreme that they name: a_cols[r, j] differs from r by at most 16, and every block row has a tile exactly 16 away. `m_rows`: the slots i * 104 to (i + 1) * 104 - 1 name block rows i * 8 to (i + 1) * 8 - 1, the rows of device i in the order of dom then bal. m_cols[s] differs from m_rows[s] by at most 32; on every device a live slot reaches exactly 32. The live slots of device i are its first m_count[i]; in every draw some device has all 104 live.
All inputs are finite; a program needn't handle non-finite values.
Results may differ from the reference program's by a relative error of at most 0.014.
Values may be sent and summed in bfloat16 or wider, within the bound.
No kernel may reach another device: no remote copies, remote signals or barrier semaphores. Data moves between devices by JAX's collectives and lax.ppermute only.
A program may use at most 64 MiB of HBM per device.

```python
import math
import jax
import jax.numpy as jnp
from jax import lax

BR_DEV = 8
TILE = 128
NRHS = 64
KA = 5
MKEEP = 13
ITERS = 2
REACH_A = 16
REACH_M = 32
TILE_DEV = 104
NB = 1024
MT = 13312


def draw_right_side(key, part):
    key_one, key_two = jax.random.split(key, 2)
    position = (jnp.arange(NB, dtype=jnp.float32)[:, None, None] * TILE + jnp.arange(TILE, dtype=jnp.float32)[None, None, :]) / (NB * TILE)
    column = jnp.exp(jax.random.uniform(key_two, (1, NRHS, 1), jnp.float32, math.log(0.3), math.log(3.0)))
    noise = jnp.clip(jax.random.normal(key_one, (NB, NRHS, TILE), jnp.float32), -4.0, 4.0)
    return noise * jnp.exp(position * math.log(3.0)) * column


def draw_a_tiles(key, part):
    key_one, key_two = jax.random.split(key)
    scale = 0.6 / math.sqrt(KA * TILE)
    noise = jnp.clip(jax.random.normal(key_one, (NB, KA, TILE, TILE), jnp.float32), -4.0, 4.0) * scale
    diag_vals = 1.5 + 1.5 * jax.random.uniform(key_two, (NB, 1, 1, TILE), jnp.float32)
    eye_mask = (jnp.arange(TILE)[:, None] == jnp.arange(TILE)[None, :]).astype(jnp.float32)
    first_slot = (jnp.arange(KA) == 0).astype(jnp.float32)[None, :, None, None]
    return (noise + first_slot * eye_mask[None, None] * diag_vals).astype(jnp.bfloat16)


def draw_a_cols(key, part):
    row_ids = jnp.arange(NB, dtype=jnp.int32)[:, None]
    offset = jax.random.randint(key, (NB, KA), -REACH_A, REACH_A + 1, dtype=jnp.int32)
    far_offset = jnp.where(row_ids + REACH_A < NB, REACH_A, -REACH_A)
    slot_ids = jnp.arange(KA, dtype=jnp.int32)[None, :]
    offset = jnp.where(slot_ids == 0, 0, jnp.where(slot_ids == 1, far_offset, offset))
    return jnp.clip(row_ids + offset, 0, NB - 1).astype(jnp.int32)


def tile_places(key):
    inner = jax.random.fold_in(key, 11)
    key_rows, key_cols = jax.random.split(inner)
    slot_ids = jnp.arange(MT, dtype=jnp.int32)
    owner_ids = slot_ids // TILE_DEV
    within = slot_ids % TILE_DEV
    spare_rows = jax.random.randint(key_rows, (MT,), 0, BR_DEV, dtype=jnp.int32)
    row_ids = owner_ids * BR_DEV + jnp.where(within < BR_DEV, within, spare_rows)
    offset = jax.random.randint(key_cols, (MT,), -REACH_M, REACH_M + 1, dtype=jnp.int32)
    far_offset = jnp.where(row_ids + REACH_M < NB, REACH_M, -REACH_M)
    offset = jnp.where(within < BR_DEV, 0, jnp.where(within == BR_DEV, far_offset, offset))
    col_ids = jnp.clip(row_ids + offset, 0, NB - 1)
    return (row_ids.astype(jnp.int32), col_ids.astype(jnp.int32))


def draw_m_rows(key, part):
    return tile_places(key)[0]


def draw_m_cols(key, part):
    return tile_places(key)[1]


def draw_m_tiles(key, part):
    key_one, key_two = jax.random.split(key)
    scale = 0.25 / math.sqrt(MKEEP * TILE)
    noise = jnp.clip(jax.random.normal(key_one, (MT, TILE, TILE), jnp.float32), -4.0, 4.0) * scale
    within = (jnp.arange(MT) % TILE_DEV)[:, None, None]
    diag_vals = 0.8 + 0.4 * jax.random.uniform(key_two, (MT, 1, TILE), jnp.float32)
    eye_mask = (jnp.arange(TILE)[:, None] == jnp.arange(TILE)[None, :]).astype(jnp.float32)
    return (noise + jnp.where(within < BR_DEV, 1.0, 0.0) * eye_mask[None] * diag_vals).astype(jnp.bfloat16)


def draw_m_count(key, part):
    key_one, key_two = jax.random.split(key)
    devices = NB // BR_DEV
    counts = jax.random.randint(key_one, (devices,), 3 * BR_DEV, 7 * BR_DEV + 1, dtype=jnp.int32)
    chosen = jax.random.randint(key_two, (), 0, devices, dtype=jnp.int32)
    return jnp.where(jnp.arange(devices, dtype=jnp.int32) == chosen, TILE_DEV, counts).astype(jnp.int32)


def setup_inputs(seed: int = 0) -> dict:
    seeds = jax.random.split(jax.random.key(seed), 8)
    return {
        "right_side": draw_right_side(jax.random.fold_in(seeds[7], 71), 0),
        "a_tiles": draw_a_tiles(jax.random.fold_in(seeds[7], 71), 0),
        "a_cols": draw_a_cols(jax.random.fold_in(seeds[7], 71), 0),
        "m_tiles": draw_m_tiles(jax.random.fold_in(seeds[7], 71), 0),
        "m_rows": draw_m_rows(jax.random.fold_in(seeds[7], 71), 0),
        "m_cols": draw_m_cols(jax.random.fold_in(seeds[7], 71), 0),
        "m_count": draw_m_count(jax.random.fold_in(seeds[7], 71), 0),
    }


HIGH = lax.Precision.HIGHEST

def gram(left, right):
    return jnp.einsum('bkc,blc->kl', left, right, precision=HIGH)

def times_small(vectors, small):
    return jnp.einsum('bkc,kl->blc', vectors, small, precision=HIGH)

def normalize(vectors, total_rows):
    lower_factor = jnp.linalg.cholesky(gram(vectors, vectors) / total_rows)
    identity = jnp.eye(vectors.shape[1], dtype=jnp.float32)
    inverse = jax.scipy.linalg.solve_triangular(lower_factor, identity, lower=True)
    return jnp.einsum('kl,blc->bkc', inverse, vectors, precision=HIGH)

def apply_a(a_tiles, a_cols, vector):
    vector = lax.optimization_barrier(vector)
    devices_count = NB // BR_DEV

    def one_block(pieces):
        tile_set, col_ids = pieces
        picked = vector[col_ids].astype(jnp.float32)
        return jnp.einsum('bjrc,bjic->bri', picked, tile_set.astype(jnp.float32))
    blocks = lax.map(one_block, (a_tiles.reshape(devices_count, BR_DEV, KA, TILE, TILE), a_cols.reshape(devices_count, BR_DEV, KA)))
    return blocks.reshape(NB, NRHS, TILE)

def apply_a_t(a_tiles, a_cols, vector):
    vector = lax.optimization_barrier(vector)
    devices_count = NB // BR_DEV

    def add_block(summed, pieces):
        tile_set, col_ids, part_vec = pieces
        contrib = jnp.einsum('bri,bjic->bjrc', part_vec.astype(jnp.float32), tile_set.astype(jnp.float32))
        return (summed.at[col_ids.reshape(-1)].add(contrib.reshape(-1, NRHS, TILE)), None)
    summed, ignored = lax.scan(add_block, jnp.zeros((NB, NRHS, TILE), jnp.float32), (a_tiles.reshape(devices_count, BR_DEV, KA, TILE, TILE), a_cols.reshape(devices_count, BR_DEV, KA), vector.reshape(devices_count, BR_DEV, NRHS, TILE)))
    return summed

def apply_m(m_tiles, m_rows, m_cols, m_count, vector):
    vector = lax.optimization_barrier(vector)
    devices_count = NB // BR_DEV

    def one_device(pieces):
        tile_set, row_ids, col_ids, live_count, device = pieces
        live_mask = (jnp.arange(TILE_DEV, dtype=jnp.int32) < live_count).astype(jnp.float32)
        picked = vector[col_ids].astype(jnp.float32)
        contrib = jnp.einsum('nrc,nic->nri', picked, tile_set.astype(jnp.float32)) * live_mask[:, None, None]
        local_rows = row_ids - device * BR_DEV
        return jax.ops.segment_sum(contrib, local_rows, num_segments=BR_DEV)
    blocks = lax.map(one_device, (m_tiles.reshape(devices_count, TILE_DEV, TILE, TILE), m_rows.reshape(devices_count, TILE_DEV), m_cols.reshape(devices_count, TILE_DEV), m_count, jnp.arange(devices_count, dtype=jnp.int32)))
    return blocks.reshape(NB, NRHS, TILE)

def apply_m_t(m_tiles, m_rows, m_cols, m_count, vector):
    vector = lax.optimization_barrier(vector)
    devices_count = NB // BR_DEV

    def add_device(summed, pieces):
        tile_set, row_ids, col_ids, live_count = pieces
        live_mask = (jnp.arange(TILE_DEV, dtype=jnp.int32) < live_count).astype(jnp.float32)
        picked = vector[row_ids].astype(jnp.float32)
        contrib = jnp.einsum('nri,nic->nrc', picked, tile_set.astype(jnp.float32)) * live_mask[:, None, None]
        return (summed.at[col_ids].add(contrib), None)
    summed, ignored = lax.scan(add_device, jnp.zeros((NB, NRHS, TILE), jnp.float32), (m_tiles.reshape(devices_count, TILE_DEV, TILE, TILE), m_rows.reshape(devices_count, TILE_DEV), m_cols.reshape(devices_count, TILE_DEV), m_count))
    return summed

def reference(right_side, a_tiles, a_cols, m_tiles, m_rows, m_cols, m_count):
    total_rows = NB * TILE
    basis = normalize(right_side, total_rows)
    shadow = basis
    solution = jnp.zeros_like(right_side)
    residual = right_side
    for iteration in range(ITERS):
        precond = apply_m(m_tiles, m_rows, m_cols, m_count, basis.astype(jnp.bfloat16))
        image = apply_a(a_tiles, a_cols, precond.astype(jnp.bfloat16))
        back = apply_a_t(a_tiles, a_cols, shadow.astype(jnp.bfloat16))
        back_image = apply_m_t(m_tiles, m_rows, m_cols, m_count, back.astype(jnp.bfloat16))
        coupling = gram(shadow, image) / total_rows
        factor = jnp.linalg.cholesky(gram(image, image))
        weights = jax.scipy.linalg.cho_solve((factor, True), gram(image, residual))
        solution = solution + times_small(precond, weights)
        residual = residual - times_small(image, weights)
        next_basis = image - times_small(basis, coupling)
        next_shadow = back_image - times_small(shadow, coupling.T)
        basis = normalize(next_basis, total_rows)
        shadow = normalize(next_shadow, total_rows)
    return (solution, residual, basis, shadow)
```

```python
import jax
import jax.numpy as jnp
from jax import lax
from jax.experimental import pallas as pl
from jax.experimental.pallas import tpu as pltpu
from jax.sharding import PartitionSpec as P

ITERS = 2
BR = 8
TILE = 128
K = 64
NT = (((1,), (1,)), ((), ()))
NN = (((1,), (0,)), ((), ()))
TN = (((0,), (0,)), ((), ()))
F32 = jnp.float32
BF16 = jnp.bfloat16
DOM, BAL = "dom", "bal"
UNROLL = 8


def hdot(a, b, dims=NN):
    return lax.dot_general(a, b, dims, precision=lax.Precision.HIGHEST, preferred_element_type=F32)


def bdot(a, b, dims):
    return lax.dot_general(a, b, dims, preferred_element_type=F32)


def swap(value, axis, size, distance):
    return lax.ppermute(value, axis, [(i, i ^ distance) for i in range(size)])


def swap_y(value, distance):
    return swap(value, BAL, lax.axis_size(BAL), distance)


def swap_core(value):
    return swap(value, DOM, lax.axis_size(DOM), 1)


def swap_next(value):
    size = lax.axis_size(DOM)
    route = []
    for i in range(1, size - 1, 2):
        route += [(i, i + 1), (i + 1, i)]
    return lax.ppermute(value, DOM, route)


def reduce_all(value):
    size = lax.axis_size(DOM)
    value = value + swap(value, DOM, size, 1)
    parts = [swap_y(value, k) for k in (1, 2, 3)]
    value = (value + parts[0]) + (parts[1] + parts[2])
    for unit in (2, 8):
        parts = [swap(value, DOM, size, k * unit) for k in (1, 2, 3)]
        value = (value + parts[0]) + (parts[1] + parts[2])
    return value


VM = pl.BlockSpec(memory_space=pltpu.VMEM)
SM = pl.BlockSpec(memory_space=pltpu.SMEM)


def call(body, name, specs, outs, scratch, args, flops=0, nbytes=0):
    return pl.pallas_call(
        body,
        name=name,
        in_specs=specs,
        out_specs=tuple(VM for _ in outs),
        out_shape=tuple(jax.ShapeDtypeStruct(s, d) for s, d in outs),
        scratch_shapes=scratch,
        cost_estimate=pl.CostEstimate(flops=flops, bytes_accessed=nbytes, transcendentals=0),
    )(*args)


def inverse_factors(mats):
    nb = K // 8
    row = lax.broadcasted_iota(jnp.int32, (8, K), 0)
    col = lax.broadcasted_iota(jnp.int32, (8, K), 1)
    work = []
    for g in mats:
        left = [g[8 * i : 8 * i + 8, :] for i in range(nb)]
        right = [jnp.where(row + 8 * i == col, 1.0, 0.0).astype(F32) for i in range(nb)]
        work.append((left, right))
    for k in range(K):
        kb, kr = divmod(k, 8)
        for left, right in work:
            prow = left[kb][kr : kr + 1, :]
            rrow = right[kb][kr : kr + 1, :]
            inv = 1.0 / prow[:, k : k + 1]
            prow = prow * inv
            rrow = rrow * inv
            for i in range(kb, nb):
                f = left[i][:, k : k + 1]
                if i == kb:
                    if kr == 7:
                        continue
                    f = jnp.where(row[:, :1] > kr, f, 0.0)
                left[i] = left[i] - f * prow
                right[i] = right[i] - f * rrow
    out = []
    for left, right in work:
        rows = []
        for i in range(nb):
            d = jnp.sum(jnp.where(row + 8 * i == col, left[i], 0.0), axis=1, keepdims=True)
            rows.append(right[i] * lax.rsqrt(d))
        out.append(jnp.concatenate(rows, axis=0))
    return out


def start_gram_kernel(x_ref, g_ref):
    g = jnp.zeros((K, K), F32)
    for b in range(BR):
        g = g + hdot(x_ref[b], x_ref[b], NT)
    g_ref[...] = g


def start_norm_kernel(g_ref, x_ref, n_ref, basis_ref, low_ref):
    (inv,) = inverse_factors([g_ref[...] * (1.0 / n_ref[0])])
    for b in range(BR):
        v = hdot(inv, x_ref[b])
        basis_ref[b] = v
        low_ref[b] = v.astype(BF16)


def apply_m_kernel(col_ref, row_ref, own_ref, cp_ref, zp_ref, tiles_ref, out_ref, low_ref, win, acc):
    win[0:32] = own_ref[...]
    win[32:64] = cp_ref[...]
    win[64:96] = zp_ref[...]
    acc[...] = jnp.zeros_like(acc)
    slots = tiles_ref.shape[0]

    def step(s, carry):
        base = s * UNROLL
        parts = []
        for u in range(UNROLL):
            parts.append(bdot(win[col_ref[base + u]], tiles_ref[base + u], NT))
        for u in range(UNROLL):
            r = row_ref[base + u]
            acc[r] = acc[r] + parts[u]
        return carry

    lax.fori_loop(0, slots // UNROLL, step, 0)
    for b in range(BR):
        v = acc[b]
        out_ref[b] = v
        low_ref[b] = v.astype(BF16)


def apply_mt_kernel(col_ref, row_ref, back0_ref, b1_ref, b2_ref, b3_ref, tiles_ref, own_ref, cp_ref, zp_ref, low, acc):
    for b in range(BR):
        v = back0_ref[b] + b1_ref[b].astype(F32) + b2_ref[b].astype(F32) + b3_ref[b].astype(F32)
        low[b] = v.astype(BF16)
    low[BR] = jnp.zeros((K, TILE), BF16)
    acc[...] = jnp.zeros_like(acc)
    slots = tiles_ref.shape[0]

    def step(s, carry):
        base = s * UNROLL
        parts = []
        for u in range(UNROLL):
            parts.append(bdot(low[row_ref[base + u]], tiles_ref[base + u], NN))
        for u in range(UNROLL):
            c = col_ref[base + u]
            acc[c] = acc[c] + parts[u]
        return carry

    lax.fori_loop(0, slots // UNROLL, step, 0)
    own_ref[...] = acc[0:32]
    cp_ref[...] = acc[32:64].astype(BF16)
    zp_ref[...] = acc[64:96].astype(BF16)


def apply_at_kernel(col_ref, low_ref, tiles_ref, own_ref, cp_ref, zp_ref, acc):
    acc[...] = jnp.zeros_like(acc)
    slots = tiles_ref.shape[1]
    for b in range(BR):
        x = low_ref[b]
        parts = [bdot(x, tiles_ref[b, j], NN) for j in range(slots)]
        for j in range(slots):
            c = col_ref[b * slots + j]
            acc[c] = acc[c] + parts[j]
    own_ref[...] = acc[0:32]
    cp_ref[...] = acc[32:48].astype(BF16)
    zp_ref[...] = acc[48:64].astype(BF16)


def collect_a_kernel(own_ref, cp_ref, zp_ref, o0_ref, o1_ref, o2_ref, o3_ref):
    o0_ref[...] = own_ref[0:8]
    o1_ref[...] = own_ref[8:16].astype(BF16)
    o2_ref[...] = (own_ref[16:24] + cp_ref[0:8].astype(F32) + zp_ref[0:8].astype(F32)).astype(BF16)
    o3_ref[...] = (own_ref[24:32] + cp_ref[8:16].astype(F32) + zp_ref[8:16].astype(F32)).astype(BF16)


def collect_m_kernel(own_ref, cp_ref, zp_ref, o0_ref, o1_ref, o2_ref, o3_ref):
    v = own_ref[...] + cp_ref[...].astype(F32) + zp_ref[...].astype(F32)
    o0_ref[...] = v[0:8]
    o1_ref[...] = v[8:16].astype(BF16)
    o2_ref[...] = v[16:24].astype(BF16)
    o3_ref[...] = v[24:32].astype(BF16)


def apply_a_kernel(col_ref, own_ref, cp_ref, zp_ref, tiles_ref, basis_ref, shadow_ref, res_ref, image_ref, g_ref, win):
    win[0:32] = own_ref[...]
    win[32:48] = cp_ref[...]
    win[48:64] = zp_ref[...]
    slots = tiles_ref.shape[1]
    gs = gi = gr = gb = None
    for b in range(BR):
        v = None
        for j in range(slots):
            p = bdot(win[col_ref[b * slots + j]], tiles_ref[b, j], NT)
            v = p if v is None else v + p
        image_ref[b] = v
        ps, pi, pr, pb = (hdot(v, o, NT) for o in (shadow_ref[b], v, res_ref[b], basis_ref[b]))
        if b == 0:
            gs, gi, gr, gb = ps, pi, pr, pb
        else:
            gs, gi, gr, gb = gs + ps, gi + pi, gr + pr, gb + pb
    g_ref[0:64, 0:64] = gs
    g_ref[0:64, 64:128] = gi
    g_ref[64:128, 0:64] = gr
    g_ref[64:128, 64:128] = gb


def back_gram_kernel(o0_ref, b1_ref, b2_ref, b3_ref, shadow_ref, bi_ref, g_ref):
    gb = gs = None
    for b in range(BR):
        v = o0_ref[b] + b1_ref[b].astype(F32) + b2_ref[b].astype(F32) + b3_ref[b].astype(F32)
        bi_ref[b] = v
        pb, ps = hdot(v, v, NT), hdot(v, shadow_ref[b], NT)
        gb, gs = (pb, ps) if b == 0 else (gb + pb, gs + ps)
    g_ref[:, 0:64] = gb
    g_ref[:, 64:128] = gs


def update_kernel(first, last, g_ref, n_ref, image_ref, bi_ref, basis_ref, shadow_ref, precond_ref, res_ref, *refs):
    if first:
        sol_ref, outs = None, refs
    else:
        sol_ref, outs = refs[0], refs[1:]
    if last:
        sol_out, res_out, basis_out, shadow_out = outs
    else:
        sol_out, res_out, basis_out, shadow_out, blow_out, slow_out = outs
    total = n_ref[0]
    coup_t = g_ref[0:64, 0:64] * (1.0 / total)
    coup = coup_t.T
    normal = g_ref[0:64, 64:128]
    target = g_ref[64:128, 0:64]
    ib = g_ref[64:128, 64:128]
    bb = g_ref[128:192, 0:64]
    bs = g_ref[128:192, 64:128]
    y = hdot(ib, coup)
    uu = normal - y - y.T + total * hdot(coup_t, coup)
    y = hdot(bs, coup_t)
    ss = bb - y - y.T + total * hdot(coup, coup_t)
    inv_n, inv_u, inv_s = inverse_factors([normal, uu * (1.0 / total), ss * (1.0 / total)])
    w_t = hdot(hdot(inv_n, target), inv_n, TN)
    for b in range(BR):
        image = image_ref[b]
        v = hdot(w_t, precond_ref[b])
        sol_out[b] = v if first else sol_ref[b] + v
        res_out[b] = res_ref[b] - hdot(w_t, image)
        v = hdot(inv_u, image - hdot(coup_t, basis_ref[b]))
        basis_out[b] = v
        if not last:
            blow_out[b] = v.astype(BF16)
        v = hdot(inv_s, bi_ref[b] - hdot(coup, shadow_ref[b]))
        shadow_out[b] = v
        if not last:
            slow_out[b] = v.astype(BF16)


def shards(right_side, a_tiles, a_cols, m_tiles, m_rows, m_cols, m_count):
    blk = (BR, K, TILE)
    total = BR * TILE * lax.axis_size((DOM, BAL))
    group = lax.axis_index(DOM)
    y = lax.axis_index(BAL)
    first_row = (group * lax.axis_size(BAL) + y) * BR
    n_arr = jnp.full((1,), float(total), F32)

    def place(cols, skip):
        dev = cols // BR
        g, rel = dev // 4, (dev % 4) ^ y
        width = 4 - skip
        local = jnp.where(
            g == group, rel, jnp.where(g == (group ^ 1), 4 + rel - skip, 4 + width + rel - skip)
        )
        return local * BR + cols % BR

    a_place = place(a_cols, 2).reshape(-1)
    m_place = place(m_cols, 0)
    live = jnp.arange(m_tiles.shape[0], dtype=jnp.int32) < m_count[0]
    m_local = jnp.where(live, m_rows - first_row, BR)

    def fetch4(low):
        return jnp.concatenate([low] + [swap_y(low, k) for k in (1, 2, 3)], 0)

    (g0,) = call(start_gram_kernel, "start_gram", [VM], [((K, K), F32)], [], (right_side,))
    g0 = reduce_all(g0)
    basis, blow = call(
        start_norm_kernel, "start_norm", [VM, VM, SM], [(blk, F32), (blk, BF16)], [], (g0, right_side, n_arr)
    )
    shadow, slow = basis, blow
    solution, residual = None, right_side
    for iteration in range(ITERS):
        last = iteration == ITERS - 1
        own4 = fetch4(blow)
        pa_own, pa_cp, pa_zp = call(
            apply_at_kernel,
            "apply_at",
            [SM, VM, VM],
            [((32, K, TILE), F32), ((16, K, TILE), BF16), ((16, K, TILE), BF16)],
            [pltpu.VMEM((64, K, TILE), F32)],
            (a_place, slow, a_tiles),
            flops=84_000_000,
            nbytes=3_000_000,
        )
        ra_zp = swap_next(pa_zp)
        ra_cp = swap_core(pa_cp)
        m_zp = swap_next(own4)
        m_cp = swap_core(own4)
        precond, plow = call(
            apply_m_kernel,
            "apply_m",
            [SM, SM, VM, VM, VM, VM],
            [(blk, F32), (blk, BF16)],
            [pltpu.VMEM((96, K, TILE), BF16), pltpu.VMEM((BR + 1, K, TILE), F32)],
            (m_place, m_local, own4, m_cp, m_zp, m_tiles),
            flops=218_000_000,
            nbytes=5_000_000,
        )
        o0, o1, o2, o3 = call(
            collect_a_kernel,
            "collect_a",
            [VM] * 3,
            [(blk, F32)] + [(blk, BF16)] * 3,
            [],
            (pa_own, ra_cp, ra_zp),
        )
        b1, b2, b3 = swap_y(o1, 1), swap_y(o2, 2), swap_y(o3, 3)
        pown4 = fetch4(plow)
        pm_own, pm_cp, pm_zp = call(
            apply_mt_kernel,
            "apply_mt",
            [SM, SM] + [VM] * 5,
            [((32, K, TILE), F32), ((32, K, TILE), BF16), ((32, K, TILE), BF16)],
            [pltpu.VMEM((BR + 1, K, TILE), BF16), pltpu.VMEM((96, K, TILE), F32)],
            (m_place, m_local, o0, b1, b2, b3, m_tiles),
            flops=218_000_000,
            nbytes=5_000_000,
        )
        a_zp = swap_next(pown4[16:32])
        a_cp = swap_core(pown4[16:32])
        rm_zp = swap_next(pm_zp)
        rm_cp = swap_core(pm_cp)
        image, g_fwd = call(
            apply_a_kernel,
            "apply_a",
            [SM] + [VM] * 7,
            [(blk, F32), ((128, 128), F32)],
            [pltpu.VMEM((64, K, TILE), BF16)],
            (a_place, pown4, a_cp, a_zp, a_tiles, basis, shadow, residual),
            flops=84_000_000,
            nbytes=3_000_000,
        )
        o0, o1, o2, o3 = call(
            collect_m_kernel,
            "collect_m",
            [VM] * 3,
            [(blk, F32)] + [(blk, BF16)] * 3,
            [],
            (pm_own, rm_cp, rm_zp),
        )
        b1, b2, b3 = swap_y(o1, 1), swap_y(o2, 2), swap_y(o3, 3)
        back_image, g_bwd = call(
            back_gram_kernel,
            "back_gram",
            [VM] * 5,
            [(blk, F32), ((64, 128), F32)],
            [],
            (o0, b1, b2, b3, shadow),
        )
        grams = reduce_all(jnp.concatenate([g_fwd, g_bwd], 0))
        args = [grams, n_arr, image, back_image, basis, shadow, precond, residual]
        if iteration:
            args.append(solution)
        outs = [(blk, F32)] * 4 + ([] if last else [(blk, BF16)] * 2)
        result = call(
            lambda *refs, f=iteration == 0, l=last: update_kernel(f, l, *refs),
            "update",
            [VM, SM] + [VM] * (len(args) - 2),
            outs,
            [],
            args,
        )
        solution, residual, basis, shadow = result[:4]
        if not last:
            blow, slow = result[4:]
    return (solution, residual, basis, shadow)


def solution(mesh):
    rows = P((DOM, BAL))
    return jax.shard_map(
        shards,
        mesh=mesh,
        in_specs=(rows,) * 7,
        out_specs=(rows,) * 4,
        check_vma=False,
    )
```

```python
import jax
import jax.numpy as jnp
from jax import lax
from jax.experimental import pallas as pl
from jax.experimental.pallas import tpu as pltpu
from jax.sharding import PartitionSpec as P

ITERS = 2
BR = 8
TILE = 128
K = 64
NT = (((1,), (1,)), ((), ()))
NN = (((1,), (0,)), ((), ()))
TN = (((0,), (0,)), ((), ()))
F32 = jnp.float32
BF16 = jnp.bfloat16
DOM, BAL = "dom", "bal"
UNROLL = 8


def hdot(a, b, dims=NN):
    return lax.dot_general(a, b, dims, precision=lax.Precision.HIGHEST, preferred_element_type=F32)


def bdot(a, b, dims):
    return lax.dot_general(a, b, dims, preferred_element_type=F32)


def swap(value, axis, size, distance):
    return lax.ppermute(value, axis, [(i, i ^ distance) for i in range(size)])


def swap_y(value, distance):
    return swap(value, BAL, lax.axis_size(BAL), distance)


def swap_core(value):
    return swap(value, DOM, lax.axis_size(DOM), 1)


def swap_next(value):
    size = lax.axis_size(DOM)
    route = []
    for i in range(1, size - 1, 2):
        route += [(i, i + 1), (i + 1, i)]
    return lax.ppermute(value, DOM, route)


def reduce_all(value):
    size = lax.axis_size(DOM)
    value = value + swap(value, DOM, size, 1)
    parts = [swap_y(value, k) for k in (1, 2, 3)]
    value = (value + parts[0]) + (parts[1] + parts[2])
    for unit in (2, 8):
        parts = [swap(value, DOM, size, k * unit) for k in (1, 2, 3)]
        value = (value + parts[0]) + (parts[1] + parts[2])
    return value


VM = pl.BlockSpec(memory_space=pltpu.VMEM)
SM = pl.BlockSpec(memory_space=pltpu.SMEM)


def call(body, name, specs, outs, scratch, args, flops=0, nbytes=0, final=False):
    args = [pltpu.with_memory_space_constraint(a, pltpu.VMEM) if s is VM else a for s, a in zip(specs, args)]
    return pl.pallas_call(
        body,
        name=name,
        in_specs=specs,
        out_specs=tuple(VM for _ in outs),
        out_shape=tuple(jax.ShapeDtypeStruct(s, d) if final else pltpu.VMEM(s, d) for s, d in outs),
        scratch_shapes=scratch,
        compiler_params=pltpu.CompilerParams(vmem_limit_bytes=24 * 2**20),
        cost_estimate=pl.CostEstimate(flops=flops, bytes_accessed=nbytes, transcendentals=0),
    )(*args)


def inverse_factors(mats):
    nb = K // 8
    row = lax.broadcasted_iota(jnp.int32, (8, K), 0)
    col = lax.broadcasted_iota(jnp.int32, (8, K), 1)
    work = []
    for g in mats:
        left = [g[8 * i : 8 * i + 8, :] for i in range(nb)]
        right = [jnp.where(row + 8 * i == col, 1.0, 0.0).astype(F32) for i in range(nb)]
        work.append((left, right))
    for k in range(K):
        kb, kr = divmod(k, 8)
        for left, right in work:
            prow = left[kb][kr : kr + 1, :]
            rrow = right[kb][kr : kr + 1, :]
            inv = 1.0 / prow[:, k : k + 1]
            prow = prow * inv
            rrow = rrow * inv
            for i in range(kb, nb):
                f = left[i][:, k : k + 1]
                if i == kb:
                    if kr == 7:
                        continue
                    f = jnp.where(row[:, :1] > kr, f, 0.0)
                left[i] = left[i] - f * prow
                right[i] = right[i] - f * rrow
    out = []
    for left, right in work:
        rows = []
        for i in range(nb):
            d = jnp.sum(jnp.where(row + 8 * i == col, left[i], 0.0), axis=1, keepdims=True)
            rows.append(right[i] * lax.rsqrt(d))
        out.append(jnp.concatenate(rows, axis=0))
    return out


def start_gram_kernel(x_ref, g_ref):
    g = jnp.zeros((K, K), F32)
    for b in range(BR):
        g = g + hdot(x_ref[b], x_ref[b], NT)
    g_ref[...] = g


def start_norm_kernel(g_ref, x_ref, n_ref, basis_ref, low_ref):
    (inv,) = inverse_factors([g_ref[...] * (1.0 / n_ref[0])])
    for b in range(BR):
        v = hdot(inv, x_ref[b])
        basis_ref[b] = v
        low_ref[b] = v.astype(BF16)


def apply_m_kernel(col_ref, row_ref, own_ref, cp_ref, zp_ref, tiles_ref, out_ref, low_ref, win, acc):
    win[0:32] = own_ref[...]
    win[32:64] = cp_ref[...]
    win[64:96] = zp_ref[...]
    acc[...] = jnp.zeros_like(acc)
    slots = tiles_ref.shape[0]

    def step(s, carry):
        base = s * UNROLL
        parts = []
        for u in range(UNROLL):
            parts.append(bdot(win[col_ref[base + u]], tiles_ref[base + u], NT))
        for u in range(UNROLL):
            r = row_ref[base + u]
            acc[r] = acc[r] + parts[u]
        return carry

    lax.fori_loop(0, slots // UNROLL, step, 0)
    for b in range(BR):
        v = acc[b]
        out_ref[b] = v
        low_ref[b] = v.astype(BF16)


def apply_mt_kernel(col_ref, row_ref, back0_ref, b1_ref, b2_ref, b3_ref, tiles_ref, own_ref, cp_ref, zp_ref, low, acc):
    for b in range(BR):
        v = back0_ref[b] + b1_ref[b].astype(F32) + b2_ref[b].astype(F32) + b3_ref[b].astype(F32)
        low[b] = v.astype(BF16)
    low[BR] = jnp.zeros((K, TILE), BF16)
    acc[...] = jnp.zeros_like(acc)
    slots = tiles_ref.shape[0]

    def step(s, carry):
        base = s * UNROLL
        parts = []
        for u in range(UNROLL):
            parts.append(bdot(low[row_ref[base + u]], tiles_ref[base + u], NN))
        for u in range(UNROLL):
            c = col_ref[base + u]
            acc[c] = acc[c] + parts[u]
        return carry

    lax.fori_loop(0, slots // UNROLL, step, 0)
    own_ref[...] = acc[0:32]
    cp_ref[...] = acc[32:64].astype(BF16)
    zp_ref[...] = acc[64:96].astype(BF16)


def apply_at_kernel(col_ref, low_ref, tiles_ref, own_ref, cp_ref, zp_ref, acc):
    acc[...] = jnp.zeros_like(acc)
    slots = tiles_ref.shape[1]
    for b in range(BR):
        x = low_ref[b]
        parts = [bdot(x, tiles_ref[b, j], NN) for j in range(slots)]
        for j in range(slots):
            c = col_ref[b * slots + j]
            acc[c] = acc[c] + parts[j]
    own_ref[...] = acc[0:32]
    cp_ref[...] = acc[32:48].astype(BF16)
    zp_ref[...] = acc[48:64].astype(BF16)


def collect_a_kernel(own_ref, cp_ref, zp_ref, o0_ref, o1_ref, o2_ref, o3_ref):
    o0_ref[...] = own_ref[0:8]
    o1_ref[...] = own_ref[8:16].astype(BF16)
    o2_ref[...] = (own_ref[16:24] + cp_ref[0:8].astype(F32) + zp_ref[0:8].astype(F32)).astype(BF16)
    o3_ref[...] = (own_ref[24:32] + cp_ref[8:16].astype(F32) + zp_ref[8:16].astype(F32)).astype(BF16)


def collect_m_kernel(own_ref, cp_ref, zp_ref, o0_ref, o1_ref, o2_ref, o3_ref):
    v = own_ref[...] + cp_ref[...].astype(F32) + zp_ref[...].astype(F32)
    o0_ref[...] = v[0:8]
    o1_ref[...] = v[8:16].astype(BF16)
    o2_ref[...] = v[16:24].astype(BF16)
    o3_ref[...] = v[24:32].astype(BF16)


def apply_a_kernel(col_ref, own_ref, cp_ref, zp_ref, tiles_ref, basis_ref, shadow_ref, res_ref, image_ref, g_ref, win):
    win[0:32] = own_ref[...]
    win[32:48] = cp_ref[...]
    win[48:64] = zp_ref[...]
    slots = tiles_ref.shape[1]
    gs = gi = gr = gb = None
    for b in range(BR):
        v = None
        for j in range(slots):
            p = bdot(win[col_ref[b * slots + j]], tiles_ref[b, j], NT)
            v = p if v is None else v + p
        image_ref[b] = v
        ps, pi, pr, pb = (hdot(v, o, NT) for o in (shadow_ref[b], v, res_ref[b], basis_ref[b]))
        if b == 0:
            gs, gi, gr, gb = ps, pi, pr, pb
        else:
            gs, gi, gr, gb = gs + ps, gi + pi, gr + pr, gb + pb
    g_ref[0:64, 0:64] = gs
    g_ref[0:64, 64:128] = gi
    g_ref[64:128, 0:64] = gr
    g_ref[64:128, 64:128] = gb


def back_gram_kernel(o0_ref, b1_ref, b2_ref, b3_ref, shadow_ref, bi_ref, g_ref):
    gb = gs = None
    for b in range(BR):
        v = o0_ref[b] + b1_ref[b].astype(F32) + b2_ref[b].astype(F32) + b3_ref[b].astype(F32)
        bi_ref[b] = v
        pb, ps = hdot(v, v, NT), hdot(v, shadow_ref[b], NT)
        gb, gs = (pb, ps) if b == 0 else (gb + pb, gs + ps)
    g_ref[:, 0:64] = gb
    g_ref[:, 64:128] = gs


def update_kernel(first, last, g_ref, n_ref, image_ref, bi_ref, basis_ref, shadow_ref, precond_ref, res_ref, *refs):
    if first:
        sol_ref, outs = None, refs
    else:
        sol_ref, outs = refs[0], refs[1:]
    if last:
        sol_out, res_out, basis_out, shadow_out = outs
    else:
        sol_out, res_out, basis_out, shadow_out, blow_out, slow_out = outs
    total = n_ref[0]
    coup_t = g_ref[0:64, 0:64] * (1.0 / total)
    coup = coup_t.T
    normal = g_ref[0:64, 64:128]
    target = g_ref[64:128, 0:64]
    ib = g_ref[64:128, 64:128]
    bb = g_ref[128:192, 0:64]
    bs = g_ref[128:192, 64:128]
    y = hdot(ib, coup)
    uu = normal - y - y.T + total * hdot(coup_t, coup)
    y = hdot(bs, coup_t)
    ss = bb - y - y.T + total * hdot(coup, coup_t)
    inv_n, inv_u, inv_s = inverse_factors([normal, uu * (1.0 / total), ss * (1.0 / total)])
    w_t = hdot(hdot(inv_n, target), inv_n, TN)
    for b in range(BR):
        image = image_ref[b]
        v = hdot(w_t, precond_ref[b])
        sol_out[b] = v if first else sol_ref[b] + v
        res_out[b] = res_ref[b] - hdot(w_t, image)
        v = hdot(inv_u, image - hdot(coup_t, basis_ref[b]))
        basis_out[b] = v
        if not last:
            blow_out[b] = v.astype(BF16)
        v = hdot(inv_s, bi_ref[b] - hdot(coup, shadow_ref[b]))
        shadow_out[b] = v
        if not last:
            slow_out[b] = v.astype(BF16)


def shards(right_side, a_tiles, a_cols, m_tiles, m_rows, m_cols, m_count):
    blk = (BR, K, TILE)
    total = BR * TILE * lax.axis_size((DOM, BAL))
    group = lax.axis_index(DOM)
    y = lax.axis_index(BAL)
    first_row = (group * lax.axis_size(BAL) + y) * BR
    n_arr = jnp.full((1,), float(total), F32)

    def place(cols, skip):
        dev = cols // BR
        g, rel = dev // 4, (dev % 4) ^ y
        width = 4 - skip
        local = jnp.where(
            g == group, rel, jnp.where(g == (group ^ 1), 4 + rel - skip, 4 + width + rel - skip)
        )
        return local * BR + cols % BR

    a_place = place(a_cols, 2).reshape(-1)
    m_place = place(m_cols, 0)
    live = jnp.arange(m_tiles.shape[0], dtype=jnp.int32) < m_count[0]
    m_local = jnp.where(live, m_rows - first_row, BR)

    def fetch4(low):
        return jnp.concatenate([low] + [swap_y(low, k) for k in (1, 2, 3)], 0)

    (g0,) = call(start_gram_kernel, "start_gram", [VM], [((K, K), F32)], [], (right_side,))
    g0 = reduce_all(g0)
    basis, blow = call(
        start_norm_kernel, "start_norm", [VM, VM, SM], [(blk, F32), (blk, BF16)], [], (g0, right_side, n_arr)
    )
    shadow, slow = basis, blow
    solution, residual = None, right_side
    for iteration in range(ITERS):
        last = iteration == ITERS - 1
        own4 = fetch4(blow)
        pa_own, pa_cp, pa_zp = call(
            apply_at_kernel,
            "apply_at",
            [SM, VM, VM],
            [((32, K, TILE), F32), ((16, K, TILE), BF16), ((16, K, TILE), BF16)],
            [pltpu.VMEM((64, K, TILE), F32)],
            (a_place, slow, a_tiles),
            flops=84_000_000,
            nbytes=3_000_000,
        )
        ra_zp = swap_next(pa_zp)
        ra_cp = swap_core(pa_cp)
        m_zp = swap_next(own4)
        m_cp = swap_core(own4)
        precond, plow = call(
            apply_m_kernel,
            "apply_m",
            [SM, SM, VM, VM, VM, VM],
            [(blk, F32), (blk, BF16)],
            [pltpu.VMEM((96, K, TILE), BF16), pltpu.VMEM((BR + 1, K, TILE), F32)],
            (m_place, m_local, own4, m_cp, m_zp, m_tiles),
            flops=218_000_000,
            nbytes=5_000_000,
        )
        o0, o1, o2, o3 = call(
            collect_a_kernel,
            "collect_a",
            [VM] * 3,
            [(blk, F32)] + [(blk, BF16)] * 3,
            [],
            (pa_own, ra_cp, ra_zp),
        )
        b1, b2, b3 = swap_y(o1, 1), swap_y(o2, 2), swap_y(o3, 3)
        pown4 = fetch4(plow)
        pm_own, pm_cp, pm_zp = call(
            apply_mt_kernel,
            "apply_mt",
            [SM, SM] + [VM] * 5,
            [((32, K, TILE), F32), ((32, K, TILE), BF16), ((32, K, TILE), BF16)],
            [pltpu.VMEM((BR + 1, K, TILE), BF16), pltpu.VMEM((96, K, TILE), F32)],
            (m_place, m_local, o0, b1, b2, b3, m_tiles),
            flops=218_000_000,
            nbytes=5_000_000,
        )
        a_zp = swap_next(pown4[16:32])
        a_cp = swap_core(pown4[16:32])
        rm_zp = swap_next(pm_zp)
        rm_cp = swap_core(pm_cp)
        image, g_fwd = call(
            apply_a_kernel,
            "apply_a",
            [SM] + [VM] * 7,
            [(blk, F32), ((128, 128), F32)],
            [pltpu.VMEM((64, K, TILE), BF16)],
            (a_place, pown4, a_cp, a_zp, a_tiles, basis, shadow, residual),
            flops=84_000_000,
            nbytes=3_000_000,
        )
        o0, o1, o2, o3 = call(
            collect_m_kernel,
            "collect_m",
            [VM] * 3,
            [(blk, F32)] + [(blk, BF16)] * 3,
            [],
            (pm_own, rm_cp, rm_zp),
        )
        b1, b2, b3 = swap_y(o1, 1), swap_y(o2, 2), swap_y(o3, 3)
        back_image, g_bwd = call(
            back_gram_kernel,
            "back_gram",
            [VM] * 5,
            [(blk, F32), ((64, 128), F32)],
            [],
            (o0, b1, b2, b3, shadow),
        )
        grams = reduce_all(jnp.concatenate([g_fwd, g_bwd], 0))
        args = [grams, n_arr, image, back_image, basis, shadow, precond, residual]
        if iteration:
            args.append(solution)
        outs = [(blk, F32)] * 4 + ([] if last else [(blk, BF16)] * 2)
        result = call(
            lambda *refs, f=iteration == 0, l=last: update_kernel(f, l, *refs),
            "update",
            [VM, SM] + [VM] * (len(args) - 2),
            outs,
            [],
            args,
            final=last,
        )
        solution, residual, basis, shadow = result[:4]
        if not last:
            blow, slow = result[4:]
    return (solution, residual, basis, shadow)


def solution(mesh):
    rows = P((DOM, BAL))
    return jax.shard_map(
        shards,
        mesh=mesh,
        in_specs=(rows,) * 7,
        out_specs=(rows,) * 4,
        check_vma=False,
    )
```

```python
import jax
import jax.numpy as jnp
from jax import lax
from jax.experimental import pallas as pl
from jax.experimental.pallas import tpu as pltpu
from jax.sharding import PartitionSpec as P

ITERS = 2
BR = 8
TILE = 128
K = 64
NT = (((1,), (1,)), ((), ()))
NN = (((1,), (0,)), ((), ()))
TN = (((0,), (0,)), ((), ()))
F32 = jnp.float32
BF16 = jnp.bfloat16
DOM, BAL = "dom", "bal"
UNROLL = 8


def hdot(a, b, dims=NN):
    return lax.dot_general(a, b, dims, precision=lax.Precision.HIGHEST, preferred_element_type=F32)


def bdot(a, b, dims):
    return lax.dot_general(a, b, dims, preferred_element_type=F32)


def swap(value, axis, size, distance):
    return lax.ppermute(value, axis, [(i, i ^ distance) for i in range(size)])


def swap_y(value, distance):
    return swap(value, BAL, lax.axis_size(BAL), distance)


def swap_core(value):
    return swap(value, DOM, lax.axis_size(DOM), 1)


def swap_next(value):
    size = lax.axis_size(DOM)
    route = []
    for i in range(1, size - 1, 2):
        route += [(i, i + 1), (i + 1, i)]
    return lax.ppermute(value, DOM, route)


def reduce_all(value):
    size = lax.axis_size(DOM)
    value = value + swap(value, DOM, size, 1)
    parts = [swap_y(value, k) for k in (1, 2, 3)]
    value = (value + parts[0]) + (parts[1] + parts[2])
    for unit in (2, 8):
        parts = [swap(value, DOM, size, k * unit) for k in (1, 2, 3)]
        value = (value + parts[0]) + (parts[1] + parts[2])
    return value


VM = pl.BlockSpec(memory_space=pltpu.VMEM)
SM = pl.BlockSpec(memory_space=pltpu.SMEM)


def call(body, name, specs, outs, scratch, args, flops=0, nbytes=0, final=False):
    args = [pltpu.with_memory_space_constraint(a, pltpu.VMEM) if s is VM else a for s, a in zip(specs, args)]
    return pl.pallas_call(
        body,
        name=name,
        in_specs=specs,
        out_specs=tuple(VM for _ in outs),
        out_shape=tuple(jax.ShapeDtypeStruct(s, d) if final else pltpu.VMEM(s, d) for s, d in outs),
        scratch_shapes=scratch,
        compiler_params=pltpu.CompilerParams(vmem_limit_bytes=24 * 2**20),
        cost_estimate=pl.CostEstimate(flops=flops, bytes_accessed=nbytes, transcendentals=0),
    )(*args)


def inverse_factors(mats):
    nb = K // 8
    row = lax.broadcasted_iota(jnp.int32, (8, K), 0)
    col = lax.broadcasted_iota(jnp.int32, (8, K), 1)
    work = []
    for g in mats:
        left = [g[8 * i : 8 * i + 8, :] for i in range(nb)]
        right = [jnp.where(row + 8 * i == col, 1.0, 0.0).astype(F32) for i in range(nb)]
        work.append((left, right))
    for k in range(K):
        kb, kr = divmod(k, 8)
        for left, right in work:
            prow = left[kb][kr : kr + 1, :]
            rrow = right[kb][kr : kr + 1, :]
            inv = 1.0 / prow[:, k : k + 1]
            prow = prow * inv
            rrow = rrow * inv
            for i in range(kb, nb):
                f = left[i][:, k : k + 1]
                if i == kb:
                    if kr == 7:
                        continue
                    f = jnp.where(row[:, :1] > kr, f, 0.0)
                left[i] = left[i] - f * prow
                right[i] = right[i] - f * rrow
    out = []
    for left, right in work:
        rows = []
        for i in range(nb):
            d = jnp.sum(jnp.where(row + 8 * i == col, left[i], 0.0), axis=1, keepdims=True)
            rows.append(right[i] * lax.rsqrt(d))
        out.append(jnp.concatenate(rows, axis=0))
    return out


def start_gram_kernel(x_ref, g_ref):
    g = jnp.zeros((K, K), F32)
    for b in range(BR):
        g = g + hdot(x_ref[b], x_ref[b], NT)
    g_ref[...] = g


def start_norm_kernel(g_ref, x_ref, n_ref, basis_ref, low_ref):
    (inv,) = inverse_factors([g_ref[...] * (1.0 / n_ref[0])])
    for b in range(BR):
        v = hdot(inv, x_ref[b])
        basis_ref[b] = v
        low_ref[b] = v.astype(BF16)


def pack_kernel(low_ref, q1_ref, q2_ref, q3_ref, pa_cp_ref, pa_zp_ref, cp_ref, zp_ref):
    for out, part in ((cp_ref, pa_cp_ref), (zp_ref, pa_zp_ref)):
        for k, src in enumerate((low_ref, q1_ref, q2_ref, q3_ref)):
            out[8 * k : 8 * k + 8] = src[...]
        out[32:48] = part[...]


def apply_m_kernel(
    col_ref, row_ref, low_ref, q1_ref, q2_ref, q3_ref, cp_ref, zp_ref, tiles_ref, pa_ref,
    out_ref, plow_ref, s1_ref, s2_ref, s3_ref, pa0_ref, win, acc,
):
    for k, src in enumerate((low_ref, q1_ref, q2_ref, q3_ref)):
        win[8 * k : 8 * k + 8] = src[...]
    win[32:64] = cp_ref[0:32]
    win[64:96] = zp_ref[0:32]
    acc[...] = jnp.zeros_like(acc)
    slots = tiles_ref.shape[0]

    def step(s, carry):
        base = s * UNROLL
        parts = []
        for u in range(UNROLL):
            parts.append(bdot(win[col_ref[base + u]], tiles_ref[base + u], NT))
        for u in range(UNROLL):
            r = row_ref[base + u]
            acc[r] = acc[r] + parts[u]
        return carry

    lax.fori_loop(0, slots // UNROLL, step, 0)
    for b in range(BR):
        v = acc[b]
        out_ref[b] = v
        v = v.astype(BF16)
        plow_ref[b] = v
        s1_ref[b] = v
        s2_ref[b] = v
        s3_ref[b] = v
    pa0_ref[...] = pa_ref[0:8]
    s1_ref[8:16] = pa_ref[8:16].astype(BF16)
    for k, out in ((0, s2_ref), (8, s3_ref)):
        v = pa_ref[16 + k : 24 + k] + cp_ref[32 + k : 40 + k].astype(F32) + zp_ref[32 + k : 40 + k].astype(F32)
        out[8:16] = v.astype(BF16)


def apply_mt_kernel(
    col_ref, row_ref, pa0_ref, r1_ref, r2_ref, r3_ref, tiles_ref, own_ref, cp_ref, zp_ref, low, acc
):
    for b in range(BR):
        v = pa0_ref[b] + r1_ref[8 + b].astype(F32) + r2_ref[8 + b].astype(F32) + r3_ref[8 + b].astype(F32)
        low[b] = v.astype(BF16)
    low[BR] = jnp.zeros((K, TILE), BF16)
    acc[...] = jnp.zeros_like(acc)
    slots = tiles_ref.shape[0]

    def step(s, carry):
        base = s * UNROLL
        parts = []
        for u in range(UNROLL):
            parts.append(bdot(low[row_ref[base + u]], tiles_ref[base + u], NN))
        for u in range(UNROLL):
            c = col_ref[base + u]
            acc[c] = acc[c] + parts[u]
        return carry

    lax.fori_loop(0, slots // UNROLL, step, 0)
    own_ref[...] = acc[0:32]
    for out, at in ((cp_ref, 32), (zp_ref, 64)):
        out[0:8] = r2_ref[0:8]
        out[8:16] = r3_ref[0:8]
        out[16:48] = acc[at : at + 32].astype(BF16)


def apply_at_kernel(col_ref, low_ref, tiles_ref, own_ref, cp_ref, zp_ref, acc):
    acc[...] = jnp.zeros_like(acc)
    slots = tiles_ref.shape[1]
    for b in range(BR):
        x = low_ref[b]
        parts = [bdot(x, tiles_ref[b, j], NN) for j in range(slots)]
        for j in range(slots):
            c = col_ref[b * slots + j]
            acc[c] = acc[c] + parts[j]
    own_ref[...] = acc[0:32]
    cp_ref[...] = acc[32:48].astype(BF16)
    zp_ref[...] = acc[48:64].astype(BF16)


def collect_m_kernel(own_ref, cp_ref, zp_ref, o0_ref, o1_ref, o2_ref, o3_ref):
    v = own_ref[...] + cp_ref[16:48].astype(F32) + zp_ref[16:48].astype(F32)
    o0_ref[...] = v[0:8]
    o1_ref[...] = v[8:16].astype(BF16)
    o2_ref[...] = v[16:24].astype(BF16)
    o3_ref[...] = v[24:32].astype(BF16)


def apply_a_kernel(
    col_ref, low_ref, r1_ref, r2_ref, r3_ref, cp_ref, zp_ref, tiles_ref, basis_ref, shadow_ref, res_ref, image_ref, g_ref, win
):
    for k, src in enumerate((low_ref, r1_ref, r2_ref, r3_ref)):
        win[8 * k : 8 * k + 8] = src[0:8]
    win[32:48] = cp_ref[0:16]
    win[48:64] = zp_ref[0:16]
    slots = tiles_ref.shape[1]
    gs = gi = gr = gb = None
    for b in range(BR):
        v = None
        for j in range(slots):
            p = bdot(win[col_ref[b * slots + j]], tiles_ref[b, j], NT)
            v = p if v is None else v + p
        image_ref[b] = v
        ps, pi, pr, pb = (hdot(v, o, NT) for o in (shadow_ref[b], v, res_ref[b], basis_ref[b]))
        if b == 0:
            gs, gi, gr, gb = ps, pi, pr, pb
        else:
            gs, gi, gr, gb = gs + ps, gi + pi, gr + pr, gb + pb
    g_ref[0:64, 0:64] = gs
    g_ref[0:64, 64:128] = gi
    g_ref[64:128, 0:64] = gr
    g_ref[64:128, 64:128] = gb


def back_gram_kernel(o0_ref, b1_ref, b2_ref, b3_ref, shadow_ref, bi_ref, g_ref):
    gb = gs = None
    for b in range(BR):
        v = o0_ref[b] + b1_ref[b].astype(F32) + b2_ref[b].astype(F32) + b3_ref[b].astype(F32)
        bi_ref[b] = v
        pb, ps = hdot(v, v, NT), hdot(v, shadow_ref[b], NT)
        gb, gs = (pb, ps) if b == 0 else (gb + pb, gs + ps)
    g_ref[:, 0:64] = gb
    g_ref[:, 64:128] = gs


def update_kernel(first, last, g_ref, n_ref, image_ref, bi_ref, basis_ref, shadow_ref, precond_ref, res_ref, *refs):
    if first:
        sol_ref, outs = None, refs
    else:
        sol_ref, outs = refs[0], refs[1:]
    if last:
        sol_out, res_out, basis_out, shadow_out = outs
    else:
        sol_out, res_out, basis_out, shadow_out, blow_out, slow_out = outs
    total = n_ref[0]
    coup_t = g_ref[0:64, 0:64] * (1.0 / total)
    coup = coup_t.T
    normal = g_ref[0:64, 64:128]
    target = g_ref[64:128, 0:64]
    ib = g_ref[64:128, 64:128]
    bb = g_ref[128:192, 0:64]
    bs = g_ref[128:192, 64:128]
    y = hdot(ib, coup)
    uu = normal - y - y.T + total * hdot(coup_t, coup)
    y = hdot(bs, coup_t)
    ss = bb - y - y.T + total * hdot(coup, coup_t)
    inv_n, inv_u, inv_s = inverse_factors([normal, uu * (1.0 / total), ss * (1.0 / total)])
    w_t = hdot(hdot(inv_n, target), inv_n, TN)
    for b in range(BR):
        image = image_ref[b]
        v = hdot(w_t, precond_ref[b])
        sol_out[b] = v if first else sol_ref[b] + v
        res_out[b] = res_ref[b] - hdot(w_t, image)
        v = hdot(inv_u, image - hdot(coup_t, basis_ref[b]))
        basis_out[b] = v
        if not last:
            blow_out[b] = v.astype(BF16)
        v = hdot(inv_s, bi_ref[b] - hdot(coup, shadow_ref[b]))
        shadow_out[b] = v
        if not last:
            slow_out[b] = v.astype(BF16)


def shards(right_side, a_tiles, a_cols, m_tiles, m_rows, m_cols, m_count):
    blk = (BR, K, TILE)
    total = BR * TILE * lax.axis_size((DOM, BAL))
    group = lax.axis_index(DOM)
    y = lax.axis_index(BAL)
    first_row = (group * lax.axis_size(BAL) + y) * BR
    n_arr = jnp.full((1,), float(total), F32)

    def place(cols, skip):
        dev = cols // BR
        g, rel = dev // 4, (dev % 4) ^ y
        width = 4 - skip
        local = jnp.where(
            g == group, rel, jnp.where(g == (group ^ 1), 4 + rel - skip, 4 + width + rel - skip)
        )
        return local * BR + cols % BR

    a_place = place(a_cols, 2).reshape(-1)
    m_place = place(m_cols, 0)
    live = jnp.arange(m_tiles.shape[0], dtype=jnp.int32) < m_count[0]
    m_local = jnp.where(live, m_rows - first_row, BR)

    (g0,) = call(start_gram_kernel, "start_gram", [VM], [((K, K), F32)], [], (right_side,))
    g0 = reduce_all(g0)
    basis, blow = call(
        start_norm_kernel, "start_norm", [VM, VM, SM], [(blk, F32), (blk, BF16)], [], (g0, right_side, n_arr)
    )
    shadow, slow = basis, blow
    solution, residual = None, right_side
    for iteration in range(ITERS):
        last = iteration == ITERS - 1
        q = [swap_y(blow, k) for k in (1, 2, 3)]
        pa_own, pa_cp, pa_zp = call(
            apply_at_kernel,
            "apply_at",
            [SM, VM, VM],
            [((32, K, TILE), F32), ((16, K, TILE), BF16), ((16, K, TILE), BF16)],
            [pltpu.VMEM((64, K, TILE), F32)],
            (a_place, slow, a_tiles),
            flops=84_000_000,
            nbytes=3_000_000,
        )
        send_cp, send_zp = call(
            pack_kernel, "pack", [VM] * 6, [((48, K, TILE), BF16)] * 2, [], (blow, *q, pa_cp, pa_zp)
        )
        got_zp = swap_next(send_zp)
        got_cp = swap_core(send_cp)
        precond, plow, s1, s2, s3, pa0 = call(
            apply_m_kernel,
            "apply_m",
            [SM, SM] + [VM] * 8,
            [(blk, F32), (blk, BF16)] + [((16, K, TILE), BF16)] * 3 + [(blk, F32)],
            [pltpu.VMEM((96, K, TILE), BF16), pltpu.VMEM((BR + 1, K, TILE), F32)],
            (m_place, m_local, blow, *q, got_cp, got_zp, m_tiles, pa_own),
            flops=218_000_000,
            nbytes=5_000_000,
        )
        r = [swap_y(s1, 1), swap_y(s2, 2), swap_y(s3, 3)]
        pm_own, send_cp, send_zp = call(
            apply_mt_kernel,
            "apply_mt",
            [SM, SM] + [VM] * 5,
            [((32, K, TILE), F32), ((48, K, TILE), BF16), ((48, K, TILE), BF16)],
            [pltpu.VMEM((BR + 1, K, TILE), BF16), pltpu.VMEM((96, K, TILE), F32)],
            (m_place, m_local, pa0, *r, m_tiles),
            flops=218_000_000,
            nbytes=5_000_000,
        )
        got_zp = swap_next(send_zp)
        got_cp = swap_core(send_cp)
        o0, o1, o2, o3 = call(
            collect_m_kernel,
            "collect_m",
            [VM] * 3,
            [(blk, F32)] + [(blk, BF16)] * 3,
            [],
            (pm_own, got_cp, got_zp),
        )
        image, g_fwd = call(
            apply_a_kernel,
            "apply_a",
            [SM] + [VM] * 10,
            [(blk, F32), ((128, 128), F32)],
            [pltpu.VMEM((64, K, TILE), BF16)],
            (a_place, plow, *r, got_cp, got_zp, a_tiles, basis, shadow, residual),
            flops=84_000_000,
            nbytes=3_000_000,
        )
        b1, b2, b3 = swap_y(o1, 1), swap_y(o2, 2), swap_y(o3, 3)
        back_image, g_bwd = call(
            back_gram_kernel,
            "back_gram",
            [VM] * 5,
            [(blk, F32), ((64, 128), F32)],
            [],
            (o0, b1, b2, b3, shadow),
        )
        grams = reduce_all(jnp.concatenate([g_fwd, g_bwd], 0))
        args = [grams, n_arr, image, back_image, basis, shadow, precond, residual]
        if iteration:
            args.append(solution)
        outs = [(blk, F32)] * 4 + ([] if last else [(blk, BF16)] * 2)
        result = call(
            lambda *refs, f=iteration == 0, l=last: update_kernel(f, l, *refs),
            "update",
            [VM, SM] + [VM] * (len(args) - 2),
            outs,
            [],
            args,
            final=last,
        )
        solution, residual, basis, shadow = result[:4]
        if not last:
            blow, slow = result[4:]
    return (solution, residual, basis, shadow)


def solution(mesh):
    rows = P((DOM, BAL))
    return jax.shard_map(
        shards,
        mesh=mesh,
        in_specs=(rows,) * 7,
        out_specs=(rows,) * 4,
        check_vma=False,
    )
```

```python
import jax
import jax.numpy as jnp
from jax import lax
from jax.experimental import pallas as pl
from jax.experimental.pallas import tpu as pltpu
from jax.sharding import PartitionSpec as P

ITERS = 2
BR = 8
TILE = 128
K = 64
NT = (((1,), (1,)), ((), ()))
NN = (((1,), (0,)), ((), ()))
TN = (((0,), (0,)), ((), ()))
F32 = jnp.float32
BF16 = jnp.bfloat16
DOM, BAL = "dom", "bal"
UNROLL = 8


def hdot(a, b, dims=NN):
    return lax.dot_general(a, b, dims, precision=lax.Precision.HIGHEST, preferred_element_type=F32)


def bdot(a, b, dims):
    return lax.dot_general(a, b, dims, preferred_element_type=F32)


def swap(value, axis, size, distance):
    return lax.ppermute(value, axis, [(i, i ^ distance) for i in range(size)])


def swap_y(value, distance):
    return swap(value, BAL, lax.axis_size(BAL), distance)


def swap_core(value):
    return swap(value, DOM, lax.axis_size(DOM), 1)


def swap_next(value):
    size = lax.axis_size(DOM)
    route = []
    for i in range(1, size - 1, 2):
        route += [(i, i + 1), (i + 1, i)]
    return lax.ppermute(value, DOM, route)


def reduce_all(value):
    size = lax.axis_size(DOM)
    value = value + swap(value, DOM, size, 1)
    parts = [swap_y(value, k) for k in (1, 2, 3)]
    value = (value + parts[0]) + (parts[1] + parts[2])
    for unit in (2, 8):
        parts = [swap(value, DOM, size, k * unit) for k in (1, 2, 3)]
        value = (value + parts[0]) + (parts[1] + parts[2])
    return value


VM = pl.BlockSpec(memory_space=pltpu.VMEM)
SM = pl.BlockSpec(memory_space=pltpu.SMEM)


def call(body, name, specs, outs, scratch, args, flops=0, nbytes=0, final=False):
    args = [pltpu.with_memory_space_constraint(a, pltpu.VMEM) if s is VM else a for s, a in zip(specs, args)]
    return pl.pallas_call(
        body,
        name=name,
        in_specs=specs,
        out_specs=tuple(VM for _ in outs),
        out_shape=tuple(jax.ShapeDtypeStruct(s, d) if final else pltpu.VMEM(s, d) for s, d in outs),
        scratch_shapes=scratch,
        compiler_params=pltpu.CompilerParams(vmem_limit_bytes=14 * 2**20),
        cost_estimate=pl.CostEstimate(flops=flops, bytes_accessed=nbytes, transcendentals=0),
    )(*args)


def inverse_factors(mats):
    nb = K // 8
    row = lax.broadcasted_iota(jnp.int32, (8, K), 0)
    col = lax.broadcasted_iota(jnp.int32, (8, K), 1)
    work = []
    for g in mats:
        left = [g[8 * i : 8 * i + 8, :] for i in range(nb)]
        right = [jnp.where(row + 8 * i == col, 1.0, 0.0).astype(F32) for i in range(nb)]
        work.append((left, right))
    for k in range(K):
        kb, kr = divmod(k, 8)
        for left, right in work:
            prow = left[kb][kr : kr + 1, :]
            rrow = right[kb][kr : kr + 1, :]
            inv = 1.0 / prow[:, k : k + 1]
            prow = prow * inv
            rrow = rrow * inv
            for i in range(kb, nb):
                f = left[i][:, k : k + 1]
                if i == kb:
                    if kr == 7:
                        continue
                    f = jnp.where(row[:, :1] > kr, f, 0.0)
                left[i] = left[i] - f * prow
                right[i] = right[i] - f * rrow
    out = []
    for left, right in work:
        rows = []
        for i in range(nb):
            d = jnp.sum(jnp.where(row + 8 * i == col, left[i], 0.0), axis=1, keepdims=True)
            rows.append(right[i] * lax.rsqrt(d))
        out.append(jnp.concatenate(rows, axis=0))
    return out


def start_gram_kernel(x_ref, g_ref):
    g = jnp.zeros((K, K), F32)
    for b in range(BR):
        g = g + hdot(x_ref[b], x_ref[b], NT)
    g_ref[...] = g


def start_norm_kernel(g_ref, x_ref, n_ref, basis_ref, low_ref):
    (inv,) = inverse_factors([g_ref[...] * (1.0 / n_ref[0])])
    for b in range(BR):
        v = hdot(inv, x_ref[b])
        basis_ref[b] = v
        low_ref[b] = v.astype(BF16)


def mid_kernel(low_ref, q1_ref, q2_ref, q3_ref, pa_ref, cp_ref, zp_ref, own4_ref, o0_ref, o1_ref, o2_ref, o3_ref):
    for k, src in enumerate((low_ref, q1_ref, q2_ref, q3_ref)):
        own4_ref[8 * k : 8 * k + 8] = src[...]
    o0_ref[...] = pa_ref[0:8]
    o1_ref[...] = pa_ref[8:16].astype(BF16)
    for k, out in ((0, o2_ref), (8, o3_ref)):
        v = pa_ref[16 + k : 24 + k] + cp_ref[k : 8 + k].astype(F32) + zp_ref[k : 8 + k].astype(F32)
        out[...] = v.astype(BF16)


def join_kernel(a_ref, b_ref, out_ref):
    out_ref[0:8] = a_ref[...]
    out_ref[8:16] = b_ref[...]


def apply_m_kernel(col_ref, row_ref, own_ref, cp_ref, zp_ref, tiles_ref, out_ref, low_ref, win, acc):
    win[0:32] = own_ref[...]
    win[32:64] = cp_ref[...]
    win[64:96] = zp_ref[...]
    acc[...] = jnp.zeros_like(acc)
    slots = tiles_ref.shape[0]

    def step(s, carry):
        base = s * UNROLL
        parts = []
        for u in range(UNROLL):
            parts.append(bdot(win[col_ref[base + u]], tiles_ref[base + u], NT))
        for u in range(UNROLL):
            r = row_ref[base + u]
            acc[r] = acc[r] + parts[u]
        return carry

    lax.fori_loop(0, slots // UNROLL, step, 0)
    for b in range(BR):
        v = acc[b]
        out_ref[b] = v
        low_ref[b] = v.astype(BF16)


def apply_mt_kernel(
    col_ref, row_ref, back0_ref, b1_ref, b2_ref, b3_ref, tiles_ref, own_ref, cp_ref, zp_ref, low, acc
):
    for b in range(BR):
        v = back0_ref[b] + b1_ref[b].astype(F32) + b2_ref[b].astype(F32) + b3_ref[b].astype(F32)
        low[b] = v.astype(BF16)
    low[BR] = jnp.zeros((K, TILE), BF16)
    acc[...] = jnp.zeros_like(acc)
    slots = tiles_ref.shape[0]

    def step(s, carry):
        base = s * UNROLL
        parts = []
        for u in range(UNROLL):
            parts.append(bdot(low[row_ref[base + u]], tiles_ref[base + u], NN))
        for u in range(UNROLL):
            c = col_ref[base + u]
            acc[c] = acc[c] + parts[u]
        return carry

    lax.fori_loop(0, slots // UNROLL, step, 0)
    own_ref[...] = acc[0:32]
    cp_ref[...] = acc[32:64].astype(BF16)
    zp_ref[...] = acc[64:96].astype(BF16)


def apply_at_kernel(col_ref, low_ref, tiles_ref, own_ref, cp_ref, zp_ref, acc):
    acc[...] = jnp.zeros_like(acc)
    slots = tiles_ref.shape[1]
    for b in range(BR):
        x = low_ref[b]
        parts = [bdot(x, tiles_ref[b, j], NN) for j in range(slots)]
        for j in range(slots):
            c = col_ref[b * slots + j]
            acc[c] = acc[c] + parts[j]
    own_ref[...] = acc[0:32]
    cp_ref[...] = acc[32:48].astype(BF16)
    zp_ref[...] = acc[48:64].astype(BF16)


def collect_m_kernel(own_ref, cp_ref, zp_ref, o0_ref, o1_ref, o2_ref, o3_ref):
    v = own_ref[...] + cp_ref[...].astype(F32) + zp_ref[...].astype(F32)
    o0_ref[...] = v[0:8]
    o1_ref[...] = v[8:16].astype(BF16)
    o2_ref[...] = v[16:24].astype(BF16)
    o3_ref[...] = v[24:32].astype(BF16)


def apply_a_kernel(
    col_ref, low_ref, r1_ref, r2_ref, r3_ref, cp_ref, zp_ref, tiles_ref, basis_ref, shadow_ref, res_ref, image_ref, g_ref, win
):
    for k, src in enumerate((low_ref, r1_ref, r2_ref, r3_ref)):
        win[8 * k : 8 * k + 8] = src[...]
    win[32:48] = cp_ref[...]
    win[48:64] = zp_ref[...]
    slots = tiles_ref.shape[1]
    gs = gi = gr = gb = None
    for b in range(BR):
        v = None
        for j in range(slots):
            p = bdot(win[col_ref[b * slots + j]], tiles_ref[b, j], NT)
            v = p if v is None else v + p
        image_ref[b] = v
        ps, pi, pr, pb = (hdot(v, o, NT) for o in (shadow_ref[b], v, res_ref[b], basis_ref[b]))
        if b == 0:
            gs, gi, gr, gb = ps, pi, pr, pb
        else:
            gs, gi, gr, gb = gs + ps, gi + pi, gr + pr, gb + pb
    g_ref[0:64, 0:64] = gs
    g_ref[0:64, 64:128] = gi
    g_ref[64:128, 0:64] = gr
    g_ref[64:128, 64:128] = gb


def back_gram_kernel(o0_ref, b1_ref, b2_ref, b3_ref, shadow_ref, bi_ref, g_ref):
    gb = gs = None
    for b in range(BR):
        v = o0_ref[b] + b1_ref[b].astype(F32) + b2_ref[b].astype(F32) + b3_ref[b].astype(F32)
        bi_ref[b] = v
        pb, ps = hdot(v, v, NT), hdot(v, shadow_ref[b], NT)
        gb, gs = (pb, ps) if b == 0 else (gb + pb, gs + ps)
    g_ref[:, 0:64] = gb
    g_ref[:, 64:128] = gs


def update_kernel(first, last, g_ref, n_ref, image_ref, bi_ref, basis_ref, shadow_ref, precond_ref, res_ref, *refs):
    if first:
        sol_ref, outs = None, refs
    else:
        sol_ref, outs = refs[0], refs[1:]
    if last:
        sol_out, res_out, basis_out, shadow_out = outs
    else:
        sol_out, res_out, basis_out, shadow_out, blow_out, slow_out = outs
    total = n_ref[0]
    coup_t = g_ref[0:64, 0:64] * (1.0 / total)
    coup = coup_t.T
    normal = g_ref[0:64, 64:128]
    target = g_ref[64:128, 0:64]
    ib = g_ref[64:128, 64:128]
    bb = g_ref[128:192, 0:64]
    bs = g_ref[128:192, 64:128]
    y = hdot(ib, coup)
    uu = normal - y - y.T + total * hdot(coup_t, coup)
    y = hdot(bs, coup_t)
    ss = bb - y - y.T + total * hdot(coup, coup_t)
    inv_n, inv_u, inv_s = inverse_factors([normal, uu * (1.0 / total), ss * (1.0 / total)])
    w_t = hdot(hdot(inv_n, target), inv_n, TN)
    for b in range(BR):
        image = image_ref[b]
        v = hdot(w_t, precond_ref[b])
        sol_out[b] = v if first else sol_ref[b] + v
        res_out[b] = res_ref[b] - hdot(w_t, image)
        v = hdot(inv_u, image - hdot(coup_t, basis_ref[b]))
        basis_out[b] = v
        if not last:
            blow_out[b] = v.astype(BF16)
        v = hdot(inv_s, bi_ref[b] - hdot(coup, shadow_ref[b]))
        shadow_out[b] = v
        if not last:
            slow_out[b] = v.astype(BF16)


def shards(right_side, a_tiles, a_cols, m_tiles, m_rows, m_cols, m_count):
    blk = (BR, K, TILE)
    total = BR * TILE * lax.axis_size((DOM, BAL))
    group = lax.axis_index(DOM)
    y = lax.axis_index(BAL)
    first_row = (group * lax.axis_size(BAL) + y) * BR
    n_arr = jnp.full((1,), float(total), F32)

    def place(cols, skip):
        dev = cols // BR
        g, rel = dev // 4, (dev % 4) ^ y
        width = 4 - skip
        local = jnp.where(
            g == group, rel, jnp.where(g == (group ^ 1), 4 + rel - skip, 4 + width + rel - skip)
        )
        return local * BR + cols % BR

    a_place = place(a_cols, 2).reshape(-1)
    m_place = place(m_cols, 0)
    live = jnp.arange(m_tiles.shape[0], dtype=jnp.int32) < m_count[0]
    m_local = jnp.where(live, m_rows - first_row, BR)

    (g0,) = call(start_gram_kernel, "start_gram", [VM], [((K, K), F32)], [], (right_side,))
    g0 = reduce_all(g0)
    basis, blow = call(
        start_norm_kernel, "start_norm", [VM, VM, SM], [(blk, F32), (blk, BF16)], [], (g0, right_side, n_arr)
    )
    shadow, slow = basis, blow
    solution, residual = None, right_side
    for iteration in range(ITERS):
        last = iteration == ITERS - 1
        q = [swap_y(blow, k) for k in (1, 2, 3)]
        pa_own, pa_cp, pa_zp = call(
            apply_at_kernel,
            "apply_at",
            [SM, VM, VM],
            [((32, K, TILE), F32), ((16, K, TILE), BF16), ((16, K, TILE), BF16)],
            [pltpu.VMEM((64, K, TILE), F32)],
            (a_place, slow, a_tiles),
            flops=84_000_000,
            nbytes=3_000_000,
        )
        ra_zp, ra_cp = swap_next(pa_zp), swap_core(pa_cp)
        own4, o0, o1, o2, o3 = call(
            mid_kernel,
            "mid",
            [VM] * 7,
            [((32, K, TILE), BF16), (blk, F32)] + [(blk, BF16)] * 3,
            [],
            (blow, *q, pa_own, ra_cp, ra_zp),
        )
        m_zp = swap_next(own4)
        b1, b2, b3 = swap_y(o1, 1), swap_y(o2, 2), swap_y(o3, 3)
        m_cp = swap_core(own4)
        pm_own, pm_cp, pm_zp = call(
            apply_mt_kernel,
            "apply_mt",
            [SM, SM] + [VM] * 5,
            [((32, K, TILE), F32), ((32, K, TILE), BF16), ((32, K, TILE), BF16)],
            [pltpu.VMEM((BR + 1, K, TILE), BF16), pltpu.VMEM((96, K, TILE), F32)],
            (m_place, m_local, o0, b1, b2, b3, m_tiles),
            flops=218_000_000,
            nbytes=5_000_000,
        )
        rm_zp, rm_cp = swap_next(pm_zp), swap_core(pm_cp)
        precond, plow = call(
            apply_m_kernel,
            "apply_m",
            [SM, SM] + [VM] * 4,
            [(blk, F32), (blk, BF16)],
            [pltpu.VMEM((96, K, TILE), BF16), pltpu.VMEM((BR + 1, K, TILE), F32)],
            (m_place, m_local, own4, m_cp, m_zp, m_tiles),
            flops=218_000_000,
            nbytes=5_000_000,
        )
        r = [swap_y(plow, k) for k in (1, 2, 3)]
        o0, o1, o2, o3 = call(
            collect_m_kernel,
            "collect_m",
            [VM] * 3,
            [(blk, F32)] + [(blk, BF16)] * 3,
            [],
            (pm_own, rm_cp, rm_zp),
        )
        (far,) = call(join_kernel, "join", [VM] * 2, [((16, K, TILE), BF16)], [], (r[1], r[2]))
        a_zp, a_cp = swap_next(far), swap_core(far)
        image, g_fwd = call(
            apply_a_kernel,
            "apply_a",
            [SM] + [VM] * 10,
            [(blk, F32), ((128, 128), F32)],
            [pltpu.VMEM((64, K, TILE), BF16)],
            (a_place, plow, *r, a_cp, a_zp, a_tiles, basis, shadow, residual),
            flops=84_000_000,
            nbytes=3_000_000,
        )
        b1, b2, b3 = swap_y(o1, 1), swap_y(o2, 2), swap_y(o3, 3)
        back_image, g_bwd = call(
            back_gram_kernel,
            "back_gram",
            [VM] * 5,
            [(blk, F32), ((64, 128), F32)],
            [],
            (o0, b1, b2, b3, shadow),
        )
        grams = reduce_all(jnp.concatenate([g_fwd, g_bwd], 0))
        args = [grams, n_arr, image, back_image, basis, shadow, precond, residual]
        if iteration:
            args.append(solution)
        outs = [(blk, F32)] * 4 + ([] if last else [(blk, BF16)] * 2)
        result = call(
            lambda *refs, f=iteration == 0, l=last: update_kernel(f, l, *refs),
            "update",
            [VM, SM] + [VM] * (len(args) - 2),
            outs,
            [],
            args,
            final=last,
        )
        solution, residual, basis, shadow = result[:4]
        if not last:
            blow, slow = result[4:]
    return (solution, residual, basis, shadow)


def solution(mesh):
    rows = P((DOM, BAL))
    return jax.shard_map(
        shards,
        mesh=mesh,
        in_specs=(rows,) * 7,
        out_specs=(rows,) * 4,
        check_vma=False,
    )
```

```python
import jax
import jax.numpy as jnp
from jax import lax
from jax.experimental import pallas as pl
from jax.experimental.pallas import tpu as pltpu
from jax.sharding import PartitionSpec as P

ITERS = 2
BR = 8
TILE = 128
K = 64
NT = (((1,), (1,)), ((), ()))
NN = (((1,), (0,)), ((), ()))
TN = (((0,), (0,)), ((), ()))
F32 = jnp.float32
BF16 = jnp.bfloat16
DOM, BAL = "dom", "bal"
UNROLL = 8


def hdot(a, b, dims=NN):
    return lax.dot_general(a, b, dims, precision=lax.Precision.HIGHEST, preferred_element_type=F32)


def bdot(a, b, dims):
    return lax.dot_general(a, b, dims, preferred_element_type=F32)


def swap(value, axis, size, distance):
    return lax.ppermute(value, axis, [(i, i ^ distance) for i in range(size)])


def swap_y(value, distance):
    return swap(value, BAL, lax.axis_size(BAL), distance)


def swap_core(value):
    return swap(value, DOM, lax.axis_size(DOM), 1)


def swap_next(value):
    size = lax.axis_size(DOM)
    route = []
    for i in range(1, size - 1, 2):
        route += [(i, i + 1), (i + 1, i)]
    return lax.ppermute(value, DOM, route)


def reduce_all(value):
    size = lax.axis_size(DOM)
    value = value + swap(value, DOM, size, 1)
    parts = [swap_y(value, k) for k in (1, 2, 3)]
    value = (value + parts[0]) + (parts[1] + parts[2])
    for unit in (2, 8):
        parts = [swap(value, DOM, size, k * unit) for k in (1, 2, 3)]
        value = (value + parts[0]) + (parts[1] + parts[2])
    return value


VM = pl.BlockSpec(memory_space=pltpu.VMEM)
SM = pl.BlockSpec(memory_space=pltpu.SMEM)


def call(body, name, specs, outs, scratch, args, flops=0, nbytes=0, final=False):
    args = [pltpu.with_memory_space_constraint(a, pltpu.VMEM) if s is VM else a for s, a in zip(specs, args)]
    return pl.pallas_call(
        body,
        name=name,
        in_specs=specs,
        out_specs=tuple(VM for _ in outs),
        out_shape=tuple(jax.ShapeDtypeStruct(s, d) if final else pltpu.VMEM(s, d) for s, d in outs),
        scratch_shapes=scratch,
        compiler_params=pltpu.CompilerParams(vmem_limit_bytes=14 * 2**20),
        cost_estimate=pl.CostEstimate(flops=flops, bytes_accessed=nbytes, transcendentals=0),
    )(*args)


def inverse_factors(mats, out_ref):
    nb = K // 8
    row = lax.broadcasted_iota(jnp.int32, (8, K), 0)
    col = lax.broadcasted_iota(jnp.int32, (8, K), 1)
    work = []
    for g in mats:
        left = [g[8 * i : 8 * i + 8, :] for i in range(nb)]
        right = [jnp.where(row + 8 * i == col, 1.0, 0.0).astype(F32) for i in range(nb)]
        work.append((left, right))
    for k in range(0, K, 2):
        kb, kr = divmod(k, 8)
        for m, (left, right) in enumerate(work):
            r0, r1 = left[kb][kr : kr + 1, :], left[kb][kr + 1 : kr + 2, :]
            q0, q1 = right[kb][kr : kr + 1, :], right[kb][kr + 1 : kr + 2, :]
            a = jnp.broadcast_to(r0[:, k : k + 1], (1, K))
            b = jnp.broadcast_to(r0[:, k + 1 : k + 2], (1, K))
            c = jnp.broadcast_to(r1[:, k + 1 : k + 2], (1, K))
            inv = 1.0 / (a * c - b * b)
            if k < K - 2:
                p0, p1 = (c * r0 - b * r1) * inv, (a * r1 - b * r0) * inv
                s0, s1 = (c * q0 - b * q1) * inv, (a * q1 - b * q0) * inv
                for i in range(kb, nb):
                    if i == kb and kr == 6:
                        continue
                    f0, f1 = left[i][:, k : k + 1], left[i][:, k + 1 : k + 2]
                    if i == kb:
                        below = row[:, :1] > kr + 1
                        f0, f1 = jnp.where(below, f0, 0.0), jnp.where(below, f1, 0.0)
                    left[i] = left[i] - (f0 * p0 + f1 * p1)
                    right[i] = right[i] - (f0 * s0 + f1 * s1)
            t = b / a
            out_ref[m, k : k + 1, :] = q0 * lax.rsqrt(a)
            out_ref[m, k + 1 : k + 2, :] = (q1 - t * q0) * lax.rsqrt(c - b * t)


def split(x):
    hi = x.astype(BF16)
    return hi, (x - hi.astype(F32)).astype(BF16)


def lanes(ref):
    return jnp.concatenate([ref[b] for b in range(BR)], axis=1)


def gram_of(a, others):
    a_hi, a_lo = a
    o_hi = jnp.concatenate([o[0] for o in others], axis=0)
    o_lo = jnp.concatenate([o[1] for o in others], axis=0)
    main = bdot(jnp.concatenate([a_hi, a_lo], axis=0), o_hi, NT)
    return main[0:K] + (main[K : 2 * K] + bdot(a_hi, o_lo, NT))


def combine(weights, parts):
    w_hi, w_lo = split(weights)
    rhs = jnp.concatenate([p[0] for p in parts] + [p[1] for p in parts], axis=0)
    m = weights.shape[0]
    lhs = jnp.concatenate([w_hi, w_lo], axis=0)
    lhs = jnp.concatenate([lhs, lhs], axis=1)
    out = bdot(lhs, rhs, NN)
    return out[0:m] + out[m : 2 * m]


def start_gram_kernel(x_ref, g_ref):
    g = jnp.zeros((K, K), F32)
    for b in range(BR):
        g = g + hdot(x_ref[b], x_ref[b], NT)
    g_ref[...] = g


def start_norm_kernel(g_ref, x_ref, n_ref, basis_ref, low_ref, inv_ref):
    inverse_factors([g_ref[...] * (1.0 / n_ref[0])], inv_ref)
    inv = inv_ref[0]
    for b in range(BR):
        v = hdot(inv, x_ref[b])
        basis_ref[b] = v
        low_ref[b] = v.astype(BF16)


def mid_kernel(low_ref, q1_ref, q2_ref, q3_ref, pa_ref, cp_ref, zp_ref, own4_ref, o0_ref, o1_ref, o2_ref, o3_ref):
    for k, src in enumerate((low_ref, q1_ref, q2_ref, q3_ref)):
        own4_ref[8 * k : 8 * k + 8] = src[...]
    o0_ref[...] = pa_ref[0:8]
    o1_ref[...] = pa_ref[8:16].astype(BF16)
    for k, out in ((0, o2_ref), (8, o3_ref)):
        v = pa_ref[16 + k : 24 + k] + cp_ref[k : 8 + k].astype(F32) + zp_ref[k : 8 + k].astype(F32)
        out[...] = v.astype(BF16)


def join_kernel(a_ref, b_ref, out_ref):
    out_ref[0:8] = a_ref[0:8]
    out_ref[8:16] = b_ref[0:8]


def apply_m_kernel(col_ref, row_ref, own_ref, cp_ref, zp_ref, tiles_ref, out_ref, low_ref, win, acc):
    win[0:32] = own_ref[...]
    win[32:64] = cp_ref[...]
    win[64:96] = zp_ref[...]
    acc[...] = jnp.zeros_like(acc)
    slots = tiles_ref.shape[0]

    def step(s, carry):
        base = s * UNROLL
        parts = []
        for u in range(UNROLL):
            parts.append(bdot(win[col_ref[base + u]], tiles_ref[base + u], NT))
        for u in range(UNROLL):
            r = row_ref[base + u]
            acc[r] = acc[r] + parts[u]
        return carry

    lax.fori_loop(0, slots // UNROLL, step, 0)
    for b in range(BR):
        v = acc[b]
        out_ref[b] = v
        low_ref[b] = v.astype(BF16)


def apply_mt_kernel(
    col_ref, row_ref, back0_ref, b1_ref, b2_ref, b3_ref, tiles_ref, own_ref, cp_ref, zp_ref, low, acc
):
    for b in range(BR):
        v = back0_ref[b] + b1_ref[b].astype(F32) + b2_ref[b].astype(F32) + b3_ref[b].astype(F32)
        low[b] = v.astype(BF16)
    low[BR] = jnp.zeros((K, TILE), BF16)
    acc[...] = jnp.zeros_like(acc)
    slots = tiles_ref.shape[0]

    def step(s, carry):
        base = s * UNROLL
        parts = []
        for u in range(UNROLL):
            parts.append(bdot(low[row_ref[base + u]], tiles_ref[base + u], NN))
        for u in range(UNROLL):
            c = col_ref[base + u]
            acc[c] = acc[c] + parts[u]
        return carry

    lax.fori_loop(0, slots // UNROLL, step, 0)
    own_ref[...] = acc[0:32]
    cp_ref[...] = acc[32:64].astype(BF16)
    zp_ref[...] = acc[64:96].astype(BF16)


def apply_at_kernel(col_ref, low_ref, tiles_ref, own_ref, cp_ref, zp_ref, acc):
    acc[...] = jnp.zeros_like(acc)
    slots = tiles_ref.shape[1]
    for b in range(BR):
        x = low_ref[b]
        parts = [bdot(x, tiles_ref[b, j], NN) for j in range(slots)]
        for j in range(slots):
            c = col_ref[b * slots + j]
            acc[c] = acc[c] + parts[j]
    own_ref[...] = acc[0:32]
    cp_ref[...] = acc[32:48].astype(BF16)
    zp_ref[...] = acc[48:64].astype(BF16)


def collect_m_kernel(low_ref, own_ref, cp_ref, zp_ref, o0_ref, s1_ref, s2_ref, s3_ref):
    v = own_ref[...] + cp_ref[...].astype(F32) + zp_ref[...].astype(F32)
    o0_ref[...] = v[0:8]
    for k, out in ((1, s1_ref), (2, s2_ref), (3, s3_ref)):
        out[0:8] = low_ref[...]
        out[8:16] = v[8 * k : 8 * k + 8].astype(BF16)


def apply_a_kernel(
    col_ref, low_ref, r1_ref, r2_ref, r3_ref, cp_ref, zp_ref, tiles_ref, basis_ref, shadow_ref, res_ref, image_ref, g_ref, win
):
    for k, src in enumerate((low_ref, r1_ref, r2_ref, r3_ref)):
        win[8 * k : 8 * k + 8] = src[0:8]
    win[32:48] = cp_ref[...]
    win[48:64] = zp_ref[...]
    slots = tiles_ref.shape[1]
    rows = []
    for b in range(BR):
        x = jnp.concatenate([win[col_ref[b * slots + j]] for j in range(slots)], axis=1)
        t = jnp.concatenate([tiles_ref[b, j] for j in range(slots)], axis=1)
        v = bdot(x, t, NT)
        image_ref[b] = v
        rows.append(v)
    image = split(jnp.concatenate(rows, axis=1))
    g = gram_of(image, [split(lanes(shadow_ref)), image, split(lanes(res_ref)), split(lanes(basis_ref))])
    g_ref[0:64] = g[:, 0:128]
    g_ref[64:128] = g[:, 128:256]


def back_gram_kernel(o0_ref, r1_ref, r2_ref, r3_ref, shadow_ref, bi_ref, g_ref):
    rows = []
    for b in range(BR):
        v = o0_ref[b] + r1_ref[8 + b].astype(F32) + r2_ref[8 + b].astype(F32) + r3_ref[8 + b].astype(F32)
        bi_ref[b] = v
        rows.append(v)
    back = split(jnp.concatenate(rows, axis=1))
    g_ref[...] = gram_of(back, [back, split(lanes(shadow_ref))])


def update_kernel(first, last, g_ref, n_ref, image_ref, bi_ref, basis_ref, shadow_ref, precond_ref, res_ref, *refs):
    refs, inv_ref, w_ref = refs[:-2], refs[-2], refs[-1]
    if first:
        sol_ref, outs = None, refs
    else:
        sol_ref, outs = refs[0], refs[1:]
    if last:
        sol_out, res_out, basis_out, shadow_out = outs
    else:
        sol_out, res_out, basis_out, shadow_out, blow_out, slow_out = outs
    total = n_ref[0]
    coup_t = g_ref[0:64, 0:64] * (1.0 / total)
    coup = coup_t.T
    normal = g_ref[0:64, 64:128]
    target = g_ref[64:128, 0:64]
    ib = g_ref[64:128, 64:128]
    bb = g_ref[128:192, 0:64]
    bs = g_ref[128:192, 64:128]
    y = hdot(ib, coup)
    uu = normal - y - y.T + total * hdot(coup_t, coup)
    y = hdot(bs, coup_t)
    ss = bb - y - y.T + total * hdot(coup, coup_t)
    inverse_factors([normal, uu * (1.0 / total), ss * (1.0 / total)], inv_ref)
    inv_n, inv_u, inv_s = inv_ref[0], inv_ref[1], inv_ref[2]
    w_t = hdot(hdot(inv_n, target), inv_n, TN)
    w_ref[0:64, 0:64] = inv_u
    w_ref[0:64, 64:128] = -hdot(inv_u, coup_t)
    w_ref[64:128, 0:64] = -w_t
    w_ref[64:128, 64:128] = jnp.zeros((K, K), F32)
    w_ref[128:192, 0:64] = inv_s
    w_ref[128:192, 64:128] = -hdot(inv_s, coup)
    w_ref[192:256, 0:64] = w_t
    w_ref[192:256, 64:128] = jnp.zeros((K, K), F32)
    zero = jnp.zeros((K, BR * TILE), BF16)
    first_two = combine(w_ref[0:128], [split(lanes(image_ref)), split(lanes(basis_ref))])
    third = combine(w_ref[128:192], [split(lanes(bi_ref)), split(lanes(shadow_ref))])
    fourth = combine(w_ref[192:256], [split(lanes(precond_ref)), (zero, zero)])
    for b in range(BR):
        at = slice(b * TILE, (b + 1) * TILE)
        v = fourth[:, at]
        sol_out[b] = v if first else sol_ref[b] + v
        res_out[b] = res_ref[b] + first_two[K : 2 * K, at]
        v = first_two[0:K, at]
        basis_out[b] = v
        if not last:
            blow_out[b] = v.astype(BF16)
        v = third[:, at]
        shadow_out[b] = v
        if not last:
            slow_out[b] = v.astype(BF16)


def shards(right_side, a_tiles, a_cols, m_tiles, m_rows, m_cols, m_count):
    blk = (BR, K, TILE)
    total = BR * TILE * lax.axis_size((DOM, BAL))
    group = lax.axis_index(DOM)
    y = lax.axis_index(BAL)
    first_row = (group * lax.axis_size(BAL) + y) * BR
    n_arr = jnp.full((1,), float(total), F32)

    def place(cols, skip):
        dev = cols // BR
        g, rel = dev // 4, (dev % 4) ^ y
        width = 4 - skip
        local = jnp.where(
            g == group, rel, jnp.where(g == (group ^ 1), 4 + rel - skip, 4 + width + rel - skip)
        )
        return local * BR + cols % BR

    a_place = place(a_cols, 2).reshape(-1)
    m_place = place(m_cols, 0)
    live = jnp.arange(m_tiles.shape[0], dtype=jnp.int32) < m_count[0]
    m_local = jnp.where(live, m_rows - first_row, BR)

    (g0,) = call(start_gram_kernel, "start_gram", [VM], [((K, K), F32)], [], (right_side,))
    g0 = reduce_all(g0)
    basis, blow = call(
        start_norm_kernel, "start_norm", [VM, VM, SM], [(blk, F32), (blk, BF16)],
        [pltpu.VMEM((1, K, K), F32)], (g0, right_side, n_arr)
    )
    shadow, slow = basis, blow
    solution, residual = None, right_side
    for iteration in range(ITERS):
        last = iteration == ITERS - 1
        q = [swap_y(blow, k) for k in (1, 2, 3)]
        pa_own, pa_cp, pa_zp = call(
            apply_at_kernel,
            "apply_at",
            [SM, VM, VM],
            [((32, K, TILE), F32), ((16, K, TILE), BF16), ((16, K, TILE), BF16)],
            [pltpu.VMEM((64, K, TILE), F32)],
            (a_place, slow, a_tiles),
            flops=84_000_000,
            nbytes=3_000_000,
        )
        ra_zp, ra_cp = swap_next(pa_zp), swap_core(pa_cp)
        own4, o0, o1, o2, o3 = call(
            mid_kernel,
            "mid",
            [VM] * 7,
            [((32, K, TILE), BF16), (blk, F32)] + [(blk, BF16)] * 3,
            [],
            (blow, *q, pa_own, ra_cp, ra_zp),
        )
        m_zp = swap_next(own4)
        b1, b2, b3 = swap_y(o1, 1), swap_y(o2, 2), swap_y(o3, 3)
        m_cp = swap_core(own4)
        pm_own, pm_cp, pm_zp = call(
            apply_mt_kernel,
            "apply_mt",
            [SM, SM] + [VM] * 5,
            [((32, K, TILE), F32), ((32, K, TILE), BF16), ((32, K, TILE), BF16)],
            [pltpu.VMEM((BR + 1, K, TILE), BF16), pltpu.VMEM((96, K, TILE), F32)],
            (m_place, m_local, o0, b1, b2, b3, m_tiles),
            flops=218_000_000,
            nbytes=5_000_000,
        )
        rm_zp, rm_cp = swap_next(pm_zp), swap_core(pm_cp)
        precond, plow = call(
            apply_m_kernel,
            "apply_m",
            [SM, SM] + [VM] * 4,
            [(blk, F32), (blk, BF16)],
            [pltpu.VMEM((96, K, TILE), BF16), pltpu.VMEM((BR + 1, K, TILE), F32)],
            (m_place, m_local, own4, m_cp, m_zp, m_tiles),
            flops=218_000_000,
            nbytes=5_000_000,
        )
        o0, s1, s2, s3 = call(
            collect_m_kernel,
            "collect_m",
            [VM] * 4,
            [(blk, F32)] + [((16, K, TILE), BF16)] * 3,
            [],
            (plow, pm_own, rm_cp, rm_zp),
        )
        r = [swap_y(s1, 1), swap_y(s2, 2), swap_y(s3, 3)]
        (far,) = call(join_kernel, "join", [VM] * 2, [((16, K, TILE), BF16)], [], (r[1], r[2]))
        a_zp, a_cp = swap_next(far), swap_core(far)
        image, g_fwd = call(
            apply_a_kernel,
            "apply_a",
            [SM] + [VM] * 10,
            [(blk, F32), ((128, 128), F32)],
            [pltpu.VMEM((64, K, TILE), BF16)],
            (a_place, plow, *r, a_cp, a_zp, a_tiles, basis, shadow, residual),
            flops=84_000_000,
            nbytes=3_000_000,
        )
        back_image, g_bwd = call(
            back_gram_kernel,
            "back_gram",
            [VM] * 5,
            [(blk, F32), ((64, 128), F32)],
            [],
            (o0, *r, shadow),
        )
        grams = reduce_all(jnp.concatenate([g_fwd, g_bwd], 0))
        args = [grams, n_arr, image, back_image, basis, shadow, precond, residual]
        if iteration:
            args.append(solution)
        outs = [(blk, F32)] * 4 + ([] if last else [(blk, BF16)] * 2)
        result = call(
            lambda *refs, f=iteration == 0, l=last: update_kernel(f, l, *refs),
            "update",
            [VM, SM] + [VM] * (len(args) - 2),
            outs,
            [pltpu.VMEM((3, K, K), F32), pltpu.VMEM((256, 128), F32)],
            args,
            final=last,
        )
        solution, residual, basis, shadow = result[:4]
        if not last:
            blow, slow = result[4:]
    return (solution, residual, basis, shadow)


def solution(mesh):
    rows = P((DOM, BAL))
    return jax.shard_map(
        shards,
        mesh=mesh,
        in_specs=(rows,) * 7,
        out_specs=(rows,) * 4,
        check_vma=False,
    )
```

```python
import jax
import jax.numpy as jnp
from jax import lax
from jax.experimental import pallas as pl
from jax.experimental.pallas import tpu as pltpu
from jax.sharding import PartitionSpec as P

ITERS = 2
BR = 8
TILE = 128
K = 64
NT = (((1,), (1,)), ((), ()))
NN = (((1,), (0,)), ((), ()))
TN = (((0,), (0,)), ((), ()))
F32 = jnp.float32
BF16 = jnp.bfloat16
DOM, BAL = "dom", "bal"
UNROLL = 8


def hdot(a, b, dims=NN):
    return lax.dot_general(a, b, dims, precision=lax.Precision.HIGHEST, preferred_element_type=F32)


def bdot(a, b, dims):
    return lax.dot_general(a, b, dims, preferred_element_type=F32)


def swap(value, axis, size, distance):
    return lax.ppermute(value, axis, [(i, i ^ distance) for i in range(size)])


def swap_y(value, distance):
    return swap(value, BAL, lax.axis_size(BAL), distance)


def swap_core(value):
    return swap(value, DOM, lax.axis_size(DOM), 1)


def swap_next(value):
    size = lax.axis_size(DOM)
    route = []
    for i in range(1, size - 1, 2):
        route += [(i, i + 1), (i + 1, i)]
    return lax.ppermute(value, DOM, route)


def reduce_yzx(value):
    size = lax.axis_size(DOM)
    parts = [swap_y(value, k) for k in (1, 2, 3)]
    value = (value + parts[0]) + (parts[1] + parts[2])
    for unit in (2, 8):
        parts = [swap(value, DOM, size, k * unit) for k in (1, 2, 3)]
        value = (value + parts[0]) + (parts[1] + parts[2])
    return value


def reduce_all(value):
    return reduce_yzx(value + swap_core(value))


def reduce_halves(first, second, take_first):
    mine = jnp.where(take_first, first, second) + swap_core(jnp.where(take_first, second, first))
    mine = reduce_yzx(mine)
    other = swap_core(mine)
    return jnp.where(take_first, mine, other), jnp.where(take_first, other, mine)


VM = pl.BlockSpec(memory_space=pltpu.VMEM)
SM = pl.BlockSpec(memory_space=pltpu.SMEM)


def call(body, name, specs, outs, scratch, args, flops=0, nbytes=0, final=False):
    args = [pltpu.with_memory_space_constraint(a, pltpu.VMEM) if s is VM else a for s, a in zip(specs, args)]
    return pl.pallas_call(
        body,
        name=name,
        in_specs=specs,
        out_specs=tuple(VM for _ in outs),
        out_shape=tuple(jax.ShapeDtypeStruct(s, d) if final else pltpu.VMEM(s, d) for s, d in outs),
        scratch_shapes=scratch,
        compiler_params=pltpu.CompilerParams(vmem_limit_bytes=14 * 2**20),
        cost_estimate=pl.CostEstimate(flops=flops, bytes_accessed=nbytes, transcendentals=0),
    )(*args)


def inverse_factors(mats, out_ref):
    nb = K // 8
    row = lax.broadcasted_iota(jnp.int32, (8, K), 0)
    col = lax.broadcasted_iota(jnp.int32, (8, K), 1)
    work = []
    for g in mats:
        left = [g[8 * i : 8 * i + 8, :] for i in range(nb)]
        right = [jnp.where(row + 8 * i == col, 1.0, 0.0).astype(F32) for i in range(nb)]
        work.append((left, right))
    for k in range(0, K, 2):
        kb, kr = divmod(k, 8)
        for m, (left, right) in enumerate(work):
            r0, r1 = left[kb][kr : kr + 1, :], left[kb][kr + 1 : kr + 2, :]
            q0, q1 = right[kb][kr : kr + 1, :], right[kb][kr + 1 : kr + 2, :]
            a = jnp.broadcast_to(r0[:, k : k + 1], (1, K))
            b = jnp.broadcast_to(r0[:, k + 1 : k + 2], (1, K))
            c = jnp.broadcast_to(r1[:, k + 1 : k + 2], (1, K))
            inv = 1.0 / (a * c - b * b)
            if k < K - 2:
                p0, p1 = (c * r0 - b * r1) * inv, (a * r1 - b * r0) * inv
                s0, s1 = (c * q0 - b * q1) * inv, (a * q1 - b * q0) * inv
                for i in range(kb, nb):
                    if i == kb and kr == 6:
                        continue
                    f0, f1 = left[i][:, k : k + 1], left[i][:, k + 1 : k + 2]
                    if i == kb:
                        below = row[:, :1] > kr + 1
                        f0, f1 = jnp.where(below, f0, 0.0), jnp.where(below, f1, 0.0)
                    left[i] = left[i] - (f0 * p0 + f1 * p1)
                    right[i] = right[i] - (f0 * s0 + f1 * s1)
            t = b / a
            out_ref[m, k : k + 1, :] = q0 * lax.rsqrt(a)
            out_ref[m, k + 1 : k + 2, :] = (q1 - t * q0) * lax.rsqrt(c - b * t)


def split(x):
    hi = x.astype(BF16)
    return hi, (x - hi.astype(F32)).astype(BF16)


def lanes(ref):
    return jnp.concatenate([ref[b] for b in range(BR)], axis=1)


def gram_of(a, others):
    a_hi, a_lo = a
    o_hi = jnp.concatenate([o[0] for o in others], axis=0)
    o_lo = jnp.concatenate([o[1] for o in others], axis=0)
    main = bdot(jnp.concatenate([a_hi, a_lo], axis=0), o_hi, NT)
    return main[0:K] + (main[K : 2 * K] + bdot(a_hi, o_lo, NT))


def combine(weights, parts):
    w_hi, w_lo = split(weights)
    rhs = jnp.concatenate([p[0] for p in parts] + [p[1] for p in parts], axis=0)
    m = weights.shape[0]
    lhs = jnp.concatenate([w_hi, w_lo], axis=0)
    lhs = jnp.concatenate([lhs, lhs], axis=1)
    out = bdot(lhs, rhs, NN)
    return out[0:m] + out[m : 2 * m]


def start_gram_kernel(x_ref, g_ref):
    g = jnp.zeros((K, K), F32)
    for b in range(BR):
        g = g + hdot(x_ref[b], x_ref[b], NT)
    g_ref[...] = g


def start_norm_kernel(g_ref, x_ref, n_ref, basis_ref, low_ref, lt_ref, inv_ref):
    g = g_ref[...] * (1.0 / n_ref[0])
    inverse_factors([g], inv_ref)
    inv = inv_ref[0]
    lt_ref[...] = hdot(inv, g)
    for b in range(BR):
        v = hdot(inv, x_ref[b])
        basis_ref[b] = v
        low_ref[b] = v.astype(BF16)


def mid_kernel(low_ref, q1_ref, q2_ref, q3_ref, pa_ref, cp_ref, zp_ref, own4_ref, o0_ref, o1_ref, o2_ref, o3_ref):
    for k, src in enumerate((low_ref, q1_ref, q2_ref, q3_ref)):
        own4_ref[8 * k : 8 * k + 8] = src[...]
    o0_ref[...] = pa_ref[0:8]
    o1_ref[...] = pa_ref[8:16].astype(BF16)
    for k, out in ((0, o2_ref), (8, o3_ref)):
        v = pa_ref[16 + k : 24 + k] + cp_ref[k : 8 + k].astype(F32) + zp_ref[k : 8 + k].astype(F32)
        out[...] = v.astype(BF16)


def join_kernel(a_ref, b_ref, out_ref):
    out_ref[0:8] = a_ref[...]
    out_ref[8:16] = b_ref[...]


def apply_m_kernel(col_ref, row_ref, own_ref, cp_ref, zp_ref, tiles_ref, out_ref, low_ref, win, acc):
    win[0:32] = own_ref[...]
    win[32:64] = cp_ref[...]
    win[64:96] = zp_ref[...]
    acc[...] = jnp.zeros_like(acc)
    slots = tiles_ref.shape[0]

    def step(s, carry):
        base = s * UNROLL
        parts = []
        for u in range(UNROLL):
            parts.append(bdot(win[col_ref[base + u]], tiles_ref[base + u], NT))
        for u in range(UNROLL):
            r = row_ref[base + u]
            acc[r] = acc[r] + parts[u]
        return carry

    lax.fori_loop(0, slots // UNROLL, step, 0)
    for b in range(BR):
        v = acc[b]
        out_ref[b] = v
        low_ref[b] = v.astype(BF16)


def apply_mt_kernel(
    col_ref, row_ref, back0_ref, b1_ref, b2_ref, b3_ref, tiles_ref, own_ref, cp_ref, zp_ref, low, acc
):
    for b in range(BR):
        v = back0_ref[b] + b1_ref[b].astype(F32) + b2_ref[b].astype(F32) + b3_ref[b].astype(F32)
        low[b] = v.astype(BF16)
    low[BR] = jnp.zeros((K, TILE), BF16)
    acc[...] = jnp.zeros_like(acc)
    slots = tiles_ref.shape[0]

    def step(s, carry):
        base = s * UNROLL
        parts = []
        for u in range(UNROLL):
            parts.append(bdot(low[row_ref[base + u]], tiles_ref[base + u], NN))
        for u in range(UNROLL):
            c = col_ref[base + u]
            acc[c] = acc[c] + parts[u]
        return carry

    lax.fori_loop(0, slots // UNROLL, step, 0)
    own_ref[...] = acc[0:32]
    cp_ref[...] = acc[32:64].astype(BF16)
    zp_ref[...] = acc[64:96].astype(BF16)


def apply_at_kernel(col_ref, low_ref, tiles_ref, own_ref, cp_ref, zp_ref, acc):
    acc[...] = jnp.zeros_like(acc)
    slots = tiles_ref.shape[1]
    for b in range(BR):
        x = low_ref[b]
        parts = [bdot(x, tiles_ref[b, j], NN) for j in range(slots)]
        for j in range(slots):
            c = col_ref[b * slots + j]
            acc[c] = acc[c] + parts[j]
    own_ref[...] = acc[0:32]
    cp_ref[...] = acc[32:48].astype(BF16)
    zp_ref[...] = acc[48:64].astype(BF16)


def collect_m_kernel(own_ref, cp_ref, zp_ref, o0_ref, o1_ref, o2_ref, o3_ref):
    v = own_ref[...] + cp_ref[...].astype(F32) + zp_ref[...].astype(F32)
    o0_ref[...] = v[0:8]
    o1_ref[...] = v[8:16].astype(BF16)
    o2_ref[...] = v[16:24].astype(BF16)
    o3_ref[...] = v[24:32].astype(BF16)


def apply_a_kernel(first, col_ref, low_ref, r1_ref, r2_ref, r3_ref, cp_ref, zp_ref, tiles_ref, shadow_ref, *refs):
    if first:
        image_ref, g_ref, win = refs
    else:
        basis_ref, res_ref, image_ref, g_ref, rest_ref, win = refs
    for k, src in enumerate((low_ref, r1_ref, r2_ref, r3_ref)):
        win[8 * k : 8 * k + 8] = src[...]
    win[32:48] = cp_ref[...]
    win[48:64] = zp_ref[...]
    slots = tiles_ref.shape[1]
    rows = []
    for b in range(BR):
        x = jnp.concatenate([win[col_ref[b * slots + j]] for j in range(slots)], axis=1)
        t = jnp.concatenate([tiles_ref[b, j] for j in range(slots)], axis=1)
        v = bdot(x, t, NT)
        image_ref[b] = v
        rows.append(v)
    image = split(jnp.concatenate(rows, axis=1))
    others = [split(lanes(shadow_ref)), image]
    if not first:
        others += [split(lanes(res_ref)), split(lanes(basis_ref))]
    g = gram_of(image, others)
    g_ref[0:64] = g[:, 0:128]
    if not first:
        g_ref[64:96] = g[0:32, 128:256]
        rest_ref[...] = g[32:64, 128:256]


def back_gram_kernel(first, o0_ref, b1_ref, b2_ref, b3_ref, shadow_ref, *refs):
    if first:
        bi_ref, g_ref = refs
    else:
        rest_ref, bi_ref, g_ref = refs
        g_ref[64:96] = rest_ref[...]
    rows = []
    for b in range(BR):
        v = o0_ref[b] + b1_ref[b].astype(F32) + b2_ref[b].astype(F32) + b3_ref[b].astype(F32)
        bi_ref[b] = v
        rows.append(v)
    back = split(jnp.concatenate(rows, axis=1))
    g_ref[0:64] = gram_of(back, [back, split(lanes(shadow_ref))])


def update_kernel(first, last, f_ref, b_ref, n_ref, image_ref, bi_ref, basis_ref, shadow_ref, precond_ref, res_ref, *refs):
    refs, inv_ref, w_ref = refs[:-2], refs[-2], refs[-1]
    if first:
        lt_ref, outs = refs[0], refs[1:]
    else:
        sol_ref, outs = refs[0], refs[1:]
    if last:
        sol_out, res_out, basis_out, shadow_out = outs
    else:
        sol_out, res_out, basis_out, shadow_out, blow_out, slow_out = outs
    total = n_ref[0]
    image_shadow = f_ref[0:64, 0:64]
    coup_t = image_shadow * (1.0 / total)
    coup = coup_t.T
    normal = f_ref[0:64, 64:128]
    bb = b_ref[0:64, 0:64]
    bs = b_ref[0:64, 64:128]
    if first:
        ib = image_shadow
        target = hdot(image_shadow, lt_ref[...])
    else:
        target = jnp.concatenate([f_ref[64:96, 0:64], b_ref[64:96, 0:64]], axis=0)
        ib = jnp.concatenate([f_ref[64:96, 64:128], b_ref[64:96, 64:128]], axis=0)
    y = hdot(ib, coup)
    uu = normal - y - y.T + total * hdot(coup_t, coup)
    y = hdot(bs, coup_t)
    ss = bb - y - y.T + total * hdot(coup, coup_t)
    inverse_factors([normal, uu * (1.0 / total), ss * (1.0 / total)], inv_ref)
    inv_n, inv_u, inv_s = inv_ref[0], inv_ref[1], inv_ref[2]
    w_t = hdot(hdot(inv_n, target), inv_n, TN)
    w_ref[0:64, 0:64] = inv_u
    w_ref[0:64, 64:128] = -hdot(inv_u, coup_t)
    w_ref[64:128, 0:64] = -w_t
    w_ref[64:128, 64:128] = jnp.zeros((K, K), F32)
    w_ref[128:192, 0:64] = inv_s
    w_ref[128:192, 64:128] = -hdot(inv_s, coup)
    w_ref[192:256, 0:64] = w_t
    w_ref[192:256, 64:128] = jnp.zeros((K, K), F32)
    zero = jnp.zeros((K, BR * TILE), BF16)
    first_two = combine(w_ref[0:128], [split(lanes(image_ref)), split(lanes(basis_ref))])
    third = combine(w_ref[128:192], [split(lanes(bi_ref)), split(lanes(shadow_ref))])
    fourth = combine(w_ref[192:256], [split(lanes(precond_ref)), (zero, zero)])
    for b in range(BR):
        at = slice(b * TILE, (b + 1) * TILE)
        v = fourth[:, at]
        sol_out[b] = v if first else sol_ref[b] + v
        res_out[b] = res_ref[b] + first_two[K : 2 * K, at]
        v = first_two[0:K, at]
        basis_out[b] = v
        if not last:
            blow_out[b] = v.astype(BF16)
        v = third[:, at]
        shadow_out[b] = v
        if not last:
            slow_out[b] = v.astype(BF16)


def shards(right_side, a_tiles, a_cols, m_tiles, m_rows, m_cols, m_count):
    blk = (BR, K, TILE)
    total = BR * TILE * lax.axis_size((DOM, BAL))
    group = lax.axis_index(DOM)
    y = lax.axis_index(BAL)
    first_row = (group * lax.axis_size(BAL) + y) * BR
    n_arr = jnp.full((1,), float(total), F32)

    def place(cols, skip):
        dev = cols // BR
        g, rel = dev // 4, (dev % 4) ^ y
        width = 4 - skip
        local = jnp.where(
            g == group, rel, jnp.where(g == (group ^ 1), 4 + rel - skip, 4 + width + rel - skip)
        )
        return local * BR + cols % BR

    a_place = place(a_cols, 2).reshape(-1)
    m_place = place(m_cols, 0)
    live = jnp.arange(m_tiles.shape[0], dtype=jnp.int32) < m_count[0]
    m_local = jnp.where(live, m_rows - first_row, BR)

    is_first_core = jnp.broadcast_to(group % 2 == 0, (1, 128))
    right_side, a_place, m_place, m_local, n_arr, is_first_core = lax.optimization_barrier(
        (right_side, a_place, m_place, m_local, n_arr, is_first_core)
    )

    (g0,) = call(start_gram_kernel, "start_gram", [VM], [((K, K), F32)], [], (right_side,))
    g0 = reduce_all(g0)
    basis, blow, lt = call(
        start_norm_kernel,
        "start_norm",
        [VM, VM, SM],
        [(blk, F32), (blk, BF16), ((K, K), F32)],
        [pltpu.VMEM((1, K, K), F32)],
        (g0, right_side, n_arr),
    )
    shadow, slow = basis, blow
    solution, residual = None, right_side
    for iteration in range(ITERS):
        last = iteration == ITERS - 1
        q = [swap_y(blow, k) for k in (1, 2, 3)]
        pa_own, pa_cp, pa_zp = call(
            apply_at_kernel,
            "apply_at",
            [SM, VM, VM],
            [((32, K, TILE), F32), ((16, K, TILE), BF16), ((16, K, TILE), BF16)],
            [pltpu.VMEM((64, K, TILE), F32)],
            (a_place, slow, a_tiles),
            flops=84_000_000,
            nbytes=3_000_000,
        )
        ra_zp, ra_cp = swap_next(pa_zp), swap_core(pa_cp)
        own4, o0, o1, o2, o3 = call(
            mid_kernel,
            "mid",
            [VM] * 7,
            [((32, K, TILE), BF16), (blk, F32)] + [(blk, BF16)] * 3,
            [],
            (blow, *q, pa_own, ra_cp, ra_zp),
        )
        m_zp = swap_next(own4)
        b1, b2, b3 = swap_y(o1, 1), swap_y(o2, 2), swap_y(o3, 3)
        m_cp = swap_core(own4)
        pm_own, pm_cp, pm_zp = call(
            apply_mt_kernel,
            "apply_mt",
            [SM, SM] + [VM] * 5,
            [((32, K, TILE), F32), ((32, K, TILE), BF16), ((32, K, TILE), BF16)],
            [pltpu.VMEM((BR + 1, K, TILE), BF16), pltpu.VMEM((96, K, TILE), F32)],
            (m_place, m_local, o0, b1, b2, b3, m_tiles),
            flops=218_000_000,
            nbytes=5_000_000,
        )
        rm_zp, rm_cp = swap_next(pm_zp), swap_core(pm_cp)
        precond, plow = call(
            apply_m_kernel,
            "apply_m",
            [SM, SM] + [VM] * 4,
            [(blk, F32), (blk, BF16)],
            [pltpu.VMEM((96, K, TILE), BF16), pltpu.VMEM((BR + 1, K, TILE), F32)],
            (m_place, m_local, own4, m_cp, m_zp, m_tiles),
            flops=218_000_000,
            nbytes=5_000_000,
        )
        r = [swap_y(plow, k) for k in (1, 2, 3)]
        (far,) = call(join_kernel, "join", [VM] * 2, [((16, K, TILE), BF16)], [], (r[1], r[2]))
        a_zp, a_cp = swap_next(far), swap_core(far)
        far, pm_own, rm_cp, rm_zp = lax.optimization_barrier((far, pm_own, rm_cp, rm_zp))
        o0, o1, o2, o3 = call(
            collect_m_kernel,
            "collect_m",
            [VM] * 3,
            [(blk, F32)] + [(blk, BF16)] * 3,
            [],
            (pm_own, rm_cp, rm_zp),
        )
        b1, b2, b3 = swap_y(o1, 1), swap_y(o2, 2), swap_y(o3, 3)
        first = iteration == 0
        height = 64 if first else 96
        image, g_fwd, *rest = call(
            lambda *refs, f=first: apply_a_kernel(f, *refs),
            "apply_a",
            [SM] + [VM] * (8 if first else 10),
            [(blk, F32), ((height, 128), F32)] + ([] if first else [((32, 128), F32)]),
            [pltpu.VMEM((64, K, TILE), BF16)],
            (a_place, plow, *r, a_cp, a_zp, a_tiles, shadow, *([] if first else [basis, residual])),
            flops=84_000_000,
            nbytes=3_000_000,
        )
        back_image, g_bwd = call(
            lambda *refs, f=first: back_gram_kernel(f, *refs),
            "back_gram",
            [VM] * (5 if first else 6),
            [(blk, F32), ((height, 128), F32)],
            [],
            (o0, b1, b2, b3, shadow, *rest),
        )
        g_fwd, g_bwd = reduce_halves(g_fwd, g_bwd, is_first_core)
        args = [g_fwd, g_bwd, n_arr, image, back_image, basis, shadow, precond, residual]
        args.append(lt if first else solution)
        outs = [(blk, F32)] * 4 + ([] if last else [(blk, BF16)] * 2)
        result = call(
            lambda *refs, f=iteration == 0, l=last: update_kernel(f, l, *refs),
            "update",
            [VM, VM, SM] + [VM] * (len(args) - 3),
            outs,
            [pltpu.VMEM((3, K, K), F32), pltpu.VMEM((256, 128), F32)],
            args,
            final=last,
        )
        solution, residual, basis, shadow = result[:4]
        if not last:
            blow, slow = result[4:]
    return (solution, residual, basis, shadow)


def solution(mesh):
    rows = P((DOM, BAL))
    return jax.shard_map(
        shards,
        mesh=mesh,
        in_specs=(rows,) * 7,
        out_specs=(rows,) * 4,
        check_vma=False,
    )
```

```python
import jax
import jax.numpy as jnp
from jax import lax
from jax.experimental import pallas as pl
from jax.experimental.pallas import tpu as pltpu
from jax.sharding import PartitionSpec as P

ITERS = 2
BR = 8
TILE = 128
K = 64
NT = (((1,), (1,)), ((), ()))
NN = (((1,), (0,)), ((), ()))
TN = (((0,), (0,)), ((), ()))
F32 = jnp.float32
BF16 = jnp.bfloat16
DOM, BAL = "dom", "bal"
UNROLL = 26


def hdot(a, b, dims=NN):
    return lax.dot_general(a, b, dims, precision=lax.Precision.HIGHEST, preferred_element_type=F32)


def bdot(a, b, dims):
    return lax.dot_general(a, b, dims, preferred_element_type=F32)


def swap(value, axis, size, distance):
    return lax.ppermute(value, axis, [(i, i ^ distance) for i in range(size)])


def swap_y(value, distance):
    return swap(value, BAL, lax.axis_size(BAL), distance)


def swap_core(value):
    return swap(value, DOM, lax.axis_size(DOM), 1)


def swap_next(value):
    size = lax.axis_size(DOM)
    route = []
    for i in range(1, size - 1, 2):
        route += [(i, i + 1), (i + 1, i)]
    return lax.ppermute(value, DOM, route)


def reduce_yzx(value):
    size = lax.axis_size(DOM)
    parts = [swap_y(value, k) for k in (1, 2, 3)]
    value = (value + parts[0]) + (parts[1] + parts[2])
    for unit in (2, 8):
        parts = [swap(value, DOM, size, k * unit) for k in (1, 2, 3)]
        value = (value + parts[0]) + (parts[1] + parts[2])
    return value


def reduce_all(value):
    return reduce_yzx(value + swap_core(value))


def reduce_halves(first, second, take_first):
    mine = jnp.where(take_first, first, second) + swap_core(jnp.where(take_first, second, first))
    mine = reduce_yzx(mine)
    other = swap_core(mine)
    return jnp.where(take_first, mine, other), jnp.where(take_first, other, mine)


VM = pl.BlockSpec(memory_space=pltpu.VMEM)
SM = pl.BlockSpec(memory_space=pltpu.SMEM)


def call(body, name, specs, outs, scratch, args, flops=0, nbytes=0, final=False):
    args = [pltpu.with_memory_space_constraint(a, pltpu.VMEM) if s is VM else a for s, a in zip(specs, args)]
    return pl.pallas_call(
        body,
        name=name,
        in_specs=specs,
        out_specs=tuple(VM for _ in outs),
        out_shape=tuple(jax.ShapeDtypeStruct(s, d) if final else pltpu.VMEM(s, d) for s, d in outs),
        scratch_shapes=scratch,
        compiler_params=pltpu.CompilerParams(vmem_limit_bytes=14 * 2**20),
        cost_estimate=pl.CostEstimate(flops=flops, bytes_accessed=nbytes, transcendentals=0),
    )(*args)


def inverse_factors(mats, out_ref):
    nb = K // 8
    row = lax.broadcasted_iota(jnp.int32, (8, K), 0)
    col = lax.broadcasted_iota(jnp.int32, (8, K), 1)
    work = []
    for g in mats:
        left = [g[8 * i : 8 * i + 8, :] for i in range(nb)]
        right = [jnp.where(row + 8 * i == col, 1.0, 0.0).astype(F32) for i in range(nb)]
        work.append((left, right))
    for k in range(0, K, 2):
        kb, kr = divmod(k, 8)
        for m, (left, right) in enumerate(work):
            r0, r1 = left[kb][kr : kr + 1, :], left[kb][kr + 1 : kr + 2, :]
            q0, q1 = right[kb][kr : kr + 1, :], right[kb][kr + 1 : kr + 2, :]
            a = jnp.broadcast_to(r0[:, k : k + 1], (1, K))
            b = jnp.broadcast_to(r0[:, k + 1 : k + 2], (1, K))
            c = jnp.broadcast_to(r1[:, k + 1 : k + 2], (1, K))
            inv = 1.0 / (a * c - b * b)
            if k < K - 2:
                p0, p1 = (c * r0 - b * r1) * inv, (a * r1 - b * r0) * inv
                s0, s1 = (c * q0 - b * q1) * inv, (a * q1 - b * q0) * inv
                for i in range(kb, nb):
                    if i == kb and kr == 6:
                        continue
                    f0, f1 = left[i][:, k : k + 1], left[i][:, k + 1 : k + 2]
                    if i == kb:
                        below = row[:, :1] > kr + 1
                        f0, f1 = jnp.where(below, f0, 0.0), jnp.where(below, f1, 0.0)
                    left[i] = left[i] - (f0 * p0 + f1 * p1)
                    right[i] = right[i] - (f0 * s0 + f1 * s1)
            t = b / a
            out_ref[m, k : k + 1, :] = q0 * lax.rsqrt(a)
            out_ref[m, k + 1 : k + 2, :] = (q1 - t * q0) * lax.rsqrt(c - b * t)


def split(x):
    hi = x.astype(BF16)
    return hi, (x - hi.astype(F32)).astype(BF16)


def lanes(ref):
    return jnp.concatenate([ref[b] for b in range(BR)], axis=1)


def gram_of(a, others):
    a_hi, a_lo = a
    o_hi = jnp.concatenate([o[0] for o in others], axis=0)
    o_lo = jnp.concatenate([o[1] for o in others], axis=0)
    main = bdot(jnp.concatenate([a_hi, a_lo], axis=0), o_hi, NT)
    return main[0:K] + (main[K : 2 * K] + bdot(a_hi, o_lo, NT))


def combine(weights, parts):
    w_hi, w_lo = split(weights)
    rhs = jnp.concatenate([p[0] for p in parts] + [p[1] for p in parts], axis=0)
    m = weights.shape[0]
    lhs = jnp.concatenate([w_hi, w_lo], axis=0)
    lhs = jnp.concatenate([lhs, lhs], axis=1)
    out = bdot(lhs, rhs, NN)
    return out[0:m] + out[m : 2 * m]


def start_gram_kernel(x_ref, g_ref):
    g = jnp.zeros((K, K), F32)
    for b in range(BR):
        g = g + hdot(x_ref[b], x_ref[b], NT)
    g_ref[...] = g


def start_norm_kernel(g_ref, x_ref, n_ref, basis_ref, low_ref, lt_ref, inv_ref):
    g = g_ref[...] * (1.0 / n_ref[0])
    inverse_factors([g], inv_ref)
    inv = inv_ref[0]
    lt_ref[...] = hdot(inv, g)
    for b in range(BR):
        v = hdot(inv, x_ref[b])
        basis_ref[b] = v
        low_ref[b] = v.astype(BF16)


def mid_kernel(low_ref, q1_ref, q2_ref, q3_ref, pa_ref, cp_ref, zp_ref, own4_ref, o0_ref, o1_ref, o2_ref, o3_ref):
    for k, src in enumerate((low_ref, q1_ref, q2_ref, q3_ref)):
        own4_ref[8 * k : 8 * k + 8] = src[...]
    o0_ref[...] = pa_ref[0:8]
    o1_ref[...] = pa_ref[8:16].astype(BF16)
    for k, out in ((0, o2_ref), (8, o3_ref)):
        v = pa_ref[16 + k : 24 + k] + cp_ref[k : 8 + k].astype(F32) + zp_ref[k : 8 + k].astype(F32)
        out[...] = v.astype(BF16)


def join_kernel(a_ref, b_ref, out_ref):
    out_ref[0:8] = a_ref[...]
    out_ref[8:16] = b_ref[...]


def apply_m_kernel(col_ref, row_ref, own_ref, cp_ref, zp_ref, tiles_ref, out_ref, low_ref, win, acc):
    win[0:32] = own_ref[...]
    win[32:64] = cp_ref[...]
    win[64:96] = zp_ref[...]
    acc[...] = jnp.zeros_like(acc)
    slots = tiles_ref.shape[0]

    def step(s, carry):
        base = s * UNROLL
        parts = []
        for u in range(UNROLL):
            parts.append(bdot(win[col_ref[base + u]], tiles_ref[base + u], NT))
        for u in range(UNROLL):
            r = row_ref[base + u]
            acc[r] = acc[r] + parts[u]
        return carry

    lax.fori_loop(0, slots // UNROLL, step, 0)
    for b in range(BR):
        v = acc[b]
        out_ref[b] = v
        low_ref[b] = v.astype(BF16)


def apply_mt_kernel(
    col_ref, row_ref, back0_ref, b1_ref, b2_ref, b3_ref, tiles_ref, own_ref, cp_ref, zp_ref, low, acc
):
    for b in range(BR):
        v = back0_ref[b] + b1_ref[b].astype(F32) + b2_ref[b].astype(F32) + b3_ref[b].astype(F32)
        low[b] = v.astype(BF16)
    low[BR] = jnp.zeros((K, TILE), BF16)
    acc[...] = jnp.zeros_like(acc)
    slots = tiles_ref.shape[0]

    def step(s, carry):
        base = s * UNROLL
        parts = []
        for u in range(UNROLL):
            parts.append(bdot(low[row_ref[base + u]], tiles_ref[base + u], NN))
        for u in range(UNROLL):
            c = col_ref[base + u]
            acc[c] = acc[c] + parts[u]
        return carry

    lax.fori_loop(0, slots // UNROLL, step, 0)
    own_ref[...] = acc[0:32]
    cp_ref[...] = acc[32:64].astype(BF16)
    zp_ref[...] = acc[64:96].astype(BF16)


def apply_at_kernel(col_ref, low_ref, tiles_ref, own_ref, cp_ref, zp_ref, acc):
    acc[...] = jnp.zeros_like(acc)
    slots = tiles_ref.shape[1]
    for b in range(BR):
        x = low_ref[b]
        parts = [bdot(x, tiles_ref[b, j], NN) for j in range(slots)]
        for j in range(slots):
            c = col_ref[b * slots + j]
            acc[c] = acc[c] + parts[j]
    own_ref[...] = acc[0:32]
    cp_ref[...] = acc[32:48].astype(BF16)
    zp_ref[...] = acc[48:64].astype(BF16)


def collect_m_kernel(own_ref, cp_ref, zp_ref, o0_ref, o1_ref, o2_ref, o3_ref):
    v = own_ref[...] + cp_ref[...].astype(F32) + zp_ref[...].astype(F32)
    o0_ref[...] = v[0:8]
    o1_ref[...] = v[8:16].astype(BF16)
    o2_ref[...] = v[16:24].astype(BF16)
    o3_ref[...] = v[24:32].astype(BF16)


def apply_a_kernel(first, col_ref, low_ref, r1_ref, r2_ref, r3_ref, cp_ref, zp_ref, tiles_ref, shadow_ref, *refs):
    if first:
        image_ref, g_ref, win = refs
    else:
        basis_ref, res_ref, image_ref, g_ref, rest_ref, win = refs
    for k, src in enumerate((low_ref, r1_ref, r2_ref, r3_ref)):
        win[8 * k : 8 * k + 8] = src[...]
    win[32:48] = cp_ref[...]
    win[48:64] = zp_ref[...]
    slots = tiles_ref.shape[1]
    rows = []
    for b in range(BR):
        x = jnp.concatenate([win[col_ref[b * slots + j]] for j in range(slots)], axis=1)
        t = jnp.concatenate([tiles_ref[b, j] for j in range(slots)], axis=1)
        v = bdot(x, t, NT)
        image_ref[b] = v
        rows.append(v)
    image = split(jnp.concatenate(rows, axis=1))
    others = [split(lanes(shadow_ref)), image]
    if not first:
        others += [split(lanes(res_ref)), split(lanes(basis_ref))]
    g = gram_of(image, others)
    g_ref[0:64] = g[:, 0:128]
    if not first:
        g_ref[64:96] = g[0:32, 128:256]
        rest_ref[...] = g[32:64, 128:256]


def back_gram_kernel(first, o0_ref, b1_ref, b2_ref, b3_ref, shadow_ref, *refs):
    if first:
        bi_ref, g_ref = refs
    else:
        rest_ref, bi_ref, g_ref = refs
        g_ref[64:96] = rest_ref[...]
    rows = []
    for b in range(BR):
        v = o0_ref[b] + b1_ref[b].astype(F32) + b2_ref[b].astype(F32) + b3_ref[b].astype(F32)
        bi_ref[b] = v
        rows.append(v)
    back = split(jnp.concatenate(rows, axis=1))
    g_ref[0:64] = gram_of(back, [back, split(lanes(shadow_ref))])


def update_kernel(first, last, f_ref, b_ref, n_ref, image_ref, bi_ref, basis_ref, shadow_ref, precond_ref, res_ref, *refs):
    refs, inv_ref, w_ref = refs[:-2], refs[-2], refs[-1]
    if first:
        lt_ref, outs = refs[0], refs[1:]
    else:
        sol_ref, outs = refs[0], refs[1:]
    if last:
        sol_out, res_out, basis_out, shadow_out = outs
    else:
        sol_out, res_out, basis_out, shadow_out, blow_out, slow_out = outs
    total = n_ref[0]
    image_shadow = f_ref[0:64, 0:64]
    coup_t = image_shadow * (1.0 / total)
    coup = coup_t.T
    normal = f_ref[0:64, 64:128]
    bb = b_ref[0:64, 0:64]
    bs = b_ref[0:64, 64:128]
    if first:
        ib = image_shadow
        target = hdot(image_shadow, lt_ref[...])
    else:
        target = jnp.concatenate([f_ref[64:96, 0:64], b_ref[64:96, 0:64]], axis=0)
        ib = jnp.concatenate([f_ref[64:96, 64:128], b_ref[64:96, 64:128]], axis=0)
    uu = normal - hdot(ib, coup_t, NT) - hdot(coup_t, ib, NT) + total * hdot(coup_t, coup_t, NT)
    ss = bb - hdot(bs, coup_t) - hdot(coup, bs, NT) + total * hdot(coup_t, coup_t, TN)
    inverse_factors([normal, uu * (1.0 / total), ss * (1.0 / total)], inv_ref)
    inv_n, inv_u, inv_s = inv_ref[0], inv_ref[1], inv_ref[2]
    w_t = hdot(hdot(inv_n, target), inv_n, TN)
    w_ref[0:64, 0:64] = inv_u
    w_ref[0:64, 64:128] = -hdot(inv_u, coup_t)
    w_ref[64:128, 0:64] = -w_t
    w_ref[64:128, 64:128] = jnp.zeros((K, K), F32)
    w_ref[128:192, 0:64] = inv_s
    w_ref[128:192, 64:128] = -hdot(inv_s, coup)
    first_two = combine(w_ref[0:128], [split(lanes(image_ref)), split(lanes(basis_ref))])
    third = combine(w_ref[128:192], [split(lanes(bi_ref)), split(lanes(shadow_ref))])
    fourth = combine(w_t, [split(lanes(precond_ref))])
    for b in range(BR):
        at = slice(b * TILE, (b + 1) * TILE)
        v = fourth[:, at]
        sol_out[b] = v if first else sol_ref[b] + v
        res_out[b] = res_ref[b] + first_two[K : 2 * K, at]
        v = first_two[0:K, at]
        basis_out[b] = v
        if not last:
            blow_out[b] = v.astype(BF16)
        v = third[:, at]
        shadow_out[b] = v
        if not last:
            slow_out[b] = v.astype(BF16)


def shards(right_side, a_tiles, a_cols, m_tiles, m_rows, m_cols, m_count):
    blk = (BR, K, TILE)
    total = BR * TILE * lax.axis_size((DOM, BAL))
    group = lax.axis_index(DOM)
    y = lax.axis_index(BAL)
    first_row = (group * lax.axis_size(BAL) + y) * BR
    n_arr = jnp.full((1,), float(total), F32)

    def place(cols, skip):
        dev = cols // BR
        g, rel = dev // 4, (dev % 4) ^ y
        width = 4 - skip
        local = jnp.where(
            g == group, rel, jnp.where(g == (group ^ 1), 4 + rel - skip, 4 + width + rel - skip)
        )
        return local * BR + cols % BR

    a_place = place(a_cols, 2).reshape(-1)
    m_place = place(m_cols, 0)
    live = jnp.arange(m_tiles.shape[0], dtype=jnp.int32) < m_count[0]
    m_local = jnp.where(live, m_rows - first_row, BR)

    is_first_core = jnp.broadcast_to(group % 2 == 0, (1, 128))
    right_side, a_place, m_place, m_local, n_arr, is_first_core = lax.optimization_barrier(
        (right_side, a_place, m_place, m_local, n_arr, is_first_core)
    )

    (g0,) = call(start_gram_kernel, "start_gram", [VM], [((K, K), F32)], [], (right_side,))
    g0 = reduce_all(g0)
    basis, blow, lt = call(
        start_norm_kernel,
        "start_norm",
        [VM, VM, SM],
        [(blk, F32), (blk, BF16), ((K, K), F32)],
        [pltpu.VMEM((1, K, K), F32)],
        (g0, right_side, n_arr),
    )
    shadow, slow = basis, blow
    solution, residual = None, right_side
    for iteration in range(ITERS):
        last = iteration == ITERS - 1
        q = [swap_y(blow, k) for k in (1, 2, 3)]
        pa_own, pa_cp, pa_zp = call(
            apply_at_kernel,
            "apply_at",
            [SM, VM, VM],
            [((32, K, TILE), F32), ((16, K, TILE), BF16), ((16, K, TILE), BF16)],
            [pltpu.VMEM((64, K, TILE), F32)],
            (a_place, slow, a_tiles),
            flops=84_000_000,
            nbytes=3_000_000,
        )
        ra_zp, ra_cp = swap_next(pa_zp), swap_core(pa_cp)
        own4, o0, o1, o2, o3 = call(
            mid_kernel,
            "mid",
            [VM] * 7,
            [((32, K, TILE), BF16), (blk, F32)] + [(blk, BF16)] * 3,
            [],
            (blow, *q, pa_own, ra_cp, ra_zp),
        )
        m_zp = swap_next(own4)
        b1, b2, b3 = swap_y(o1, 1), swap_y(o2, 2), swap_y(o3, 3)
        m_cp = swap_core(own4)
        pm_own, pm_cp, pm_zp = call(
            apply_mt_kernel,
            "apply_mt",
            [SM, SM] + [VM] * 5,
            [((32, K, TILE), F32), ((32, K, TILE), BF16), ((32, K, TILE), BF16)],
            [pltpu.VMEM((BR + 1, K, TILE), BF16), pltpu.VMEM((96, K, TILE), F32)],
            (m_place, m_local, o0, b1, b2, b3, m_tiles),
            flops=218_000_000,
            nbytes=5_000_000,
        )
        rm_zp, rm_cp = swap_next(pm_zp), swap_core(pm_cp)
        precond, plow = call(
            apply_m_kernel,
            "apply_m",
            [SM, SM] + [VM] * 4,
            [(blk, F32), (blk, BF16)],
            [pltpu.VMEM((96, K, TILE), BF16), pltpu.VMEM((BR + 1, K, TILE), F32)],
            (m_place, m_local, own4, m_cp, m_zp, m_tiles),
            flops=218_000_000,
            nbytes=5_000_000,
        )
        r = [swap_y(plow, k) for k in (1, 2, 3)]
        (far,) = call(join_kernel, "join", [VM] * 2, [((16, K, TILE), BF16)], [], (r[1], r[2]))
        a_zp, a_cp = swap_next(far), swap_core(far)
        far, pm_own, rm_cp, rm_zp = lax.optimization_barrier((far, pm_own, rm_cp, rm_zp))
        o0, o1, o2, o3 = call(
            collect_m_kernel,
            "collect_m",
            [VM] * 3,
            [(blk, F32)] + [(blk, BF16)] * 3,
            [],
            (pm_own, rm_cp, rm_zp),
        )
        b1, b2, b3 = swap_y(o1, 1), swap_y(o2, 2), swap_y(o3, 3)
        first = iteration == 0
        height = 64 if first else 96
        image, g_fwd, *rest = call(
            lambda *refs, f=first: apply_a_kernel(f, *refs),
            "apply_a",
            [SM] + [VM] * (8 if first else 10),
            [(blk, F32), ((height, 128), F32)] + ([] if first else [((32, 128), F32)]),
            [pltpu.VMEM((64, K, TILE), BF16)],
            (a_place, plow, *r, a_cp, a_zp, a_tiles, shadow, *([] if first else [basis, residual])),
            flops=84_000_000,
            nbytes=3_000_000,
        )
        back_image, g_bwd = call(
            lambda *refs, f=first: back_gram_kernel(f, *refs),
            "back_gram",
            [VM] * (5 if first else 6),
            [(blk, F32), ((height, 128), F32)],
            [],
            (o0, b1, b2, b3, shadow, *rest),
        )
        g_fwd, g_bwd = reduce_halves(g_fwd, g_bwd, is_first_core)
        args = [g_fwd, g_bwd, n_arr, image, back_image, basis, shadow, precond, residual]
        args.append(lt if first else solution)
        outs = [(blk, F32)] * 4 + ([] if last else [(blk, BF16)] * 2)
        result = call(
            lambda *refs, f=iteration == 0, l=last: update_kernel(f, l, *refs),
            "update",
            [VM, VM, SM] + [VM] * (len(args) - 3),
            outs,
            [pltpu.VMEM((3, K, K), F32), pltpu.VMEM((192, 128), F32)],
            args,
            final=last,
        )
        solution, residual, basis, shadow = result[:4]
        if not last:
            blow, slow = result[4:]
    return (solution, residual, basis, shadow)


def solution(mesh):
    rows = P((DOM, BAL))
    return jax.shard_map(
        shards,
        mesh=mesh,
        in_specs=(rows,) * 7,
        out_specs=(rows,) * 4,
        check_vma=False,
    )
```

```python
import jax
import jax.numpy as jnp
from jax import lax
from jax.experimental import pallas as pl
from jax.experimental.pallas import tpu as pltpu
from jax.sharding import PartitionSpec as P


ITERS = 2
BR = 8
TILE = 128
K = 64
NT = (((1,), (1,)), ((), ()))
NN = (((1,), (0,)), ((), ()))
TN = (((0,), (0,)), ((), ()))
F32 = jnp.float32
BF16 = jnp.bfloat16
DOM, BAL = "dom", "bal"
UNROLL = 26


def hdot(a, b, dims=NN):
    return lax.dot_general(a, b, dims, precision=lax.Precision.HIGHEST, preferred_element_type=F32)


def bdot(a, b, dims):
    return lax.dot_general(a, b, dims, preferred_element_type=F32)


def swap(value, axis, size, distance):
    return lax.ppermute(value, axis, [(i, i ^ distance) for i in range(size)])


def swap_y(value, distance):
    return swap(value, BAL, lax.axis_size(BAL), distance)


def swap_core(value):
    return swap(value, DOM, lax.axis_size(DOM), 1)


def swap_next(value):
    size = lax.axis_size(DOM)
    route = []
    for i in range(1, size - 1, 2):
        route += [(i, i + 1), (i + 1, i)]
    return lax.ppermute(value, DOM, route)


def reduce_yzx(value):
    size = lax.axis_size(DOM)
    parts = [swap_y(value, k) for k in (1, 2, 3)]
    value = (value + parts[0]) + (parts[1] + parts[2])
    for unit in (2, 8):
        parts = [swap(value, DOM, size, k * unit) for k in (1, 2, 3)]
        value = (value + parts[0]) + (parts[1] + parts[2])
    return value


def reduce_all(value):
    return reduce_yzx(value + swap_core(value))


def reduce_halves(first, second, take_first):
    mine = jnp.where(take_first, first, second) + swap_core(jnp.where(take_first, second, first))
    mine = reduce_yzx(mine)
    other = swap_core(mine)
    return jnp.where(take_first, mine, other), jnp.where(take_first, other, mine)


VM = pl.BlockSpec(memory_space=pltpu.VMEM)
SM = pl.BlockSpec(memory_space=pltpu.SMEM)


def call(body, specs, outs, scratch, args, flops=0, nbytes=0, final=False):
    args = [pltpu.with_memory_space_constraint(a, pltpu.VMEM) if s is VM else a for s, a in zip(specs, args)]
    return pl.pallas_call(
        body,
        in_specs=specs,
        out_specs=tuple(VM for _ in outs),
        out_shape=tuple(jax.ShapeDtypeStruct(s, d) if final else pltpu.VMEM(s, d) for s, d in outs),
        scratch_shapes=scratch,
        compiler_params=pltpu.CompilerParams(vmem_limit_bytes=14 * 2**20),
        cost_estimate=pl.CostEstimate(flops=flops, bytes_accessed=nbytes, transcendentals=0),
    )(*args)


def inverse_factors(mats, out_ref):
    nb = K // 8
    row = lax.broadcasted_iota(jnp.int32, (8, K), 0)
    col = lax.broadcasted_iota(jnp.int32, (8, K), 1)
    work = []
    for g in mats:
        left = [g[8 * i : 8 * i + 8, :] for i in range(nb)]
        right = [jnp.where(row + 8 * i == col, 1.0, 0.0).astype(F32) for i in range(nb)]
        work.append((left, right))
    for k in range(0, K, 2):
        kb, kr = divmod(k, 8)
        for m, (left, right) in enumerate(work):
            r0, r1 = left[kb][kr : kr + 1, :], left[kb][kr + 1 : kr + 2, :]
            q0, q1 = right[kb][kr : kr + 1, :], right[kb][kr + 1 : kr + 2, :]
            a = jnp.broadcast_to(r0[:, k : k + 1], (1, K))
            b = jnp.broadcast_to(r0[:, k + 1 : k + 2], (1, K))
            c = jnp.broadcast_to(r1[:, k + 1 : k + 2], (1, K))
            inv = 1.0 / (a * c - b * b)
            if k < K - 2:
                p0, p1 = (c * r0 - b * r1) * inv, (a * r1 - b * r0) * inv
                s0, s1 = (c * q0 - b * q1) * inv, (a * q1 - b * q0) * inv
                for i in range(kb, nb):
                    if i == kb and kr == 6:
                        continue
                    f0, f1 = left[i][:, k : k + 1], left[i][:, k + 1 : k + 2]
                    if i == kb:
                        below = row[:, :1] > kr + 1
                        f0, f1 = jnp.where(below, f0, 0.0), jnp.where(below, f1, 0.0)
                    left[i] = left[i] - (f0 * p0 + f1 * p1)
                    right[i] = right[i] - (f0 * s0 + f1 * s1)
            t = b / a
            out_ref[m, k : k + 1, :] = q0 * lax.rsqrt(a)
            out_ref[m, k + 1 : k + 2, :] = (q1 - t * q0) * lax.rsqrt(c - b * t)


def split(x):
    hi = x.astype(BF16)
    return hi, (x - hi.astype(F32)).astype(BF16)


def lanes(ref):
    return jnp.concatenate([ref[b] for b in range(BR)], axis=1)


def gram_of(a, others):
    a_hi, a_lo = a
    o_hi = jnp.concatenate([o[0] for o in others], axis=0)
    o_lo = jnp.concatenate([o[1] for o in others], axis=0)
    main = bdot(jnp.concatenate([a_hi, a_lo], axis=0), o_hi, NT)
    return main[0:K] + (main[K : 2 * K] + bdot(a_hi, o_lo, NT))


def combine(weights, parts):
    w_hi, w_lo = split(weights)
    rhs = jnp.concatenate([p[0] for p in parts] + [p[1] for p in parts], axis=0)
    m = weights.shape[0]
    lhs = jnp.concatenate([w_hi, w_lo], axis=0)
    lhs = jnp.concatenate([lhs, lhs], axis=1)
    out = bdot(lhs, rhs, NN)
    return out[0:m] + out[m : 2 * m]


def start_gram_kernel(x_ref, g_ref):
    g = jnp.zeros((K, K), F32)
    for b in range(BR):
        g = g + hdot(x_ref[b], x_ref[b], NT)
    g_ref[...] = g


def start_norm_kernel(g_ref, x_ref, n_ref, basis_ref, low_ref, lt_ref, inv_ref):
    g = g_ref[...] * (1.0 / n_ref[0])
    inverse_factors([g], inv_ref)
    inv = inv_ref[0]
    lt_ref[...] = hdot(inv, g)
    for b in range(BR):
        v = hdot(inv, x_ref[b])
        basis_ref[b] = v
        low_ref[b] = v.astype(BF16)


def mid_kernel(low_ref, q1_ref, q2_ref, q3_ref, pa_ref, cp_ref, zp_ref, own4_ref, o0_ref, o1_ref, o2_ref, o3_ref):
    for k, src in enumerate((low_ref, q1_ref, q2_ref, q3_ref)):
        own4_ref[8 * k : 8 * k + 8] = src[...]
    o0_ref[...] = pa_ref[0:8]
    o1_ref[...] = pa_ref[8:16].astype(BF16)
    for k, out in ((0, o2_ref), (8, o3_ref)):
        v = pa_ref[16 + k : 24 + k] + cp_ref[k : 8 + k].astype(F32) + zp_ref[k : 8 + k].astype(F32)
        out[...] = v.astype(BF16)


def join_kernel(a_ref, b_ref, out_ref):
    out_ref[0:8] = a_ref[...]
    out_ref[8:16] = b_ref[...]


def apply_m_kernel(col_ref, row_ref, own_ref, cp_ref, zp_ref, tiles_ref, out_ref, low_ref, win, acc):
    win[0:32] = own_ref[...]
    win[32:64] = cp_ref[...]
    win[64:96] = zp_ref[...]
    acc[...] = jnp.zeros_like(acc)
    slots = tiles_ref.shape[0]

    def step(s, carry):
        base = s * UNROLL
        parts = []
        for u in range(UNROLL):
            parts.append(bdot(win[col_ref[base + u]], tiles_ref[base + u], NT))
        for u in range(UNROLL):
            r = row_ref[base + u]
            acc[r] = acc[r] + parts[u]
        return carry

    lax.fori_loop(0, slots // UNROLL, step, 0)
    for b in range(BR):
        v = acc[b]
        out_ref[b] = v
        low_ref[b] = v.astype(BF16)


def apply_mt_kernel(
    col_ref, row_ref, back0_ref, b1_ref, b2_ref, b3_ref, tiles_ref, own_ref, cp_ref, zp_ref, low, acc
):
    for b in range(BR):
        v = back0_ref[b] + b1_ref[b].astype(F32) + b2_ref[b].astype(F32) + b3_ref[b].astype(F32)
        low[b] = v.astype(BF16)
    low[BR] = jnp.zeros((K, TILE), BF16)
    acc[...] = jnp.zeros_like(acc)
    slots = tiles_ref.shape[0]

    def step(s, carry):
        base = s * UNROLL
        parts = []
        for u in range(UNROLL):
            parts.append(bdot(low[row_ref[base + u]], tiles_ref[base + u], NN))
        for u in range(UNROLL):
            c = col_ref[base + u]
            acc[c] = acc[c] + parts[u]
        return carry

    lax.fori_loop(0, slots // UNROLL, step, 0)
    own_ref[...] = acc[0:32]
    cp_ref[...] = acc[32:64].astype(BF16)
    zp_ref[...] = acc[64:96].astype(BF16)


def apply_at_kernel(col_ref, low_ref, tiles_ref, own_ref, cp_ref, zp_ref, acc):
    acc[...] = jnp.zeros_like(acc)
    slots = tiles_ref.shape[1]
    for b in range(BR):
        x = low_ref[b]
        parts = [bdot(x, tiles_ref[b, j], NN) for j in range(slots)]
        for j in range(slots):
            c = col_ref[b * slots + j]
            acc[c] = acc[c] + parts[j]
    own_ref[...] = acc[0:32]
    cp_ref[...] = acc[32:48].astype(BF16)
    zp_ref[...] = acc[48:64].astype(BF16)


def collect_m_kernel(own_ref, cp_ref, zp_ref, o0_ref, o1_ref, o2_ref, o3_ref):
    v = own_ref[...] + cp_ref[...].astype(F32) + zp_ref[...].astype(F32)
    o0_ref[...] = v[0:8]
    o1_ref[...] = v[8:16].astype(BF16)
    o2_ref[...] = v[16:24].astype(BF16)
    o3_ref[...] = v[24:32].astype(BF16)


def apply_a_kernel(first, col_ref, low_ref, r1_ref, r2_ref, r3_ref, cp_ref, zp_ref, tiles_ref, shadow_ref, *refs):
    if first:
        image_ref, g_ref, win = refs
    else:
        basis_ref, res_ref, image_ref, g_ref, rest_ref, win = refs
    for k, src in enumerate((low_ref, r1_ref, r2_ref, r3_ref)):
        win[8 * k : 8 * k + 8] = src[...]
    win[32:48] = cp_ref[...]
    win[48:64] = zp_ref[...]
    slots = tiles_ref.shape[1]
    rows = []
    for b in range(BR):
        x = jnp.concatenate([win[col_ref[b * slots + j]] for j in range(slots)], axis=1)
        t = jnp.concatenate([tiles_ref[b, j] for j in range(slots)], axis=1)
        v = bdot(x, t, NT)
        image_ref[b] = v
        rows.append(v)
    image = split(jnp.concatenate(rows, axis=1))
    others = [split(lanes(shadow_ref)), image]
    if not first:
        others += [split(lanes(res_ref)), split(lanes(basis_ref))]
    g = gram_of(image, others)
    g_ref[0:64] = g[:, 0:128]
    if not first:
        g_ref[64:96] = g[0:32, 128:256]
        rest_ref[...] = g[32:64, 128:256]


def back_gram_kernel(first, o0_ref, b1_ref, b2_ref, b3_ref, shadow_ref, *refs):
    if first:
        bi_ref, g_ref = refs
    else:
        rest_ref, bi_ref, g_ref = refs
        g_ref[64:96] = rest_ref[...]
    rows = []
    for b in range(BR):
        v = o0_ref[b] + b1_ref[b].astype(F32) + b2_ref[b].astype(F32) + b3_ref[b].astype(F32)
        bi_ref[b] = v
        rows.append(v)
    back = split(jnp.concatenate(rows, axis=1))
    g_ref[0:64] = gram_of(back, [back, split(lanes(shadow_ref))])


def update_kernel(first, last, f_ref, b_ref, n_ref, image_ref, bi_ref, basis_ref, shadow_ref, precond_ref, res_ref, *refs):
    refs, inv_ref, w_ref = refs[:-2], refs[-2], refs[-1]
    if first:
        lt_ref, outs = refs[0], refs[1:]
    else:
        sol_ref, outs = refs[0], refs[1:]
    if last:
        sol_out, res_out, basis_out, shadow_out = outs
    else:
        sol_out, res_out, basis_out, shadow_out, blow_out, slow_out = outs
    total = n_ref[0]
    image_shadow = f_ref[0:64, 0:64]
    coup_t = image_shadow * (1.0 / total)
    coup = coup_t.T
    normal = f_ref[0:64, 64:128]
    bb = b_ref[0:64, 0:64]
    bs = b_ref[0:64, 64:128]
    if first:
        ib = image_shadow
        target = hdot(image_shadow, lt_ref[...])
    else:
        target = jnp.concatenate([f_ref[64:96, 0:64], b_ref[64:96, 0:64]], axis=0)
        ib = jnp.concatenate([f_ref[64:96, 64:128], b_ref[64:96, 64:128]], axis=0)
    uu = normal - hdot(ib, coup_t, NT) - hdot(coup_t, ib, NT) + total * hdot(coup_t, coup_t, NT)
    ss = bb - hdot(bs, coup_t) - hdot(coup, bs, NT) + total * hdot(coup_t, coup_t, TN)
    for m, v in enumerate((normal, uu * (1.0 / total), ss * (1.0 / total))):
        inv_ref[m] = v
    inverse_factors([inv_ref[m] for m in range(3)], inv_ref)
    inv_n, inv_u, inv_s = inv_ref[0], inv_ref[1], inv_ref[2]
    w_t = hdot(hdot(inv_n, target), inv_n, TN)
    w_ref[0:64, 0:64] = inv_u
    w_ref[0:64, 64:128] = -hdot(inv_u, coup_t)
    w_ref[64:128, 0:64] = -w_t
    w_ref[64:128, 64:128] = jnp.zeros((K, K), F32)
    w_ref[128:192, 0:64] = inv_s
    w_ref[128:192, 64:128] = -hdot(inv_s, coup)
    first_two = combine(w_ref[0:128], [split(lanes(image_ref)), split(lanes(basis_ref))])
    third = combine(w_ref[128:192], [split(lanes(bi_ref)), split(lanes(shadow_ref))])
    fourth = combine(w_t, [split(lanes(precond_ref))])
    for b in range(BR):
        at = slice(b * TILE, (b + 1) * TILE)
        v = fourth[:, at]
        sol_out[b] = v if first else sol_ref[b] + v
        res_out[b] = res_ref[b] + first_two[K : 2 * K, at]
        v = first_two[0:K, at]
        basis_out[b] = v
        if not last:
            blow_out[b] = v.astype(BF16)
        v = third[:, at]
        shadow_out[b] = v
        if not last:
            slow_out[b] = v.astype(BF16)


def shards(right_side, a_tiles, a_cols, m_tiles, m_rows, m_cols, m_count):
    blk = (BR, K, TILE)
    total = BR * TILE * lax.axis_size((DOM, BAL))
    group = lax.axis_index(DOM)
    y = lax.axis_index(BAL)
    first_row = (group * lax.axis_size(BAL) + y) * BR
    n_arr = jnp.full((1,), float(total), F32)

    def place(cols, skip):
        dev = cols // BR
        g, rel = dev // 4, (dev % 4) ^ y
        width = 4 - skip
        local = jnp.where(
            g == group, rel, jnp.where(g == (group ^ 1), 4 + rel - skip, 4 + width + rel - skip)
        )
        return local * BR + cols % BR

    a_place = place(a_cols, 2).reshape(-1)
    m_place = place(m_cols, 0)
    live = jnp.arange(m_tiles.shape[0], dtype=jnp.int32) < m_count[0]
    m_local = jnp.where(live, m_rows - first_row, BR)

    is_first_core = jnp.broadcast_to(group % 2 == 0, (1, 128))
    right_side, a_place, m_place, m_local, n_arr, is_first_core = lax.optimization_barrier(
        (right_side, a_place, m_place, m_local, n_arr, is_first_core)
    )

    (g0,) = call(start_gram_kernel, [VM], [((K, K), F32)], [], (right_side,))
    g0 = reduce_all(g0)
    basis, blow, lt = call(
        start_norm_kernel,
        [VM, VM, SM],
        [(blk, F32), (blk, BF16), ((K, K), F32)],
        [pltpu.VMEM((1, K, K), F32)],
        (g0, right_side, n_arr),
    )
    shadow, slow = basis, blow
    solution, residual = None, right_side
    for iteration in range(ITERS):
        last = iteration == ITERS - 1
        q = [swap_y(blow, k) for k in (1, 2, 3)]
        pa_own, pa_cp, pa_zp = call(
            apply_at_kernel,
            [SM, VM, VM],
            [((32, K, TILE), F32), ((16, K, TILE), BF16), ((16, K, TILE), BF16)],
            [pltpu.VMEM((64, K, TILE), F32)],
            (a_place, slow, a_tiles),
            flops=84_000_000,
            nbytes=3_000_000,
        )
        ra_zp, ra_cp = swap_next(pa_zp), swap_core(pa_cp)
        own4, o0, o1, o2, o3 = call(
            mid_kernel,
            [VM] * 7,
            [((32, K, TILE), BF16), (blk, F32)] + [(blk, BF16)] * 3,
            [],
            (blow, *q, pa_own, ra_cp, ra_zp),
        )
        m_zp = swap_next(own4)
        b1, b2, b3 = (swap_y(o, k) for k, o in ((1, o1), (2, o2), (3, o3)))
        m_cp = swap_core(own4)
        pm_own, pm_cp, pm_zp = call(
            apply_mt_kernel,
            [SM, SM] + [VM] * 5,
            [((32, K, TILE), F32), ((32, K, TILE), BF16), ((32, K, TILE), BF16)],
            [pltpu.VMEM((BR + 1, K, TILE), BF16), pltpu.VMEM((96, K, TILE), F32)],
            (m_place, m_local, o0, b1, b2, b3, m_tiles),
            flops=218_000_000,
            nbytes=5_000_000,
        )
        rm_zp, rm_cp = swap_next(pm_zp), swap_core(pm_cp)
        precond, plow = call(
            apply_m_kernel,
            [SM, SM] + [VM] * 4,
            [(blk, F32), (blk, BF16)],
            [pltpu.VMEM((96, K, TILE), BF16), pltpu.VMEM((BR + 1, K, TILE), F32)],
            (m_place, m_local, own4, m_cp, m_zp, m_tiles),
            flops=218_000_000,
            nbytes=5_000_000,
        )
        r = [swap_y(plow, k) for k in (1, 2, 3)]
        (far,) = call(join_kernel, [VM] * 2, [((16, K, TILE), BF16)], [], (r[1], r[2]))
        a_zp, a_cp = swap_next(far), swap_core(far)
        far, pm_own, rm_cp, rm_zp = lax.optimization_barrier((far, pm_own, rm_cp, rm_zp))
        o0, o1, o2, o3 = call(
            collect_m_kernel, [VM] * 3, [(blk, F32)] + [(blk, BF16)] * 3, [], (pm_own, rm_cp, rm_zp)
        )
        b1, b2, b3 = (swap_y(o, k) for k, o in ((1, o1), (2, o2), (3, o3)))
        first = iteration == 0
        height = 64 if first else 96
        image, g_fwd, *rest = call(
            lambda *refs, f=first: apply_a_kernel(f, *refs),
            [SM] + [VM] * (8 if first else 10),
            [(blk, F32), ((height, 128), F32)] + ([] if first else [((32, 128), F32)]),
            [pltpu.VMEM((64, K, TILE), BF16)],
            (a_place, plow, *r, a_cp, a_zp, a_tiles, shadow, *([] if first else [basis, residual])),
            flops=84_000_000,
            nbytes=3_000_000,
        )
        back_image, g_bwd = call(
            lambda *refs, f=first: back_gram_kernel(f, *refs),
            [VM] * (5 if first else 6),
            [(blk, F32), ((height, 128), F32)],
            [],
            (o0, b1, b2, b3, shadow, *rest),
        )
        g_fwd, g_bwd = reduce_halves(g_fwd, g_bwd, is_first_core)
        args = [g_fwd, g_bwd, n_arr, image, back_image, basis, shadow, precond, residual]
        args.append(lt if first else solution)
        outs = [(blk, F32)] * 4 + ([] if last else [(blk, BF16)] * 2)
        result = call(
            lambda *refs, f=iteration == 0, l=last: update_kernel(f, l, *refs),
            [VM, VM, SM] + [VM] * (len(args) - 3),
            outs,
            [pltpu.VMEM((3, K, K), F32), pltpu.VMEM((192, 128), F32)],
            args,
            final=last,
        )
        solution, residual, basis, shadow = result[:4]
        if not last:
            blow, slow = result[4:]
    return (solution, residual, basis, shadow)


def solution(mesh):
    rows = P((DOM, BAL))
    return jax.shard_map(
        shards,
        mesh=mesh,
        in_specs=(rows,) * 7,
        out_specs=(rows,) * 4,
        check_vma=False,
    )
```

```python
import jax
import jax.numpy as jnp
from jax import lax
from jax.experimental import pallas as pl
from jax.experimental.pallas import tpu as pltpu
from jax.sharding import PartitionSpec as P


ITERS = 2
BR = 8
TILE = 128
K = 64
NT = (((1,), (1,)), ((), ()))
NN = (((1,), (0,)), ((), ()))
TN = (((0,), (0,)), ((), ()))
F32 = jnp.float32
BF16 = jnp.bfloat16
DOM, BAL = "dom", "bal"
UNROLL = 26


def hdot(a, b, dims=NN):
    return lax.dot_general(a, b, dims, precision=lax.Precision.HIGHEST, preferred_element_type=F32)


def bdot(a, b, dims):
    return lax.dot_general(a, b, dims, preferred_element_type=F32)


def swap(value, axis, size, distance):
    return lax.ppermute(value, axis, [(i, i ^ distance) for i in range(size)])


def swap_y(value, distance):
    return swap(value, BAL, lax.axis_size(BAL), distance)


def swap_core(value):
    return swap(value, DOM, lax.axis_size(DOM), 1)


def swap_next(value):
    size = lax.axis_size(DOM)
    route = []
    for i in range(1, size - 1, 2):
        route += [(i, i + 1), (i + 1, i)]
    return lax.ppermute(value, DOM, route)


def reduce_all(value):
    size = lax.axis_size(DOM)
    value = value + swap_core(value)
    for unit in (None, 2, 8):
        parts = []
        for k in (1, 2, 3):
            if unit is None:
                parts.append(swap_y(value, k))
            else:
                parts.append(swap(value, DOM, size, k * unit))
        value = (value + parts[0]) + (parts[1] + parts[2])
    return value


VM = pl.BlockSpec(memory_space=pltpu.VMEM)
SM = pl.BlockSpec(memory_space=pltpu.SMEM)


def call(body, specs, outs, scratch, args, flops=0, nbytes=0, final=False):
    args = [pltpu.with_memory_space_constraint(a, pltpu.VMEM) if s is VM else a for s, a in zip(specs, args)]
    return pl.pallas_call(
        body,
        in_specs=specs,
        out_specs=tuple(VM for _ in outs),
        out_shape=tuple(jax.ShapeDtypeStruct(s, d) if final else pltpu.VMEM(s, d) for s, d in outs),
        scratch_shapes=scratch,
        compiler_params=pltpu.CompilerParams(vmem_limit_bytes=14 * 2**20),
        cost_estimate=pl.CostEstimate(flops=flops, bytes_accessed=nbytes, transcendentals=0),
    )(*args)


def inverse_factors(mats, out_ref):
    nb = K // 8
    row = lax.broadcasted_iota(jnp.int32, (8, K), 0)
    col = lax.broadcasted_iota(jnp.int32, (8, K), 1)
    work = []
    for g in mats:
        left = [g[8 * i : 8 * i + 8, :] for i in range(nb)]
        right = [jnp.where(row + 8 * i == col, 1.0, 0.0).astype(F32) for i in range(nb)]
        work.append((left, right))
    for k in range(0, K, 2):
        kb, kr = divmod(k, 8)
        for m, (left, right) in enumerate(work):
            r0, r1 = left[kb][kr : kr + 1, :], left[kb][kr + 1 : kr + 2, :]
            q0, q1 = right[kb][kr : kr + 1, :], right[kb][kr + 1 : kr + 2, :]
            a = jnp.broadcast_to(r0[:, k : k + 1], (1, K))
            b = jnp.broadcast_to(r0[:, k + 1 : k + 2], (1, K))
            c = jnp.broadcast_to(r1[:, k + 1 : k + 2], (1, K))
            inv = 1.0 / (a * c - b * b)
            if k < K - 2:
                p0, p1 = (c * r0 - b * r1) * inv, (a * r1 - b * r0) * inv
                s0, s1 = (c * q0 - b * q1) * inv, (a * q1 - b * q0) * inv
                for i in range(kb, nb):
                    if i == kb and kr == 6:
                        continue
                    f0, f1 = left[i][:, k : k + 1], left[i][:, k + 1 : k + 2]
                    if i == kb:
                        below = row[:, :1] > kr + 1
                        f0, f1 = jnp.where(below, f0, 0.0), jnp.where(below, f1, 0.0)
                    left[i] = left[i] - (f0 * p0 + f1 * p1)
                    right[i] = right[i] - (f0 * s0 + f1 * s1)
            t = b / a
            out_ref[m, k : k + 1, :] = q0 * lax.rsqrt(a)
            out_ref[m, k + 1 : k + 2, :] = (q1 - t * q0) * lax.rsqrt(c - b * t)


def split(x):
    hi = x.astype(BF16)
    return hi, (x - hi.astype(F32)).astype(BF16)


def lanes(ref):
    return jnp.concatenate([ref[b] for b in range(BR)], axis=1)


def gram_of(a, others):
    a_hi, a_lo = a
    o_hi = jnp.concatenate([o[0] for o in others], axis=0)
    o_lo = jnp.concatenate([o[1] for o in others], axis=0)
    main = bdot(jnp.concatenate([a_hi, a_lo], axis=0), o_hi, NT)
    return main[0:K] + (main[K : 2 * K] + bdot(a_hi, o_lo, NT))


def combine(weights, parts):
    w_hi, w_lo = split(weights)
    rhs = jnp.concatenate([p[0] for p in parts] + [p[1] for p in parts], axis=0)
    m = weights.shape[0]
    lhs = jnp.concatenate([w_hi, w_lo], axis=0)
    lhs = jnp.concatenate([lhs, lhs], axis=1)
    out = bdot(lhs, rhs, NN)
    return out[0:m] + out[m : 2 * m]


def start_gram_kernel(x_ref, g_ref):
    g = jnp.zeros((K, K), F32)
    for b in range(BR):
        g = g + hdot(x_ref[b], x_ref[b], NT)
    g_ref[...] = g


def start_norm_kernel(g_ref, x_ref, n_ref, basis_ref, low_ref, lt_ref, inv_ref):
    g = g_ref[...] * (1.0 / n_ref[0])
    inverse_factors([g], inv_ref)
    inv = inv_ref[0]
    lt_ref[...] = hdot(inv, g)
    for b in range(BR):
        v = hdot(inv, x_ref[b])
        basis_ref[b] = v
        low_ref[b] = v.astype(BF16)


def mid_kernel(low_ref, q1_ref, q2_ref, q3_ref, pa_ref, cp_ref, zp_ref, own4_ref, o0_ref, o1_ref, o2_ref, o3_ref):
    for k, src in enumerate((low_ref, q1_ref, q2_ref, q3_ref)):
        own4_ref[8 * k : 8 * k + 8] = src[...]
    o0_ref[...] = pa_ref[0:8]
    o1_ref[...] = pa_ref[8:16].astype(BF16)
    for k, out in ((0, o2_ref), (8, o3_ref)):
        v = pa_ref[16 + k : 24 + k] + cp_ref[k : 8 + k].astype(F32) + zp_ref[k : 8 + k].astype(F32)
        out[...] = v.astype(BF16)


def join_kernel(a_ref, b_ref, out_ref):
    out_ref[0:8] = a_ref[...]
    out_ref[8:16] = b_ref[...]


def apply_m_kernel(col_ref, row_ref, own_ref, cp_ref, zp_ref, tiles_ref, out_ref, low_ref, win, acc):
    win[0:32] = own_ref[...]
    win[32:64] = cp_ref[...]
    win[64:96] = zp_ref[...]
    acc[...] = jnp.zeros_like(acc)
    slots = tiles_ref.shape[0]

    def step(s, carry):
        base = s * UNROLL
        parts = []
        for u in range(UNROLL):
            parts.append(bdot(win[col_ref[base + u]], tiles_ref[base + u], NT))
        for u in range(UNROLL):
            r = row_ref[base + u]
            acc[r] = acc[r] + parts[u]
        return carry

    lax.fori_loop(0, slots // UNROLL, step, 0)
    for b in range(BR):
        v = acc[b]
        out_ref[b] = v
        low_ref[b] = v.astype(BF16)


def apply_mt_kernel(
    col_ref, row_ref, back0_ref, b1_ref, b2_ref, b3_ref, tiles_ref, own_ref, cp_ref, zp_ref, low, acc
):
    for b in range(BR):
        v = back0_ref[b] + b1_ref[b].astype(F32) + b2_ref[b].astype(F32) + b3_ref[b].astype(F32)
        low[b] = v.astype(BF16)
    low[BR] = jnp.zeros((K, TILE), BF16)
    acc[...] = jnp.zeros_like(acc)
    slots = tiles_ref.shape[0]

    def step(s, carry):
        base = s * UNROLL
        parts = []
        for u in range(UNROLL):
            parts.append(bdot(low[row_ref[base + u]], tiles_ref[base + u], NN))
        for u in range(UNROLL):
            c = col_ref[base + u]
            acc[c] = acc[c] + parts[u]
        return carry

    lax.fori_loop(0, slots // UNROLL, step, 0)
    own_ref[...] = acc[0:32]
    cp_ref[...] = acc[32:64].astype(BF16)
    zp_ref[...] = acc[64:96].astype(BF16)


def apply_at_kernel(col_ref, low_ref, tiles_ref, own_ref, cp_ref, zp_ref, acc):
    acc[...] = jnp.zeros_like(acc)
    slots = tiles_ref.shape[1]
    for b in range(BR):
        x = low_ref[b]
        parts = [bdot(x, tiles_ref[b, j], NN) for j in range(slots)]
        for j in range(slots):
            c = col_ref[b * slots + j]
            acc[c] = acc[c] + parts[j]
    own_ref[...] = acc[0:32]
    cp_ref[...] = acc[32:48].astype(BF16)
    zp_ref[...] = acc[48:64].astype(BF16)


def collect_m_kernel(own_ref, cp_ref, zp_ref, o0_ref, o1_ref, o2_ref, o3_ref):
    v = own_ref[...] + cp_ref[...].astype(F32) + zp_ref[...].astype(F32)
    o0_ref[...] = v[0:8]
    o1_ref[...] = v[8:16].astype(BF16)
    o2_ref[...] = v[16:24].astype(BF16)
    o3_ref[...] = v[24:32].astype(BF16)


def apply_a_kernel(first, col_ref, low_ref, r1_ref, r2_ref, r3_ref, cp_ref, zp_ref, tiles_ref, shadow_ref, *refs):
    if first:
        image_ref, g_ref, win = refs
    else:
        basis_ref, res_ref, image_ref, g_ref, rest_ref, win = refs
    for k, src in enumerate((low_ref, r1_ref, r2_ref, r3_ref)):
        win[8 * k : 8 * k + 8] = src[...]
    win[32:48] = cp_ref[...]
    win[48:64] = zp_ref[...]
    slots = tiles_ref.shape[1]
    rows = []
    for b in range(BR):
        x = jnp.concatenate([win[col_ref[b * slots + j]] for j in range(slots)], axis=1)
        t = jnp.concatenate([tiles_ref[b, j] for j in range(slots)], axis=1)
        v = bdot(x, t, NT)
        image_ref[b] = v
        rows.append(v)
    image = split(jnp.concatenate(rows, axis=1))
    others = [split(lanes(shadow_ref)), image]
    if not first:
        others += [split(lanes(res_ref)), split(lanes(basis_ref))]
    g = gram_of(image, others)
    g_ref[0:64] = g[:, 0:128]
    if not first:
        g_ref[64:96] = g[0:32, 128:256]
        rest_ref[...] = g[32:64, 128:256]


def back_gram_kernel(first, o0_ref, b1_ref, b2_ref, b3_ref, shadow_ref, *refs):
    if first:
        bi_ref, g_ref = refs
    else:
        rest_ref, bi_ref, g_ref = refs
        g_ref[64:96] = rest_ref[...]
    rows = []
    for b in range(BR):
        v = o0_ref[b] + b1_ref[b].astype(F32) + b2_ref[b].astype(F32) + b3_ref[b].astype(F32)
        bi_ref[b] = v
        rows.append(v)
    back = split(jnp.concatenate(rows, axis=1))
    g_ref[0:64] = gram_of(back, [back, split(lanes(shadow_ref))])


def update_kernel(first, last, g_ref, n_ref, image_ref, bi_ref, basis_ref, shadow_ref, precond_ref, res_ref, *refs):
    refs, inv_ref, w_ref = refs[:-2], refs[-2], refs[-1]
    if first:
        lt_ref, outs = refs[0], refs[1:]
    else:
        sol_ref, outs = refs[0], refs[1:]
    if last:
        sol_out, res_out, basis_out, shadow_out = outs
    else:
        sol_out, res_out, basis_out, shadow_out, blow_out, slow_out = outs
    half = g_ref.shape[0] // 2
    f_ref, b_ref = g_ref.at[0:half], g_ref.at[half : 2 * half]
    total = n_ref[0]
    image_shadow = f_ref[0:64, 0:64]
    coup_t = image_shadow * (1.0 / total)
    coup = coup_t.T
    normal = f_ref[0:64, 64:128]
    bb = b_ref[0:64, 0:64]
    bs = b_ref[0:64, 64:128]
    if first:
        ib = image_shadow
        target = hdot(image_shadow, lt_ref[...])
    else:
        target = jnp.concatenate([f_ref[64:96, 0:64], b_ref[64:96, 0:64]], axis=0)
        ib = jnp.concatenate([f_ref[64:96, 64:128], b_ref[64:96, 64:128]], axis=0)
    uu = normal - hdot(ib, coup_t, NT) - hdot(coup_t, ib, NT) + total * hdot(coup_t, coup_t, NT)
    ss = bb - hdot(bs, coup_t) - hdot(coup, bs, NT) + total * hdot(coup_t, coup_t, TN)
    for m, v in enumerate((normal, uu * (1.0 / total), ss * (1.0 / total))):
        inv_ref[m] = v
    inverse_factors([inv_ref[m] for m in range(3)], inv_ref)
    inv_n, inv_u, inv_s = inv_ref[0], inv_ref[1], inv_ref[2]
    w_t = hdot(hdot(inv_n, target), inv_n, TN)
    w_ref[0:64, 0:64] = inv_u
    w_ref[0:64, 64:128] = -hdot(inv_u, coup_t)
    w_ref[64:128, 0:64] = -w_t
    w_ref[64:128, 64:128] = jnp.zeros((K, K), F32)
    w_ref[128:192, 0:64] = inv_s
    w_ref[128:192, 64:128] = -hdot(inv_s, coup)
    first_two = combine(w_ref[0:128], [split(lanes(image_ref)), split(lanes(basis_ref))])
    third = combine(w_ref[128:192], [split(lanes(bi_ref)), split(lanes(shadow_ref))])
    fourth = combine(w_t, [split(lanes(precond_ref))])
    for b in range(BR):
        at = slice(b * TILE, (b + 1) * TILE)
        v = fourth[:, at]
        sol_out[b] = v if first else sol_ref[b] + v
        res_out[b] = res_ref[b] + first_two[K : 2 * K, at]
        v = first_two[0:K, at]
        basis_out[b] = v
        if not last:
            blow_out[b] = v.astype(BF16)
        v = third[:, at]
        shadow_out[b] = v
        if not last:
            slow_out[b] = v.astype(BF16)


def shards(right_side, a_tiles, a_cols, m_tiles, m_rows, m_cols, m_count):
    blk = (BR, K, TILE)
    total = BR * TILE * lax.axis_size((DOM, BAL))
    group = lax.axis_index(DOM)
    y = lax.axis_index(BAL)
    first_row = (group * lax.axis_size(BAL) + y) * BR
    n_arr = jnp.full((1,), float(total), F32)

    def place(cols, skip):
        dev = cols // BR
        g, rel = dev // 4, (dev % 4) ^ y
        width = 4 - skip
        local = jnp.where(
            g == group, rel, jnp.where(g == (group ^ 1), 4 + rel - skip, 4 + width + rel - skip)
        )
        return local * BR + cols % BR

    a_place = place(a_cols, 2).reshape(-1)
    m_place = place(m_cols, 0)
    live = jnp.arange(m_tiles.shape[0], dtype=jnp.int32) < m_count[0]
    m_local = jnp.where(live, m_rows - first_row, BR)

    right_side, a_place, m_place, m_local, n_arr = lax.optimization_barrier(
        (right_side, a_place, m_place, m_local, n_arr)
    )

    (g0,) = call(start_gram_kernel, [VM], [((K, K), F32)], [], (right_side,))
    g0 = reduce_all(g0)
    basis, blow, lt = call(
        start_norm_kernel,
        [VM, VM, SM],
        [(blk, F32), (blk, BF16), ((K, K), F32)],
        [pltpu.VMEM((1, K, K), F32)],
        (g0, right_side, n_arr),
    )
    shadow, slow = basis, blow
    solution, residual = None, right_side
    for iteration in range(ITERS):
        last = iteration == ITERS - 1
        q = [swap_y(blow, k) for k in (1, 2, 3)]
        pa_own, pa_cp, pa_zp = call(
            apply_at_kernel,
            [SM, VM, VM],
            [((32, K, TILE), F32), ((16, K, TILE), BF16), ((16, K, TILE), BF16)],
            [pltpu.VMEM((64, K, TILE), F32)],
            (a_place, slow, a_tiles),
            flops=84_000_000,
            nbytes=3_000_000,
        )
        ra_zp, ra_cp = swap_next(pa_zp), swap_core(pa_cp)
        own4, o0, o1, o2, o3 = call(
            mid_kernel,
            [VM] * 7,
            [((32, K, TILE), BF16), (blk, F32)] + [(blk, BF16)] * 3,
            [],
            (blow, *q, pa_own, ra_cp, ra_zp),
        )
        m_zp = swap_next(own4)
        b1, b2, b3 = (swap_y(o, k) for k, o in ((1, o1), (2, o2), (3, o3)))
        m_cp = swap_core(own4)
        pm_own, pm_cp, pm_zp = call(
            apply_mt_kernel,
            [SM, SM] + [VM] * 5,
            [((32, K, TILE), F32), ((32, K, TILE), BF16), ((32, K, TILE), BF16)],
            [pltpu.VMEM((BR + 1, K, TILE), BF16), pltpu.VMEM((96, K, TILE), F32)],
            (m_place, m_local, o0, b1, b2, b3, m_tiles),
            flops=218_000_000,
            nbytes=5_000_000,
        )
        rm_zp, rm_cp = swap_next(pm_zp), swap_core(pm_cp)
        precond, plow = call(
            apply_m_kernel,
            [SM, SM] + [VM] * 4,
            [(blk, F32), (blk, BF16)],
            [pltpu.VMEM((96, K, TILE), BF16), pltpu.VMEM((BR + 1, K, TILE), F32)],
            (m_place, m_local, own4, m_cp, m_zp, m_tiles),
            flops=218_000_000,
            nbytes=5_000_000,
        )
        r = [swap_y(plow, k) for k in (1, 2, 3)]
        (far,) = call(join_kernel, [VM] * 2, [((16, K, TILE), BF16)], [], (r[1], r[2]))
        a_zp, a_cp = swap_next(far), swap_core(far)
        far, pm_own, rm_cp, rm_zp = lax.optimization_barrier((far, pm_own, rm_cp, rm_zp))
        o0, o1, o2, o3 = call(
            collect_m_kernel, [VM] * 3, [(blk, F32)] + [(blk, BF16)] * 3, [], (pm_own, rm_cp, rm_zp)
        )
        b1, b2, b3 = (swap_y(o, k) for k, o in ((1, o1), (2, o2), (3, o3)))
        first = iteration == 0
        height = 64 if first else 96
        image, g_fwd, *rest = call(
            lambda *refs, f=first: apply_a_kernel(f, *refs),
            [SM] + [VM] * (8 if first else 10),
            [(blk, F32), ((height, 128), F32)] + ([] if first else [((32, 128), F32)]),
            [pltpu.VMEM((64, K, TILE), BF16)],
            (a_place, plow, *r, a_cp, a_zp, a_tiles, shadow, *([] if first else [basis, residual])),
            flops=84_000_000,
            nbytes=3_000_000,
        )
        back_image, g_bwd = call(
            lambda *refs, f=first: back_gram_kernel(f, *refs),
            [VM] * (5 if first else 6),
            [(blk, F32), ((height, 128), F32)],
            [],
            (o0, b1, b2, b3, shadow, *rest),
        )
        grams = reduce_all(jnp.concatenate([g_fwd, g_bwd], 0))
        args = [grams, n_arr, image, back_image, basis, shadow, precond, residual]
        args.append(lt if first else solution)
        outs = [(blk, F32)] * 4 + ([] if last else [(blk, BF16)] * 2)
        result = call(
            lambda *refs, f=iteration == 0, l=last: update_kernel(f, l, *refs),
            [VM, SM] + [VM] * (len(args) - 2),
            outs,
            [pltpu.VMEM((3, K, K), F32), pltpu.VMEM((192, 128), F32)],
            args,
            final=last,
        )
        solution, residual, basis, shadow = result[:4]
        if not last:
            blow, slow = result[4:]
    return (solution, residual, basis, shadow)


def solution(mesh):
    rows = P((DOM, BAL))
    return jax.shard_map(
        shards,
        mesh=mesh,
        in_specs=(rows,) * 7,
        out_specs=(rows,) * 4,
        check_vma=False,
    )
```

```python
import jax
import jax.numpy as jnp
from jax import lax
from jax.experimental import pallas as pl
from jax.experimental.pallas import tpu as pltpu
from jax.sharding import PartitionSpec as P


ITERS = 2
BR = 8
TILE = 128
K = 64
NT = (((1,), (1,)), ((), ()))
NN = (((1,), (0,)), ((), ()))
TN = (((0,), (0,)), ((), ()))
F32 = jnp.float32
BF16 = jnp.bfloat16
DOM, BAL = "dom", "bal"
UNROLL = 26


def hdot(a, b, dims=NN):
    return lax.dot_general(a, b, dims, precision=lax.Precision.HIGHEST, preferred_element_type=F32)


def bdot(a, b, dims):
    return lax.dot_general(a, b, dims, preferred_element_type=F32)


def swap(value, axis, size, distance):
    return lax.ppermute(value, axis, [(i, i ^ distance) for i in range(size)])


def swap_y(value, distance):
    return swap(value, BAL, lax.axis_size(BAL), distance)


def swap_core(value):
    return swap(value, DOM, lax.axis_size(DOM), 1)


def swap_next(value):
    size = lax.axis_size(DOM)
    route = []
    for i in range(1, size - 1, 2):
        route += [(i, i + 1), (i + 1, i)]
    return lax.ppermute(value, DOM, route)


def reduce_yzx(value):
    size = lax.axis_size(DOM)
    for unit in (None, 2, 8):
        parts = []
        for k in (1, 2, 3):
            if unit is None:
                parts.append(swap_y(value, k))
            else:
                parts.append(swap(value, DOM, size, k * unit))
        value = (value + parts[0]) + (parts[1] + parts[2])
    return value


def reduce_all(value):
    return reduce_yzx(value + swap_core(value))


def reduce_halves(first, second, take_first):
    mine = jnp.where(take_first, first, second) + swap_core(jnp.where(take_first, second, first))
    mine = reduce_yzx(mine)
    other = swap_core(mine)
    return jnp.where(take_first, mine, other), jnp.where(take_first, other, mine)


VM = pl.BlockSpec(memory_space=pltpu.VMEM)
SM = pl.BlockSpec(memory_space=pltpu.SMEM)


def call(body, specs, outs, scratch, args, flops=0, nbytes=0, final=False):
    args = [pltpu.with_memory_space_constraint(a, pltpu.VMEM) if s is VM else a for s, a in zip(specs, args)]
    return pl.pallas_call(
        body,
        in_specs=specs,
        out_specs=tuple(VM for _ in outs),
        out_shape=tuple(jax.ShapeDtypeStruct(s, d) if final else pltpu.VMEM(s, d) for s, d in outs),
        scratch_shapes=scratch,
        compiler_params=pltpu.CompilerParams(vmem_limit_bytes=14 * 2**20),
        cost_estimate=pl.CostEstimate(flops=flops, bytes_accessed=nbytes, transcendentals=0),
    )(*args)


def inverse_factors(mats, out_ref):
    nb = K // 8
    row = lax.broadcasted_iota(jnp.int32, (8, K), 0)
    col = lax.broadcasted_iota(jnp.int32, (8, K), 1)
    work = []
    for g in mats:
        left = [g[8 * i : 8 * i + 8, :] for i in range(nb)]
        right = [jnp.where(row + 8 * i == col, 1.0, 0.0).astype(F32) for i in range(nb)]
        work.append((left, right))
    for k in range(0, K, 2):
        kb, kr = divmod(k, 8)
        for m, (left, right) in enumerate(work):
            r0, r1 = left[kb][kr : kr + 1, :], left[kb][kr + 1 : kr + 2, :]
            q0, q1 = right[kb][kr : kr + 1, :], right[kb][kr + 1 : kr + 2, :]
            a = jnp.broadcast_to(r0[:, k : k + 1], (1, K))
            b = jnp.broadcast_to(r0[:, k + 1 : k + 2], (1, K))
            c = jnp.broadcast_to(r1[:, k + 1 : k + 2], (1, K))
            inv = 1.0 / (a * c - b * b)
            if k < K - 2:
                p0, p1 = (c * r0 - b * r1) * inv, (a * r1 - b * r0) * inv
                s0, s1 = (c * q0 - b * q1) * inv, (a * q1 - b * q0) * inv
                for i in range(kb, nb):
                    if i == kb and kr == 6:
                        continue
                    f0, f1 = left[i][:, k : k + 1], left[i][:, k + 1 : k + 2]
                    if i == kb:
                        below = row[:, :1] > kr + 1
                        f0, f1 = jnp.where(below, f0, 0.0), jnp.where(below, f1, 0.0)
                    left[i] = left[i] - (f0 * p0 + f1 * p1)
                    right[i] = right[i] - (f0 * s0 + f1 * s1)
            t = b / a
            out_ref[m, k : k + 1, :] = q0 * lax.rsqrt(a)
            out_ref[m, k + 1 : k + 2, :] = (q1 - t * q0) * lax.rsqrt(c - b * t)


def split(x):
    hi = x.astype(BF16)
    return hi, (x - hi.astype(F32)).astype(BF16)


def lanes(ref):
    return jnp.concatenate([ref[b] for b in range(BR)], axis=1)


def gram_of(a, others):
    a_hi, a_lo = a
    o_hi = jnp.concatenate([o[0] for o in others], axis=0)
    o_lo = jnp.concatenate([o[1] for o in others], axis=0)
    main = bdot(jnp.concatenate([a_hi, a_lo], axis=0), o_hi, NT)
    return main[0:K] + (main[K : 2 * K] + bdot(a_hi, o_lo, NT))


def combine(weights, parts):
    w_hi, w_lo = split(weights)
    rhs = jnp.concatenate([p[0] for p in parts] + [p[1] for p in parts], axis=0)
    m = weights.shape[0]
    lhs = jnp.concatenate([w_hi, w_lo], axis=0)
    lhs = jnp.concatenate([lhs, lhs], axis=1)
    out = bdot(lhs, rhs, NN)
    return out[0:m] + out[m : 2 * m]


def start_gram_kernel(x_ref, g_ref):
    g = jnp.zeros((K, K), F32)
    for b in range(BR):
        g = g + hdot(x_ref[b], x_ref[b], NT)
    g_ref[...] = g


def start_norm_kernel(g_ref, x_ref, n_ref, basis_ref, low_ref, lt_ref, inv_ref):
    g = g_ref[...] * (1.0 / n_ref[0])
    inverse_factors([g], inv_ref)
    inv = inv_ref[0]
    lt_ref[...] = hdot(inv, g)
    for b in range(BR):
        v = hdot(inv, x_ref[b])
        basis_ref[b] = v
        low_ref[b] = v.astype(BF16)


def mid_kernel(low_ref, q1_ref, q2_ref, q3_ref, pa_ref, cp_ref, zp_ref, own4_ref, o0_ref, o1_ref, o2_ref, o3_ref):
    for k, src in enumerate((low_ref, q1_ref, q2_ref, q3_ref)):
        own4_ref[8 * k : 8 * k + 8] = src[...]
    o0_ref[...] = pa_ref[0:8]
    o1_ref[...] = pa_ref[8:16].astype(BF16)
    for k, out in ((0, o2_ref), (8, o3_ref)):
        v = pa_ref[16 + k : 24 + k] + cp_ref[k : 8 + k].astype(F32) + zp_ref[k : 8 + k].astype(F32)
        out[...] = v.astype(BF16)


def join_kernel(a_ref, b_ref, out_ref):
    out_ref[0:8] = a_ref[...]
    out_ref[8:16] = b_ref[...]


def apply_m_kernel(col_ref, row_ref, own_ref, cp_ref, zp_ref, tiles_ref, out_ref, low_ref, win, acc):
    win[0:32] = own_ref[...]
    win[32:64] = cp_ref[...]
    win[64:96] = zp_ref[...]
    acc[...] = jnp.zeros_like(acc)
    slots = tiles_ref.shape[0]

    def step(s, carry):
        base = s * UNROLL
        parts = []
        for u in range(UNROLL):
            parts.append(bdot(win[col_ref[base + u]], tiles_ref[base + u], NT))
        for u in range(UNROLL):
            r = row_ref[base + u]
            acc[r] = acc[r] + parts[u]
        return carry

    lax.fori_loop(0, slots // UNROLL, step, 0)
    for b in range(BR):
        v = acc[b]
        out_ref[b] = v
        low_ref[b] = v.astype(BF16)


def apply_mt_kernel(
    col_ref, row_ref, back0_ref, b1_ref, b2_ref, b3_ref, tiles_ref, own_ref, cp_ref, zp_ref, low, acc
):
    for b in range(BR):
        v = back0_ref[b] + b1_ref[b].astype(F32) + b2_ref[b].astype(F32) + b3_ref[b].astype(F32)
        low[b] = v.astype(BF16)
    low[BR] = jnp.zeros((K, TILE), BF16)
    acc[...] = jnp.zeros_like(acc)
    slots = tiles_ref.shape[0]

    def step(s, carry):
        base = s * UNROLL
        parts = []
        for u in range(UNROLL):
            parts.append(bdot(low[row_ref[base + u]], tiles_ref[base + u], NN))
        for u in range(UNROLL):
            c = col_ref[base + u]
            acc[c] = acc[c] + parts[u]
        return carry

    lax.fori_loop(0, slots // UNROLL, step, 0)
    own_ref[...] = acc[0:32]
    cp_ref[...] = acc[32:64].astype(BF16)
    zp_ref[...] = acc[64:96].astype(BF16)


def apply_at_kernel(col_ref, low_ref, tiles_ref, own_ref, cp_ref, zp_ref, acc):
    acc[...] = jnp.zeros_like(acc)
    slots = tiles_ref.shape[1]
    for b in range(BR):
        x = low_ref[b]
        parts = [bdot(x, tiles_ref[b, j], NN) for j in range(slots)]
        for j in range(slots):
            c = col_ref[b * slots + j]
            acc[c] = acc[c] + parts[j]
    own_ref[...] = acc[0:32]
    cp_ref[...] = acc[32:48].astype(BF16)
    zp_ref[...] = acc[48:64].astype(BF16)


def collect_m_kernel(own_ref, cp_ref, zp_ref, o0_ref, o1_ref, o2_ref, o3_ref):
    v = own_ref[...] + cp_ref[...].astype(F32) + zp_ref[...].astype(F32)
    o0_ref[...] = v[0:8]
    o1_ref[...] = v[8:16].astype(BF16)
    o2_ref[...] = v[16:24].astype(BF16)
    o3_ref[...] = v[24:32].astype(BF16)


def apply_a_kernel(first, col_ref, low_ref, r1_ref, r2_ref, r3_ref, cp_ref, zp_ref, tiles_ref, shadow_ref, *refs):
    if first:
        image_ref, g_ref, win = refs
    else:
        basis_ref, res_ref, image_ref, g_ref, rest_ref, win = refs
    for k, src in enumerate((low_ref, r1_ref, r2_ref, r3_ref)):
        win[8 * k : 8 * k + 8] = src[...]
    win[32:48] = cp_ref[...]
    win[48:64] = zp_ref[...]
    slots = tiles_ref.shape[1]
    rows = []
    for b in range(BR):
        x = jnp.concatenate([win[col_ref[b * slots + j]] for j in range(slots)], axis=1)
        t = jnp.concatenate([tiles_ref[b, j] for j in range(slots)], axis=1)
        v = bdot(x, t, NT)
        image_ref[b] = v
        rows.append(v)
    image = split(jnp.concatenate(rows, axis=1))
    others = [split(lanes(shadow_ref)), image]
    if not first:
        others += [split(lanes(res_ref)), split(lanes(basis_ref))]
    g = gram_of(image, others)
    g_ref[0:64] = g[:, 0:128]
    if not first:
        g_ref[64:96] = g[0:32, 128:256]
        rest_ref[...] = g[32:64, 128:256]


def back_gram_kernel(first, o0_ref, b1_ref, b2_ref, b3_ref, shadow_ref, *refs):
    if first:
        bi_ref, g_ref = refs
    else:
        rest_ref, bi_ref, g_ref = refs
        g_ref[64:96] = rest_ref[...]
    rows = []
    for b in range(BR):
        v = o0_ref[b] + b1_ref[b].astype(F32) + b2_ref[b].astype(F32) + b3_ref[b].astype(F32)
        bi_ref[b] = v
        rows.append(v)
    back = split(jnp.concatenate(rows, axis=1))
    g_ref[0:64] = gram_of(back, [back, split(lanes(shadow_ref))])


def update_kernel(first, last, f_ref, b_ref, n_ref, image_ref, bi_ref, basis_ref, shadow_ref, precond_ref, res_ref, *refs):
    refs, inv_ref, w_ref = refs[:-2], refs[-2], refs[-1]
    if first:
        lt_ref, outs = refs[0], refs[1:]
    else:
        sol_ref, outs = refs[0], refs[1:]
    if last:
        sol_out, res_out, basis_out, shadow_out = outs
    else:
        sol_out, res_out, basis_out, shadow_out, blow_out, slow_out = outs
    total = n_ref[0]
    image_shadow = f_ref[0:64, 0:64]
    coup_t = image_shadow * (1.0 / total)
    coup = coup_t.T
    normal = f_ref[0:64, 64:128]
    bb = b_ref[0:64, 0:64]
    bs = b_ref[0:64, 64:128]
    if first:
        ib = image_shadow
        target = hdot(image_shadow, lt_ref[...])
    else:
        target = jnp.concatenate([f_ref[64:96, 0:64], b_ref[64:96, 0:64]], axis=0)
        ib = jnp.concatenate([f_ref[64:96, 64:128], b_ref[64:96, 64:128]], axis=0)
    uu = normal - hdot(ib, coup_t, NT) - hdot(coup_t, ib, NT) + total * hdot(coup_t, coup_t, NT)
    ss = bb - hdot(bs, coup_t) - hdot(coup, bs, NT) + total * hdot(coup_t, coup_t, TN)
    for m, v in enumerate((normal, uu * (1.0 / total), ss * (1.0 / total))):
        inv_ref[m] = v
    inverse_factors([inv_ref[m] for m in range(3)], inv_ref)
    inv_n, inv_u, inv_s = inv_ref[0], inv_ref[1], inv_ref[2]
    w_t = hdot(hdot(inv_n, target), inv_n, TN)
    w_ref[0:64, 0:64] = inv_u
    w_ref[0:64, 64:128] = -hdot(inv_u, coup_t)
    w_ref[64:128, 0:64] = -w_t
    w_ref[64:128, 64:128] = jnp.zeros((K, K), F32)
    w_ref[128:192, 0:64] = inv_s
    w_ref[128:192, 64:128] = -hdot(inv_s, coup)
    first_two = combine(w_ref[0:128], [split(lanes(image_ref)), split(lanes(basis_ref))])
    third = combine(w_ref[128:192], [split(lanes(bi_ref)), split(lanes(shadow_ref))])
    fourth = combine(w_t, [split(lanes(precond_ref))])
    for b in range(BR):
        at = slice(b * TILE, (b + 1) * TILE)
        v = fourth[:, at]
        sol_out[b] = v if first else sol_ref[b] + v
        res_out[b] = res_ref[b] + first_two[K : 2 * K, at]
        v = first_two[0:K, at]
        basis_out[b] = v
        if not last:
            blow_out[b] = v.astype(BF16)
        v = third[:, at]
        shadow_out[b] = v
        if not last:
            slow_out[b] = v.astype(BF16)


def shards(right_side, a_tiles, a_cols, m_tiles, m_rows, m_cols, m_count):
    blk = (BR, K, TILE)
    total = BR * TILE * lax.axis_size((DOM, BAL))
    group = lax.axis_index(DOM)
    y = lax.axis_index(BAL)
    first_row = (group * lax.axis_size(BAL) + y) * BR
    n_arr = jnp.full((1,), float(total), F32)

    def place(cols, skip):
        dev = cols // BR
        g, rel = dev // 4, (dev % 4) ^ y
        width = 4 - skip
        local = jnp.where(
            g == group, rel, jnp.where(g == (group ^ 1), 4 + rel - skip, 4 + width + rel - skip)
        )
        return local * BR + cols % BR

    a_place = place(a_cols, 2).reshape(-1)
    m_place = place(m_cols, 0)
    live = jnp.arange(m_tiles.shape[0], dtype=jnp.int32) < m_count[0]
    m_local = jnp.where(live, m_rows - first_row, BR)

    is_first_core = jnp.broadcast_to(group % 2 == 0, (1, 128))
    right_side, a_place, m_place, m_local, n_arr, is_first_core = lax.optimization_barrier(
        (right_side, a_place, m_place, m_local, n_arr, is_first_core)
    )

    (g0,) = call(start_gram_kernel, [VM], [((K, K), F32)], [], (right_side,))
    g0 = reduce_all(g0)
    basis, blow, lt = call(
        start_norm_kernel,
        [VM, VM, SM],
        [(blk, F32), (blk, BF16), ((K, K), F32)],
        [pltpu.VMEM((1, K, K), F32)],
        (g0, right_side, n_arr),
    )
    shadow, slow = basis, blow
    solution, residual = None, right_side
    for iteration in range(ITERS):
        last = iteration == ITERS - 1
        q = [swap_y(blow, k) for k in (1, 2, 3)]
        pa_own, pa_cp, pa_zp = call(
            apply_at_kernel,
            [SM, VM, VM],
            [((32, K, TILE), F32), ((16, K, TILE), BF16), ((16, K, TILE), BF16)],
            [pltpu.VMEM((64, K, TILE), F32)],
            (a_place, slow, a_tiles),
            flops=84_000_000,
            nbytes=3_000_000,
        )
        ra_zp, ra_cp = swap_next(pa_zp), swap_core(pa_cp)
        own4, o0, o1, o2, o3 = call(
            mid_kernel,
            [VM] * 7,
            [((32, K, TILE), BF16), (blk, F32)] + [(blk, BF16)] * 3,
            [],
            (blow, *q, pa_own, ra_cp, ra_zp),
        )
        m_zp = swap_next(own4)
        b1, b2, b3 = (swap_y(o, k) for k, o in ((1, o1), (2, o2), (3, o3)))
        m_cp = swap_core(own4)
        pm_own, pm_cp, pm_zp = call(
            apply_mt_kernel,
            [SM, SM] + [VM] * 5,
            [((32, K, TILE), F32), ((32, K, TILE), BF16), ((32, K, TILE), BF16)],
            [pltpu.VMEM((BR + 1, K, TILE), BF16), pltpu.VMEM((96, K, TILE), F32)],
            (m_place, m_local, o0, b1, b2, b3, m_tiles),
            flops=218_000_000,
            nbytes=5_000_000,
        )
        rm_zp, rm_cp = swap_next(pm_zp), swap_core(pm_cp)
        precond, plow = call(
            apply_m_kernel,
            [SM, SM] + [VM] * 4,
            [(blk, F32), (blk, BF16)],
            [pltpu.VMEM((96, K, TILE), BF16), pltpu.VMEM((BR + 1, K, TILE), F32)],
            (m_place, m_local, own4, m_cp, m_zp, m_tiles),
            flops=218_000_000,
            nbytes=5_000_000,
        )
        r = [swap_y(plow, k) for k in (1, 2, 3)]
        (far,) = call(join_kernel, [VM] * 2, [((16, K, TILE), BF16)], [], (r[1], r[2]))
        a_zp, a_cp = swap_next(far), swap_core(far)
        far, pm_own, rm_cp, rm_zp = lax.optimization_barrier((far, pm_own, rm_cp, rm_zp))
        o0, o1, o2, o3 = call(
            collect_m_kernel, [VM] * 3, [(blk, F32)] + [(blk, BF16)] * 3, [], (pm_own, rm_cp, rm_zp)
        )
        b1, b2, b3 = (swap_y(o, k) for k, o in ((1, o1), (2, o2), (3, o3)))
        first = iteration == 0
        height = 64 if first else 96
        image, g_fwd, *rest = call(
            lambda *refs, f=first: apply_a_kernel(f, *refs),
            [SM] + [VM] * (8 if first else 10),
            [(blk, F32), ((height, 128), F32)] + ([] if first else [((32, 128), F32)]),
            [pltpu.VMEM((64, K, TILE), BF16)],
            (a_place, plow, *r, a_cp, a_zp, a_tiles, shadow, *([] if first else [basis, residual])),
            flops=84_000_000,
            nbytes=3_000_000,
        )
        back_image, g_bwd = call(
            lambda *refs, f=first: back_gram_kernel(f, *refs),
            [VM] * (5 if first else 6),
            [(blk, F32), ((height, 128), F32)],
            [],
            (o0, b1, b2, b3, shadow, *rest),
        )
        g_fwd, g_bwd = reduce_halves(g_fwd, g_bwd, is_first_core)
        args = [g_fwd, g_bwd, n_arr, image, back_image, basis, shadow, precond, residual]
        args.append(lt if first else solution)
        outs = [(blk, F32)] * 4 + ([] if last else [(blk, BF16)] * 2)
        result = call(
            lambda *refs, f=iteration == 0, l=last: update_kernel(f, l, *refs),
            [VM, VM, SM] + [VM] * (len(args) - 3),
            outs,
            [pltpu.VMEM((3, K, K), F32), pltpu.VMEM((192, 128), F32)],
            args,
            final=last,
        )
        solution, residual, basis, shadow = result[:4]
        if not last:
            blow, slow = result[4:]
    return (solution, residual, basis, shadow)


def solution(mesh):
    rows = P((DOM, BAL))
    return jax.shard_map(
        shards,
        mesh=mesh,
        in_specs=(rows,) * 7,
        out_specs=(rows,) * 4,
        check_vma=False,
    )
```

```python
import jax
import jax.numpy as jnp
from jax import lax
from jax.experimental import pallas as pl
from jax.experimental.pallas import tpu as pltpu
from jax.sharding import PartitionSpec as P


ITERS = 2
BR = 8
TILE = 128
K = 64
NT = (((1,), (1,)), ((), ()))
NN = (((1,), (0,)), ((), ()))
TN = (((0,), (0,)), ((), ()))
F32 = jnp.float32
BF16 = jnp.bfloat16
DOM, BAL = "dom", "bal"
UNROLL = 26


def hdot(a, b, dims=NN):
    return lax.dot_general(a, b, dims, precision=lax.Precision.HIGHEST, preferred_element_type=F32)


def bdot(a, b, dims):
    return lax.dot_general(a, b, dims, preferred_element_type=F32)


def swap(value, axis, size, distance):
    return lax.ppermute(value, axis, [(i, i ^ distance) for i in range(size)])


def swap_y(value, distance):
    return swap(value, BAL, lax.axis_size(BAL), distance)


def swap_core(value):
    return swap(value, DOM, lax.axis_size(DOM), 1)


def swap_next(value):
    size = lax.axis_size(DOM)
    route = []
    for i in range(1, size - 1, 2):
        route += [(i, i + 1), (i + 1, i)]
    return lax.ppermute(value, DOM, route)


def reduce_yzx(value):
    size = lax.axis_size(DOM)
    for unit in (None, 2, 8):
        parts = []
        for k in (1, 2, 3):
            if unit is None:
                parts.append(swap_y(value, k))
            else:
                parts.append(swap(value, DOM, size, k * unit))
        value = (value + parts[0]) + (parts[1] + parts[2])
    return value


def reduce_all(value):
    return reduce_yzx(value + swap_core(value))


def reduce_halves(first, second, take_first):
    mine = jnp.where(take_first, first, second) + swap_core(jnp.where(take_first, second, first))
    mine = reduce_yzx(mine)
    other = swap_core(mine)
    return jnp.where(take_first, mine, other), jnp.where(take_first, other, mine)


VM = pl.BlockSpec(memory_space=pltpu.VMEM)
SM = pl.BlockSpec(memory_space=pltpu.SMEM)


def call(body, specs, outs, scratch, args, flops=0, nbytes=0, final=False):
    args = [pltpu.with_memory_space_constraint(a, pltpu.VMEM) if s is VM else a for s, a in zip(specs, args)]
    return pl.pallas_call(
        body,
        in_specs=specs,
        out_specs=tuple(VM for _ in outs),
        out_shape=tuple(jax.ShapeDtypeStruct(s, d) if final else pltpu.VMEM(s, d) for s, d in outs),
        scratch_shapes=scratch,
        compiler_params=pltpu.CompilerParams(vmem_limit_bytes=14 * 2**20),
        cost_estimate=pl.CostEstimate(flops=flops, bytes_accessed=nbytes, transcendentals=0),
    )(*args)


def inverse_factors(mats, out_ref):
    nb = K // 8
    row = lax.broadcasted_iota(jnp.int32, (8, K), 0)
    col = lax.broadcasted_iota(jnp.int32, (8, K), 1)
    work = []
    for g in mats:
        left = [g[8 * i : 8 * i + 8, :] for i in range(nb)]
        right = [jnp.where(row + 8 * i == col, 1.0, 0.0).astype(F32) for i in range(nb)]
        work.append((left, right))
    for k in range(0, K, 2):
        kb, kr = divmod(k, 8)
        for m, (left, right) in enumerate(work):
            r0, r1 = left[kb][kr : kr + 1, :], left[kb][kr + 1 : kr + 2, :]
            q0, q1 = right[kb][kr : kr + 1, :], right[kb][kr + 1 : kr + 2, :]
            a = jnp.broadcast_to(r0[:, k : k + 1], (1, K))
            b = jnp.broadcast_to(r0[:, k + 1 : k + 2], (1, K))
            c = jnp.broadcast_to(r1[:, k + 1 : k + 2], (1, K))
            inv = 1.0 / (a * c - b * b)
            if k < K - 2:
                p0, p1 = (c * r0 - b * r1) * inv, (a * r1 - b * r0) * inv
                s0, s1 = (c * q0 - b * q1) * inv, (a * q1 - b * q0) * inv
                for i in range(kb, nb):
                    if i == kb and kr == 6:
                        continue
                    f0, f1 = left[i][:, k : k + 1], left[i][:, k + 1 : k + 2]
                    if i == kb:
                        below = row[:, :1] > kr + 1
                        f0, f1 = jnp.where(below, f0, 0.0), jnp.where(below, f1, 0.0)
                    left[i] = left[i] - (f0 * p0 + f1 * p1)
                    right[i] = right[i] - (f0 * s0 + f1 * s1)
            t = b / a
            out_ref[m, k : k + 1, :] = q0 * lax.rsqrt(a)
            out_ref[m, k + 1 : k + 2, :] = (q1 - t * q0) * lax.rsqrt(c - b * t)


def split(x):
    hi = x.astype(BF16)
    return hi, (x - hi.astype(F32)).astype(BF16)


def lanes(ref):
    return jnp.concatenate([ref[b] for b in range(BR)], axis=1)


def gram_of(a, others):
    a_hi, a_lo = a
    o_hi = jnp.concatenate([o[0] for o in others], axis=0)
    o_lo = jnp.concatenate([o[1] for o in others], axis=0)
    main = bdot(jnp.concatenate([a_hi, a_lo], axis=0), o_hi, NT)
    return main[0:K] + (main[K : 2 * K] + bdot(a_hi, o_lo, NT))


def combine(weights, parts):
    w_hi, w_lo = split(weights)
    rhs = jnp.concatenate([p[0] for p in parts] + [p[1] for p in parts], axis=0)
    m = weights.shape[0]
    lhs = jnp.concatenate([w_hi, w_lo], axis=0)
    lhs = jnp.concatenate([lhs, lhs], axis=1)
    out = bdot(lhs, rhs, NN)
    return out[0:m] + out[m : 2 * m]


def start_gram_kernel(x_ref, g_ref):
    g = jnp.zeros((K, K), F32)
    for b in range(BR):
        g = g + hdot(x_ref[b], x_ref[b], NT)
    g_ref[...] = g


def start_norm_kernel(g_ref, x_ref, n_ref, basis_ref, low_ref, lt_ref, inv_ref):
    g = g_ref[...] * (1.0 / n_ref[0])
    inverse_factors([g], inv_ref)
    inv = inv_ref[0]
    lt_ref[...] = hdot(inv, g)
    for b in range(BR):
        v = hdot(inv, x_ref[b])
        basis_ref[b] = v
        low_ref[b] = v.astype(BF16)


def pack_kernel(low_ref, q1_ref, q2_ref, q3_ref, own4_ref):
    for k, src in enumerate((low_ref, q1_ref, q2_ref, q3_ref)):
        own4_ref[8 * k : 8 * k + 8] = src[...]


def mid_kernel(pa_ref, cp_ref, zp_ref, o0_ref, o1_ref, o2_ref, o3_ref):
    o0_ref[...] = pa_ref[0:8]
    o1_ref[...] = pa_ref[8:16].astype(BF16)
    for k, out in ((0, o2_ref), (8, o3_ref)):
        v = pa_ref[16 + k : 24 + k] + cp_ref[k : 8 + k].astype(F32) + zp_ref[k : 8 + k].astype(F32)
        out[...] = v.astype(BF16)


def join_kernel(a_ref, b_ref, out_ref):
    out_ref[0:8] = a_ref[...]
    out_ref[8:16] = b_ref[...]


def apply_m_kernel(col_ref, row_ref, own_ref, cp_ref, zp_ref, tiles_ref, out_ref, low_ref, win, acc):
    win[0:32] = own_ref[...]
    win[32:64] = cp_ref[...]
    win[64:96] = zp_ref[...]
    acc[...] = jnp.zeros_like(acc)
    slots = tiles_ref.shape[0]

    def step(s, carry):
        base = s * UNROLL
        parts = []
        for u in range(UNROLL):
            parts.append(bdot(win[col_ref[base + u]], tiles_ref[base + u], NT))
        for u in range(UNROLL):
            r = row_ref[base + u]
            acc[r] = acc[r] + parts[u]
        return carry

    lax.fori_loop(0, slots // UNROLL, step, 0)
    for b in range(BR):
        v = acc[b]
        out_ref[b] = v
        low_ref[b] = v.astype(BF16)


def apply_mt_kernel(
    col_ref, row_ref, back0_ref, b1_ref, b2_ref, b3_ref, tiles_ref, own_ref, cp_ref, zp_ref, low, acc
):
    for b in range(BR):
        v = back0_ref[b] + b1_ref[b].astype(F32) + b2_ref[b].astype(F32) + b3_ref[b].astype(F32)
        low[b] = v.astype(BF16)
    low[BR] = jnp.zeros((K, TILE), BF16)
    acc[...] = jnp.zeros_like(acc)
    slots = tiles_ref.shape[0]

    def step(s, carry):
        base = s * UNROLL
        parts = []
        for u in range(UNROLL):
            parts.append(bdot(low[row_ref[base + u]], tiles_ref[base + u], NN))
        for u in range(UNROLL):
            c = col_ref[base + u]
            acc[c] = acc[c] + parts[u]
        return carry

    lax.fori_loop(0, slots // UNROLL, step, 0)
    own_ref[...] = acc[0:32]
    cp_ref[...] = acc[32:64].astype(BF16)
    zp_ref[...] = acc[64:96].astype(BF16)


def apply_at_kernel(col_ref, low_ref, tiles_ref, own_ref, cp_ref, zp_ref, acc):
    acc[...] = jnp.zeros_like(acc)
    slots = tiles_ref.shape[1]
    for b in range(BR):
        x = low_ref[b]
        parts = [bdot(x, tiles_ref[b, j], NN) for j in range(slots)]
        for j in range(slots):
            c = col_ref[b * slots + j]
            acc[c] = acc[c] + parts[j]
    own_ref[...] = acc[0:32]
    cp_ref[...] = acc[32:48].astype(BF16)
    zp_ref[...] = acc[48:64].astype(BF16)


def collect_m_kernel(own_ref, cp_ref, zp_ref, o0_ref, o1_ref, o2_ref, o3_ref):
    v = own_ref[...] + cp_ref[...].astype(F32) + zp_ref[...].astype(F32)
    o0_ref[...] = v[0:8]
    o1_ref[...] = v[8:16].astype(BF16)
    o2_ref[...] = v[16:24].astype(BF16)
    o3_ref[...] = v[24:32].astype(BF16)


def apply_a_kernel(first, col_ref, low_ref, r1_ref, r2_ref, r3_ref, cp_ref, zp_ref, tiles_ref, shadow_ref, *refs):
    if first:
        image_ref, g_ref, win = refs
    else:
        basis_ref, res_ref, image_ref, g_ref, rest_ref, win = refs
    for k, src in enumerate((low_ref, r1_ref, r2_ref, r3_ref)):
        win[8 * k : 8 * k + 8] = src[...]
    win[32:48] = cp_ref[...]
    win[48:64] = zp_ref[...]
    slots = tiles_ref.shape[1]
    rows = []
    for b in range(BR):
        x = jnp.concatenate([win[col_ref[b * slots + j]] for j in range(slots)], axis=1)
        t = jnp.concatenate([tiles_ref[b, j] for j in range(slots)], axis=1)
        v = bdot(x, t, NT)
        image_ref[b] = v
        rows.append(v)
    image = split(jnp.concatenate(rows, axis=1))
    others = [split(lanes(shadow_ref)), image]
    if not first:
        others += [split(lanes(res_ref)), split(lanes(basis_ref))]
    g = gram_of(image, others)
    g_ref[0:64] = g[:, 0:128]
    if not first:
        g_ref[64:96] = g[0:32, 128:256]
        rest_ref[...] = g[32:64, 128:256]


def back_gram_kernel(first, o0_ref, b1_ref, b2_ref, b3_ref, shadow_ref, *refs):
    if first:
        bi_ref, g_ref = refs
    else:
        rest_ref, bi_ref, g_ref = refs
        g_ref[64:96] = rest_ref[...]
    rows = []
    for b in range(BR):
        v = o0_ref[b] + b1_ref[b].astype(F32) + b2_ref[b].astype(F32) + b3_ref[b].astype(F32)
        bi_ref[b] = v
        rows.append(v)
    back = split(jnp.concatenate(rows, axis=1))
    g_ref[0:64] = gram_of(back, [back, split(lanes(shadow_ref))])


def update_kernel(first, last, f_ref, b_ref, n_ref, image_ref, bi_ref, basis_ref, shadow_ref, precond_ref, res_ref, *refs):
    refs, inv_ref, w_ref = refs[:-2], refs[-2], refs[-1]
    if first:
        lt_ref, outs = refs[0], refs[1:]
    else:
        sol_ref, outs = refs[0], refs[1:]
    if last:
        sol_out, res_out, basis_out, shadow_out = outs
    else:
        sol_out, res_out, basis_out, shadow_out, blow_out, slow_out = outs
    total = n_ref[0]
    image_shadow = f_ref[0:64, 0:64]
    coup_t = image_shadow * (1.0 / total)
    coup = coup_t.T
    normal = f_ref[0:64, 64:128]
    bb = b_ref[0:64, 0:64]
    bs = b_ref[0:64, 64:128]
    if first:
        ib = image_shadow
        target = hdot(image_shadow, lt_ref[...])
    else:
        target = jnp.concatenate([f_ref[64:96, 0:64], b_ref[64:96, 0:64]], axis=0)
        ib = jnp.concatenate([f_ref[64:96, 64:128], b_ref[64:96, 64:128]], axis=0)
    uu = normal - hdot(ib, coup_t, NT) - hdot(coup_t, ib, NT) + total * hdot(coup_t, coup_t, NT)
    ss = bb - hdot(bs, coup_t) - hdot(coup, bs, NT) + total * hdot(coup_t, coup_t, TN)
    for m, v in enumerate((normal, uu * (1.0 / total), ss * (1.0 / total))):
        inv_ref[m] = v
    inverse_factors([inv_ref[m] for m in range(3)], inv_ref)
    inv_n, inv_u, inv_s = inv_ref[0], inv_ref[1], inv_ref[2]
    w_t = hdot(hdot(inv_n, target), inv_n, TN)
    w_ref[0:64, 0:64] = inv_u
    w_ref[0:64, 64:128] = -hdot(inv_u, coup_t)
    w_ref[64:128, 0:64] = -w_t
    w_ref[64:128, 64:128] = jnp.zeros((K, K), F32)
    w_ref[128:192, 0:64] = inv_s
    w_ref[128:192, 64:128] = -hdot(inv_s, coup)
    first_two = combine(w_ref[0:128], [split(lanes(image_ref)), split(lanes(basis_ref))])
    third = combine(w_ref[128:192], [split(lanes(bi_ref)), split(lanes(shadow_ref))])
    fourth = combine(w_t, [split(lanes(precond_ref))])
    for b in range(BR):
        at = slice(b * TILE, (b + 1) * TILE)
        v = fourth[:, at]
        sol_out[b] = v if first else sol_ref[b] + v
        res_out[b] = res_ref[b] + first_two[K : 2 * K, at]
        v = first_two[0:K, at]
        basis_out[b] = v
        if not last:
            blow_out[b] = v.astype(BF16)
        v = third[:, at]
        shadow_out[b] = v
        if not last:
            slow_out[b] = v.astype(BF16)


def shards(right_side, a_tiles, a_cols, m_tiles, m_rows, m_cols, m_count):
    blk = (BR, K, TILE)
    total = BR * TILE * lax.axis_size((DOM, BAL))
    group = lax.axis_index(DOM)
    y = lax.axis_index(BAL)
    first_row = (group * lax.axis_size(BAL) + y) * BR
    n_arr = jnp.full((1,), float(total), F32)

    def place(cols, skip):
        dev = cols // BR
        g, rel = dev // 4, (dev % 4) ^ y
        width = 4 - skip
        local = jnp.where(
            g == group, rel, jnp.where(g == (group ^ 1), 4 + rel - skip, 4 + width + rel - skip)
        )
        return local * BR + cols % BR

    a_place = place(a_cols, 2).reshape(-1)
    m_place = place(m_cols, 0)
    live = jnp.arange(m_tiles.shape[0], dtype=jnp.int32) < m_count[0]
    m_local = jnp.where(live, m_rows - first_row, BR)

    is_first_core = jnp.broadcast_to(group % 2 == 0, (1, 128))
    right_side, a_place, m_place, m_local, n_arr, is_first_core = lax.optimization_barrier(
        (right_side, a_place, m_place, m_local, n_arr, is_first_core)
    )

    (g0,) = call(start_gram_kernel, [VM], [((K, K), F32)], [], (right_side,))
    g0 = reduce_all(g0)
    basis, blow, lt = call(
        start_norm_kernel,
        [VM, VM, SM],
        [(blk, F32), (blk, BF16), ((K, K), F32)],
        [pltpu.VMEM((1, K, K), F32)],
        (g0, right_side, n_arr),
    )
    shadow, slow = basis, blow
    solution, residual = None, right_side
    for iteration in range(ITERS):
        last = iteration == ITERS - 1
        q = [swap_y(blow, k) for k in (1, 2, 3)]
        pa_own, pa_cp, pa_zp = call(
            apply_at_kernel,
            [SM, VM, VM],
            [((32, K, TILE), F32), ((16, K, TILE), BF16), ((16, K, TILE), BF16)],
            [pltpu.VMEM((64, K, TILE), F32)],
            (a_place, slow, a_tiles),
            flops=84_000_000,
            nbytes=3_000_000,
        )
        ra_zp, ra_cp = swap_next(pa_zp), swap_core(pa_cp)
        (own4,) = call(pack_kernel, [VM] * 4, [((32, K, TILE), BF16)], [], (blow, *q))
        m_zp = swap_next(own4)
        o0, o1, o2, o3 = call(
            mid_kernel, [VM] * 3, [(blk, F32)] + [(blk, BF16)] * 3, [], (pa_own, ra_cp, ra_zp)
        )
        b1, b2, b3 = (swap_y(o, k) for k, o in ((1, o1), (2, o2), (3, o3)))
        m_cp = swap_core(own4)
        pm_own, pm_cp, pm_zp = call(
            apply_mt_kernel,
            [SM, SM] + [VM] * 5,
            [((32, K, TILE), F32), ((32, K, TILE), BF16), ((32, K, TILE), BF16)],
            [pltpu.VMEM((BR + 1, K, TILE), BF16), pltpu.VMEM((96, K, TILE), F32)],
            (m_place, m_local, o0, b1, b2, b3, m_tiles),
            flops=218_000_000,
            nbytes=5_000_000,
        )
        rm_zp, rm_cp = swap_next(pm_zp), swap_core(pm_cp)
        precond, plow = call(
            apply_m_kernel,
            [SM, SM] + [VM] * 4,
            [(blk, F32), (blk, BF16)],
            [pltpu.VMEM((96, K, TILE), BF16), pltpu.VMEM((BR + 1, K, TILE), F32)],
            (m_place, m_local, own4, m_cp, m_zp, m_tiles),
            flops=218_000_000,
            nbytes=5_000_000,
        )
        r = [swap_y(plow, k) for k in (1, 2, 3)]
        (far,) = call(join_kernel, [VM] * 2, [((16, K, TILE), BF16)], [], (r[1], r[2]))
        a_zp, a_cp = swap_next(far), swap_core(far)
        far, pm_own, rm_cp, rm_zp = lax.optimization_barrier((far, pm_own, rm_cp, rm_zp))
        o0, o1, o2, o3 = call(
            collect_m_kernel, [VM] * 3, [(blk, F32)] + [(blk, BF16)] * 3, [], (pm_own, rm_cp, rm_zp)
        )
        b1, b2, b3 = (swap_y(o, k) for k, o in ((1, o1), (2, o2), (3, o3)))
        first = iteration == 0
        height = 64 if first else 96
        image, g_fwd, *rest = call(
            lambda *refs, f=first: apply_a_kernel(f, *refs),
            [SM] + [VM] * (8 if first else 10),
            [(blk, F32), ((height, 128), F32)] + ([] if first else [((32, 128), F32)]),
            [pltpu.VMEM((64, K, TILE), BF16)],
            (a_place, plow, *r, a_cp, a_zp, a_tiles, shadow, *([] if first else [basis, residual])),
            flops=84_000_000,
            nbytes=3_000_000,
        )
        back_image, g_bwd = call(
            lambda *refs, f=first: back_gram_kernel(f, *refs),
            [VM] * (5 if first else 6),
            [(blk, F32), ((height, 128), F32)],
            [],
            (o0, b1, b2, b3, shadow, *rest),
        )
        g_fwd, g_bwd = reduce_halves(g_fwd, g_bwd, is_first_core)
        args = [g_fwd, g_bwd, n_arr, image, back_image, basis, shadow, precond, residual]
        args.append(lt if first else solution)
        outs = [(blk, F32)] * 4 + ([] if last else [(blk, BF16)] * 2)
        result = call(
            lambda *refs, f=iteration == 0, l=last: update_kernel(f, l, *refs),
            [VM, VM, SM] + [VM] * (len(args) - 3),
            outs,
            [pltpu.VMEM((3, K, K), F32), pltpu.VMEM((192, 128), F32)],
            args,
            final=last,
        )
        solution, residual, basis, shadow = result[:4]
        if not last:
            blow, slow = result[4:]
    return (solution, residual, basis, shadow)


def solution(mesh):
    rows = P((DOM, BAL))
    return jax.shard_map(
        shards,
        mesh=mesh,
        in_specs=(rows,) * 7,
        out_specs=(rows,) * 4,
        check_vma=False,
    )
```
